128 devices in a mesh: grp: 4 (over y_hi, core), blk: 32 (over z, x, y_lo).
Axes of the slice: x: 4, y: 4 (y_hi: 2, y_lo: 2; y = y_hi * 2 + y_lo), z: 4, core: 2. Of those that a mesh axis runs over, the one named last changes fastest.
Arguments:
- state: float32 [4, 3, 512, 4096], P('grp', None, None, 'blk'), may hold values from -1 to 1
- material: float32 [4, 3, 512, 4096], P('grp', None, None, 'blk'), may hold values from 0.5 to 2
- occupied: int32 [16384], P(('grp', 'blk')), may hold values from 0 to 1, as said below
- brick_column: int32 [16384, 1], P(('grp', 'blk')), may hold values from 0 to 31, as said below
- brick_octant: int32 [16384], P(('grp', 'blk')), may hold values from 0 to 383
Outputs:
- new_state: float32 [4, 3, 512, 4096], P('grp', None, None, 'blk')
The draws below stay inside these ranges and needn't reach their ends.
Inputs may be any that keep to these rules, and one draw needn't show every extreme that they name: `brick_column`: the rows of one device name at most 8 elements of one column, and exactly 8 of some column; rows of grp index 3 are not read. `brick_octant`: rows of grp index 3 are not read. The slots e < 8 of every device are occupied.
All inputs are finite; a program needn't handle non-finite values.
Results may differ from the reference program's by a relative error of at most 0.00074.
Values may be sent and summed in bfloat16 or wider, within the bound.
A program may use at most 128 MiB of HBM per device.

```python
import math
import jax
import jax.numpy as jnp
from jax import lax

E_DEV = 128
STEPS = 2
CAP = 8
N_GRP = 4
N_BLK = 32


def draw_brick_column(key, part):
    slot_total = N_BLK * CAP
    device_total = N_GRP * N_BLK

    def one_device(device_at):
        device_key = jax.random.fold_in(key, device_at + 11)
        noise_key, bias_key, pick_key = jax.random.split(device_key, 3)
        noise = jax.random.randint(noise_key, (slot_total,), 0, 2 ** 15)
        column_bias = jax.random.randint(bias_key, (N_BLK,), 0, 4)
        chosen = jax.random.randint(pick_key, (), 0, N_BLK)
        chosen = jnp.where(device_at == 2 * N_BLK + N_BLK - 1, 0, jnp.where(device_at == 0, N_BLK - 1, chosen))
        column_bias = jnp.where(jnp.arange(N_BLK) == chosen, 4, column_bias)
        slot_column = jnp.arange(slot_total) // CAP
        scores = (noise + column_bias[slot_column] * 2 ** 15) * slot_total + jnp.arange(slot_total)
        best_scores, picked = lax.top_k(scores, E_DEV)
        return (picked // CAP).astype(jnp.int32)
    columns = jax.vmap(one_device)(jnp.arange(device_total))
    return columns.reshape(device_total * E_DEV, 1).astype(jnp.int32)


def draw_occupied(key, part):
    total = N_GRP * N_BLK * E_DEV
    rolled = jax.random.randint(jax.random.fold_in(key, 5), (total,), 0, 4)
    position = jnp.arange(total) % E_DEV
    return jnp.where(position < CAP, 1, jnp.where(rolled < 3, 1, 0)).astype(jnp.int32)


def place_ends(result, rng, low, top_value):
    longest = result.shape.index(max(result.shape))
    spots = []
    for shift in (0, 1):
        where = [jax.random.randint(jax.random.fold_in(rng, axis), (), 0, length) for axis, length in enumerate(result.shape)]
        where[longest] = (where[longest] + shift) % result.shape[longest]
        spots.append(tuple(where))
    return result.at[spots[0]].set(low).at[spots[1]].set(top_value)


def level_of(rng, shape, cuts, smallest, top_value):
    loudness, own = 1.0, jax.random.fold_in(rng, 6)
    for dim, shards_of in cuts:
        draws = jnp.exp(jax.random.uniform(jax.random.fold_in(own, dim), (shards_of,), jnp.float32, smallest / len(cuts), top_value / len(cuts)))
        loudness = loudness * jnp.repeat(draws, shape[dim] // shards_of).reshape([-1 if axis == dim else 1 for axis in range(len(shape))])
    return loudness


def setup_inputs(seed: int = 0) -> dict:
    seeds = jax.random.split(jax.random.key(seed), 6)
    state = jnp.clip(jax.random.uniform(seeds[0], (N_GRP, 3, 512, N_BLK * E_DEV), jnp.float32, -1.0, 1.0) * level_of(seeds[0], (N_GRP, 3, 512, N_BLK * E_DEV), ((0, 4), (3, 32)), -0.4, 0.0), -1.0, 1.0)
    material = jnp.clip(jnp.exp(math.log(2.0) - 1.3862944 * jax.random.uniform(seeds[1], (N_GRP, 3, 512, N_BLK * E_DEV), jnp.float32) ** level_of(seeds[1], (N_GRP, 3, 512, N_BLK * E_DEV), ((0, 4), (3, 32)), -0.2, 0.2)), 0.5, 2.0)
    occupied = draw_occupied(jax.random.fold_in(seeds[5], 71), 0)
    brick_column = draw_brick_column(jax.random.fold_in(seeds[5], 71), 0)
    brick_octant = place_ends(jax.random.randint(seeds[4], (N_GRP * N_BLK * E_DEV,), 0, 3 * E_DEV), jax.random.fold_in(seeds[4], 1), 0, (3 * E_DEV) - 1).astype(jnp.int32)
    return dict(state=state, material=material, occupied=occupied, brick_column=brick_column, brick_octant=brick_octant)


UNIT_LENGTH = 0.02
TIME_STEP = 0.1
PENALTY = 1.0
PRESSURE_SCALE = 0.05
DILATION_SCALE = 50.0
SWEEP_STEP = 0.03
SOURCE_RATE = 2.0
CUBIC_TERM = 0.3


def node_diff(values, axis):
    length = values.shape[axis]
    lower_part = lax.slice_in_dim(values, 1, 2, axis=axis) - lax.slice_in_dim(values, 0, 1, axis=axis)
    middle = 0.5 * (lax.slice_in_dim(values, 2, length, axis=axis) - lax.slice_in_dim(values, 0, length - 2, axis=axis))
    upper_part = lax.slice_in_dim(values, length - 1, length, axis=axis) - lax.slice_in_dim(values, length - 2, length - 1, axis=axis)
    return jnp.concatenate([lower_part, middle, upper_part], axis=axis)


def deformation(current):
    displaced = UNIT_LENGTH * current
    return [[node_diff(displaced[i], j) + (1.0 if i == j else 0.0) for j in range(3)] for i in range(3)]


def determinant(grads):
    return (grads[0][0] * (grads[1][1] * grads[2][2] - grads[1][2] * grads[2][1])
            - grads[0][1] * (grads[1][0] * grads[2][2] - grads[1][2] * grads[2][0])
            + grads[0][2] * (grads[1][0] * grads[2][1] - grads[1][1] * grads[2][0]))


def cofactors(grads):
    return [[grads[1][1] * grads[2][2] - grads[1][2] * grads[2][1], grads[1][2] * grads[2][0] - grads[1][0] * grads[2][2], grads[1][0] * grads[2][1] - grads[1][1] * grads[2][0]],
            [grads[0][2] * grads[2][1] - grads[0][1] * grads[2][2], grads[0][0] * grads[2][2] - grads[0][2] * grads[2][0], grads[0][1] * grads[2][0] - grads[0][0] * grads[2][1]],
            [grads[0][1] * grads[1][2] - grads[0][2] * grads[1][1], grads[0][2] * grads[1][0] - grads[0][0] * grads[1][2], grads[0][0] * grads[1][1] - grads[0][1] * grads[1][0]]]


def dilation_rows(current, filled):
    grads = deformation(current)
    change = (determinant(grads) - 1.0) * filled * DILATION_SCALE
    return change.reshape(512, -1).astype(jnp.bfloat16)


def mech_update(current, material, pressure, filled, neighbours, first_mask, last_mask):
    grads = deformation(current)
    strain = [[0.5 * (sum(grads[k][i] * grads[k][j] for k in range(3)) - (1.0 if i == j else 0.0)) for j in range(3)] for i in range(3)]
    strain_trace = strain[0][0] + strain[1][1] + strain[2][2]
    shear, lame_first, mobility = material[0], material[1], material[2]
    stress_second = [[2.0 * shear * strain[i][j] + (lame_first * strain_trace if i == j else 0.0) for j in range(3)] for i in range(3)]
    cofactor_f = cofactors(grads)
    first_pk = [[sum(grads[i][k] * stress_second[k][j] for k in range(3)) - pressure * cofactor_f[i][j] for j in range(3)] for i in range(3)]
    forces = jnp.stack([sum(node_diff(first_pk[i][j], j) for j in range(3)) for i in range(3)])
    x_below, x_below_fill, x_above, x_above_fill = neighbours
    penalty = PENALTY * UNIT_LENGTH
    forces = forces.at[:, 0].add(penalty * x_below_fill * (x_below - current[:, 0]))
    forces = forces.at[:, 7].add(penalty * x_above_fill * (x_above - current[:, 7]))
    zero_face = jnp.zeros_like(current[:, :, :, 0, :1])
    zero_fill = jnp.zeros_like(filled[:1])
    z_below = jnp.concatenate([zero_face, current[:, :, :, 7, :-1]], axis=-1)
    z_below_fill = jnp.concatenate([zero_fill, filled[:-1]]) * (1.0 - first_mask)
    z_above = jnp.concatenate([current[:, :, :, 0, 1:], zero_face], axis=-1)
    z_above_fill = jnp.concatenate([filled[1:], zero_fill]) * (1.0 - last_mask)
    forces = forces.at[:, :, :, 0].add(penalty * z_below_fill * (z_below - current[:, :, :, 0]))
    forces = forces.at[:, :, :, 7].add(penalty * z_above_fill * (z_above - current[:, :, :, 7]))
    return current + (TIME_STEP / UNIT_LENGTH) * mobility * filled * forces


def pressure_cells(fraction):
    return (fraction + CUBIC_TERM * fraction * fraction * fraction).astype(jnp.bfloat16)


def diffuse(padded, coeff_field):
    centre = padded[1:-1]
    beside = jnp.pad(centre, ((0, 0), (1, 1), (1, 1)), mode="edge")
    weight_all = 0.5 + padded * padded
    weight_centre = weight_all[1:-1]
    inflow = 0.5 * (weight_centre + weight_all[2:]) * (padded[2:] - centre)
    inflow = inflow + 0.5 * (weight_centre + weight_all[:-2]) * (padded[:-2] - centre)
    for neighbour in (beside[:, 2:, 1:-1], beside[:, :-2, 1:-1], beside[:, 1:-1, 2:], beside[:, 1:-1, :-2]):
        inflow = inflow + 0.5 * (weight_centre + 0.5 + neighbour * neighbour) * (neighbour - centre)
    return centre + SWEEP_STEP * coeff_field * inflow


def to_octants(brick_field):
    depth = brick_field.shape[2]
    blocks = brick_field.reshape(2, 8, 2, 8, depth // 8, 8)
    return blocks.transpose(1, 3, 5, 0, 2, 4).reshape(512, 4 * (depth // 8))


def from_octants(octant_table, depth):
    blocks = octant_table.reshape(8, 8, 8, 2, 2, depth // 8)
    return blocks.transpose(3, 0, 4, 1, 5, 2).reshape(16, 16, depth)


def reference(state, material, occupied, brick_column, brick_octant):
    slab_width = N_BLK * E_DEV
    depth = 6 * E_DEV
    octant_count = 3 * E_DEV
    filled = occupied.reshape(4, slab_width).astype(jnp.float32)
    column = brick_column[:, 0].reshape(4, slab_width)[:3].reshape(-1)
    octant = brick_octant.reshape(4, slab_width)[:3].reshape(-1)
    target = (column * octant_count + octant).astype(jnp.int32)
    mechanics = [state[g].reshape(3, 8, 8, 8, slab_width) for g in range(3)]
    materials = [material[g].reshape(3, 8, 8, 8, slab_width) for g in range(3)]

    def to_bricks(slab):
        return slab.reshape(3, 512, N_BLK, E_DEV).transpose(2, 0, 1, 3).reshape(N_BLK * 16, 16, depth)

    fraction = to_bricks(state[3])
    diffusivity = to_bricks(material[3])
    element_at = jnp.arange(slab_width)
    first_mask = (element_at % E_DEV == 0).astype(jnp.float32)
    last_mask = (element_at % E_DEV == E_DEV - 1).astype(jnp.float32)
    zero_face = jnp.zeros((3, 8, 8, E_DEV), jnp.float32)
    zero_fill = jnp.zeros((E_DEV,), jnp.float32)
    for step_at in range(STEPS):
        per_column = pressure_cells(fraction).reshape(N_BLK, 16, 16, depth)
        octant_table = jax.vmap(to_octants)(per_column).transpose(1, 0, 2).reshape(512, N_BLK * octant_count)
        pressure = octant_table[:, target].astype(jnp.float32) * PRESSURE_SCALE
        dilations = jnp.concatenate([dilation_rows(mechanics[g], filled[g]) for g in range(3)], axis=1)
        deposit_sum = jnp.zeros((512, N_BLK * octant_count), jnp.float32).at[:, target].add(dilations.astype(jnp.float32))
        deposit_cells = jax.vmap(lambda table: from_octants(table, depth))(
            deposit_sum.reshape(512, N_BLK, octant_count).transpose(1, 0, 2)).reshape(N_BLK * 16, 16, depth)
        fraction = fraction + SWEEP_STEP * SOURCE_RATE * deposit_cells
        for sweep_at in range(2):
            fraction = diffuse(jnp.pad(fraction, ((1, 1), (0, 0), (0, 0))), diffusivity)
        updated = []
        for g in range(3):
            current = mechanics[g]
            x_below = jnp.concatenate([zero_face, current[:, 7, :, :, :-E_DEV]], axis=-1)
            x_below_fill = jnp.concatenate([zero_fill, filled[g][:-E_DEV]])
            x_above = jnp.concatenate([current[:, 0, :, :, E_DEV:], zero_face], axis=-1)
            x_above_fill = jnp.concatenate([filled[g][E_DEV:], zero_fill])
            neighbours = (x_below, x_below_fill, x_above, x_above_fill)
            own_pressure = pressure[:, g * slab_width:(g + 1) * slab_width].reshape(8, 8, 8, slab_width)
            updated.append(mech_update(current, materials[g], own_pressure, filled[g], neighbours, first_mask, last_mask))
        mechanics = updated
    solvent_slab = fraction.reshape(N_BLK, 3, 512, E_DEV).transpose(1, 2, 0, 3).reshape(3, 512, slab_width)
    return jnp.stack([mech.reshape(3, 512, slab_width) for mech in mechanics] + [solvent_slab])
```

```python
import jax
import jax.numpy as jnp
from jax import lax
from jax.sharding import PartitionSpec as P

STEPS = 2


UNIT_LENGTH = 0.02
TIME_STEP = 0.1
PENALTY = 1.0
PRESSURE_SCALE = 0.05
DILATION_SCALE = 50.0
SWEEP_STEP = 0.03
SOURCE_RATE = 2.0
CUBIC_TERM = 0.3


def passed_along(block, axis, distance):
    devices = range(lax.axis_size(axis))
    route = [(i - distance, i) for i in devices if i - distance in devices]
    return lax.ppermute(block, axis, route)


def padded_2(array, sides, width):
    for axis, dim in sides:
        devices, length = (lax.axis_size(axis), array.shape[dim])
        up = [(i, (i + 1) % devices) for i in range(devices - 1)]
        down = [(j, i) for i, j in up]
        last = lax.slice_in_dim(array, length - width, length, axis=dim)
        initial = lax.slice_in_dim(array, 0, width, axis=dim)
        before = lax.ppermute(last, axis, up)
        after = lax.ppermute(initial, axis, down)
        array = jnp.concatenate([before, array, after], axis=dim)
    return array


def node_diff(values, axis):
    length = values.shape[axis]
    lower_part = lax.slice_in_dim(values, 1, 2, axis=axis) - lax.slice_in_dim(
        values, 0, 1, axis=axis
    )
    middle = 0.5 * (
        lax.slice_in_dim(values, 2, length, axis=axis)
        - lax.slice_in_dim(values, 0, length - 2, axis=axis)
    )
    upper_part = lax.slice_in_dim(values, length - 1, length, axis=axis) - lax.slice_in_dim(
        values, length - 2, length - 1, axis=axis
    )
    return jnp.concatenate([lower_part, middle, upper_part], axis=axis)


def deformation(current):
    displaced = UNIT_LENGTH * current
    return [
        [node_diff(displaced[i], j) + (1.0 if i == j else 0.0) for j in range(3)] for i in range(3)
    ]


def determinant(grads):
    return (
        grads[0][0] * (grads[1][1] * grads[2][2] - grads[1][2] * grads[2][1])
        - grads[0][1] * (grads[1][0] * grads[2][2] - grads[1][2] * grads[2][0])
        + grads[0][2] * (grads[1][0] * grads[2][1] - grads[1][1] * grads[2][0])
    )


def cofactors(grads):
    return [
        [
            grads[1][1] * grads[2][2] - grads[1][2] * grads[2][1],
            grads[1][2] * grads[2][0] - grads[1][0] * grads[2][2],
            grads[1][0] * grads[2][1] - grads[1][1] * grads[2][0],
        ],
        [
            grads[0][2] * grads[2][1] - grads[0][1] * grads[2][2],
            grads[0][0] * grads[2][2] - grads[0][2] * grads[2][0],
            grads[0][1] * grads[2][0] - grads[0][0] * grads[2][1],
        ],
        [
            grads[0][1] * grads[1][2] - grads[0][2] * grads[1][1],
            grads[0][2] * grads[1][0] - grads[0][0] * grads[1][2],
            grads[0][0] * grads[1][1] - grads[0][1] * grads[1][0],
        ],
    ]


def dilation_rows(current, filled):
    grads = deformation(current)
    change = (determinant(grads) - 1.0) * filled * DILATION_SCALE
    return change.reshape(512, -1).astype(jnp.bfloat16)


def mech_update(current, material, pressure, filled, neighbours, first_mask, last_mask):
    grads = deformation(current)
    strain = [
        [
            0.5 * (sum((grads[k][i] * grads[k][j] for k in range(3))) - (1.0 if i == j else 0.0))
            for j in range(3)
        ]
        for i in range(3)
    ]
    strain_trace = strain[0][0] + strain[1][1] + strain[2][2]
    shear, lame_first, mobility = (material[0], material[1], material[2])
    stress_second = [
        [
            2.0 * shear * strain[i][j] + (lame_first * strain_trace if i == j else 0.0)
            for j in range(3)
        ]
        for i in range(3)
    ]
    cofactor_f = cofactors(grads)
    first_pk = [
        [
            sum((grads[i][k] * stress_second[k][j] for k in range(3))) - pressure * cofactor_f[i][j]
            for j in range(3)
        ]
        for i in range(3)
    ]
    forces = jnp.stack([sum((node_diff(first_pk[i][j], j) for j in range(3))) for i in range(3)])
    x_below, x_below_fill, x_above, x_above_fill = neighbours
    penalty = PENALTY * UNIT_LENGTH
    forces = forces.at[:, 0].add(penalty * x_below_fill * (x_below - current[:, 0]))
    forces = forces.at[:, 7].add(penalty * x_above_fill * (x_above - current[:, 7]))
    zero_face = jnp.zeros_like(current[:, :, :, 0, :1])
    zero_fill = jnp.zeros_like(filled[:1])
    z_below = jnp.concatenate([zero_face, current[:, :, :, 7, :-1]], axis=-1)
    z_below_fill = jnp.concatenate([zero_fill, filled[:-1]]) * (1.0 - first_mask)
    z_above = jnp.concatenate([current[:, :, :, 0, 1:], zero_face], axis=-1)
    z_above_fill = jnp.concatenate([filled[1:], zero_fill]) * (1.0 - last_mask)
    forces = forces.at[:, :, :, 0].add(penalty * z_below_fill * (z_below - current[:, :, :, 0]))
    forces = forces.at[:, :, :, 7].add(penalty * z_above_fill * (z_above - current[:, :, :, 7]))
    return current + TIME_STEP / UNIT_LENGTH * mobility * filled * forces


def pressure_cells(fraction):
    return (fraction + CUBIC_TERM * fraction * fraction * fraction).astype(jnp.bfloat16)


def diffuse(padded, coeff_field):
    centre = padded[1:-1]
    beside = jnp.pad(centre, ((0, 0), (1, 1), (1, 1)), mode="edge")
    weight_all = 0.5 + padded * padded
    weight_centre = weight_all[1:-1]
    inflow = 0.5 * (weight_centre + weight_all[2:]) * (padded[2:] - centre)
    inflow = inflow + 0.5 * (weight_centre + weight_all[:-2]) * (padded[:-2] - centre)
    for neighbour in (
        beside[:, 2:, 1:-1],
        beside[:, :-2, 1:-1],
        beside[:, 1:-1, 2:],
        beside[:, 1:-1, :-2],
    ):
        inflow = inflow + 0.5 * (weight_centre + 0.5 + neighbour * neighbour) * (neighbour - centre)
    return centre + SWEEP_STEP * coeff_field * inflow


def to_octants(brick_field):
    depth = brick_field.shape[2]
    blocks = brick_field.reshape(2, 8, 2, 8, depth // 8, 8)
    return blocks.transpose(1, 3, 5, 0, 2, 4).reshape(512, 4 * (depth // 8))


def from_octants(octant_table, depth):
    blocks = octant_table.reshape(8, 8, 8, 2, 2, depth // 8)
    return blocks.transpose(3, 0, 4, 1, 5, 2).reshape(16, 16, depth)


def shards(state, material, occupied, brick_column, brick_octant):
    e_dev = state.shape[-1]
    n_blk = lax.axis_size("blk")
    n_grp = lax.axis_size("grp")
    capacity = max(2, 2 * e_dev // n_blk)
    slot_count = n_grp * n_blk * capacity
    column_width = n_blk * capacity
    depth = 6 * e_dev
    octant_count = 3 * e_dev
    grp_at = lax.axis_index("grp")
    blk_at = lax.axis_index("blk")
    solvent = grp_at == n_grp - 1
    current = state.reshape(3, 8, 8, 8, e_dev)
    node_material = material.reshape(3, 8, 8, 8, e_dev)
    diffusivity = material.reshape(16, 16, depth)
    filled = occupied.astype(jnp.float32)
    element_at = jnp.arange(e_dev)
    first_mask = (element_at == 0).astype(jnp.float32)
    last_mask = (element_at == e_dev - 1).astype(jnp.float32)
    column = brick_column[:, 0]
    same_before = (column[:, None] == column[None, :]) & (element_at[None, :] < element_at[:, None])
    column_rank = jnp.sum(same_before.astype(jnp.int32), axis=1)
    column_slots = column * capacity + column_rank
    my_slots = (n_grp - 1) * column_width + column_slots
    requests = jnp.full((slot_count,), -1, jnp.int32).at[my_slots].set(brick_octant)
    requests = jnp.where(solvent, jnp.full_like(requests, -1), requests)
    asked_for = lax.all_to_all(requests, ("grp", "blk"), split_axis=0, concat_axis=0, tiled=True)
    is_valid = asked_for >= 0
    gather_index = jnp.where(is_valid, asked_for, 0)
    drop_index = jnp.where(is_valid, asked_for, octant_count)
    empty_buffer = jnp.zeros((512, slot_count), jnp.bfloat16)
    keep_lower = jnp.where(blk_at == 0, 0.0, 1.0)
    keep_upper = jnp.where(blk_at == n_blk - 1, 0.0, 1.0)
    rim_mask = jnp.concatenate(
        [
            keep_lower * jnp.ones((1,), jnp.float32),
            jnp.ones((16,), jnp.float32),
            keep_upper * jnp.ones((1,), jnp.float32),
        ]
    )[:, None, None]

    def build_pressure(start):
        octant_table = to_octants(pressure_cells(start.reshape(16, 16, depth)))
        return jnp.where(
            is_valid[None, :], octant_table[:, gather_index], jnp.zeros((), jnp.bfloat16)
        )

    def build_dilation(start):
        return empty_buffer.at[:, my_slots].set(dilation_rows(start, filled))

    def deposit(brick_field, arrived):
        deposit_sum = (
            jnp.zeros((512, octant_count), jnp.float32)
            .at[:, drop_index]
            .add(arrived.astype(jnp.float32), mode="drop")
        )
        return brick_field + SWEEP_STEP * SOURCE_RATE * from_octants(deposit_sum, depth)

    def keep_field(brick_field, arrived):
        return brick_field

    for step_at in range(STEPS):
        outgoing = lax.cond(solvent, build_pressure, build_dilation, current)
        incoming = lax.all_to_all(outgoing, ("grp", "blk"), split_axis=1, concat_axis=1, tiled=True)
        x_below = passed_along((current[:, 7], filled), "blk", 1)
        x_above = passed_along((current[:, 0], filled), "blk", -1)
        neighbours = (x_below[0], x_below[1], x_above[0], x_above[1])
        brick_field = lax.cond(
            solvent, deposit, keep_field, current.reshape(16, 16, depth), incoming
        )
        stacked = jnp.stack([brick_field, diffusivity])
        padded_pair = padded_2(stacked, (("blk", 1),), 2)

        def two_sweeps(pair, coeff_field):
            inner_rim = diffuse(pair[0], pair[1][1:-1]) * rim_mask
            return diffuse(inner_rim, coeff_field)

        brick_field = lax.cond(
            solvent, two_sweeps, lambda pair, coeff_field: pair[0][2:-2], padded_pair, diffusivity
        )

        def mech_step(start, arrived):
            pressure = arrived[:, my_slots].astype(jnp.float32) * PRESSURE_SCALE
            return mech_update(
                start,
                node_material,
                pressure.reshape(8, 8, 8, e_dev),
                filled,
                neighbours,
                first_mask,
                last_mask,
            )

        advanced = lax.cond(solvent, lambda start, arrived: start, mech_step, current, incoming)
        current = jnp.where(solvent, brick_field.reshape(3, 8, 8, 8, e_dev), advanced)
    return current.reshape(state.shape)


def solution(mesh):
    in_specs = (
        P("grp", None, None, "blk"),
        P("grp", None, None, "blk"),
        P(("grp", "blk")),
        P(("grp", "blk"), None),
        P(("grp", "blk")),
    )
    out_specs = P("grp", None, None, "blk")
    return jax.shard_map(shards, mesh=mesh, in_specs=in_specs, out_specs=out_specs, check_vma=False)
```

```python
import functools

import jax
import jax.numpy as jnp
from jax import lax
from jax.experimental import pallas as pl
from jax.experimental.pallas import tpu as pltpu
from jax.sharding import PartitionSpec as P

STEPS = 2
UNIT_LENGTH = 0.02
TIME_STEP = 0.1
PENALTY = 1.0
PRESSURE_SCALE = 0.05
DILATION_SCALE = 50.0
SWEEP_STEP = 0.03
SOURCE_RATE = 2.0
CUBIC_TERM = 0.3

MESH = pl.DeviceIdType.MESH
F32 = jnp.float32
BF16 = jnp.bfloat16
LANES = 128
NODES = 512
CAP = 8
DEPTH_OCTANTS = 96
LAYER = 128


def iota(shape, dim):
    return lax.broadcasted_iota(jnp.int32, shape, dim)


def flag(mask, dtype=F32):
    return jnp.where(mask, 1.0, 0.0).astype(dtype)


def wait_all(ref, sem):
    pltpu.make_async_copy(ref, ref, sem).wait()


def rows_of(ref, start, count):
    return ref[pl.ds(pl.multiple_of(start, count), count), :]


def slab(ref, r, i):
    return rows_of(ref, r * 512 + i * 64, 64).reshape(8, 8, LANES)


def put_slab(ref, r, i, value):
    ref[pl.ds(pl.multiple_of(r * 512 + i * 64, 64), 64), :] = value.reshape(64, LANES)


def along_j(s):
    return jnp.concatenate([s[1:2] - s[0:1], 0.5 * (s[2:] - s[:-2]), s[7:8] - s[6:7]], axis=0)


def along_k(s):
    k = iota(s.shape, 1)
    edge = (k == 0) | (k == 7)
    upper = jnp.where(k == 7, s, pltpu.roll(s, 7, 1))
    lower = jnp.where(k == 0, s, pltpu.roll(s, 1, 1))
    return (upper - lower) * jnp.where(edge, 1.0, 0.5)


def i_span(i):
    below, above = jnp.maximum(i - 1, 0), jnp.minimum(i + 1, 7)
    return below, above, jnp.where((i == 0) | (i == 7), 1.0, 0.5)


def gradients(cur, i):
    below, above, scale = i_span(i)
    grads = []
    for r in range(3):
        s = slab(cur, r, i)
        row = [
            (slab(cur, r, above) - slab(cur, r, below)) * (UNIT_LENGTH * scale),
            along_j(s) * UNIT_LENGTH,
            along_k(s) * UNIT_LENGTH,
        ]
        row[r] = row[r] + 1.0
        grads.append(row)
    return grads


def cofactors(f):
    return [
        [
            f[1][1] * f[2][2] - f[1][2] * f[2][1],
            f[1][2] * f[2][0] - f[1][0] * f[2][2],
            f[1][0] * f[2][1] - f[1][1] * f[2][0],
        ],
        [
            f[0][2] * f[2][1] - f[0][1] * f[2][2],
            f[0][0] * f[2][2] - f[0][2] * f[2][0],
            f[0][1] * f[2][0] - f[0][0] * f[2][1],
        ],
        [
            f[0][1] * f[1][2] - f[0][2] * f[1][1],
            f[0][2] * f[1][0] - f[0][0] * f[1][2],
            f[0][0] * f[1][1] - f[0][1] * f[1][0],
        ],
    ]


def kernel(
    n_grp,
    n_blk,
    state_ref,
    material_ref,
    occupied_ref,
    column_ref,
    octant_ref,
    out_ref,
    cur,
    mat,
    perm,
    oct_send,
    dil_send,
    dil_rows,
    press_in,
    press,
    face_in,
    fill_in,
    fill_send,
    piola,
    part,
    oct_in,
    dil_in,
    press_send,
    hits,
    select,
    pieces,
    phi_a,
    phi_b,
    diff,
    pi_rows,
    load_sem,
    oct_send_sem,
    oct_sem,
    dil_send_sem,
    dil_sem,
    press_send_sem,
    press_sem,
    face_send_sem,
    face_sem,
    fill_send_sem,
    fill_sem,
    halo_send_sem,
    halo_sem,
    rim_send_sem,
    rim_sem,
):
    grp, blk = lax.axis_index("grp"), lax.axis_index("blk")
    n_mech = n_grp - 1
    solvent = grp == n_mech
    barrier = pltpu.get_barrier_semaphore()
    has_below, has_above = blk > 0, blk < n_blk - 1
    loads = [
        pltpu.make_async_copy(state_ref, cur, load_sem.at[0]),
        pltpu.make_async_copy(material_ref, mat, load_sem.at[1]),
    ]
    for copy in loads:
        copy.start()

    def greet(g, c):
        pl.semaphore_signal(barrier, inc=1, device_id=(g, c), device_id_type=MESH)

    @pl.when(has_below)
    def _():
        greet(grp, blk - 1)

    @pl.when(has_above)
    def _():
        greet(grp, blk + 1)

    beside = jnp.where(has_below, 1, 0) + jnp.where(has_above, 1, 0)

    def send(src, dst, send_sem, recv_sem, g, c):
        copy = pltpu.make_async_remote_copy(
            src_ref=src,
            dst_ref=dst,
            send_sem=send_sem,
            recv_sem=recv_sem,
            device_id=(g, c),
            device_id_type=MESH,
        )
        copy.start()

    def mechanics():
        def greet_column(it, carry):
            greet(n_mech, lax.rem(blk + it, n_blk))
            return carry

        lax.fori_loop(0, n_blk, greet_column, 0)
        filled = occupied_ref[...].astype(F32)
        column = column_ref[...].astype(F32)
        square = (LANES, LANES)
        across = jnp.broadcast_to(column, square)
        diagonal = iota(square, 0) == iota(square, 1)
        down = jnp.sum(jnp.where(diagonal, across, 0.0), axis=1, keepdims=True)
        before = (down == across) & (iota(square, 0) < iota(square, 1))
        rank = jnp.sum(flag(before), axis=0, keepdims=True)
        slot = column * CAP + rank
        slots = n_blk * CAP
        hit = iota((slots, LANES), 0).astype(F32) == slot
        perm[...] = flag(hit, BF16)
        wanted = jnp.sum(
            jnp.where(hit, octant_ref[...].astype(F32) + 1.0, 0.0), axis=1, keepdims=True
        )
        oct_send[...] = jnp.broadcast_to(wanted - 1.0, (slots, LANES)).reshape(n_blk, CAP, LANES)
        fill_send[...] = jnp.broadcast_to(filled, (8, LANES))
        k = iota((8, LANES), 0)
        e = iota((8, LANES), 1)
        filled_8 = jnp.broadcast_to(filled, (8, LANES))
        fill_below = jnp.where(e == 0, 0.0, pltpu.roll(filled_8, 1, 1))
        fill_above = jnp.where(e == LANES - 1, 0.0, pltpu.roll(filled_8, LANES - 1, 1))
        k_weight = (PENALTY * UNIT_LENGTH) * jnp.where(
            k == 0, fill_below, jnp.where(k == 7, fill_above, 0.0)
        )

        pl.semaphore_wait(barrier, n_blk + beside)

        mine = grp * n_blk + blk

        def send_octants(it, carry):
            c = lax.rem(blk + 11 * grp + it, n_blk)
            send(oct_send.at[c], oct_in.at[mine], oct_send_sem, oct_sem, n_mech, c)
            return carry

        lax.fori_loop(0, n_blk, send_octants, 0)

        @pl.when(has_above)
        def _():
            send(fill_send, fill_in.at[0], fill_send_sem.at[1], fill_sem.at[0], grp, blk + 1)

        @pl.when(has_below)
        def _():
            send(fill_send, fill_in.at[1], fill_send_sem.at[0], fill_sem.at[1], grp, blk - 1)

        @pl.when(jnp.logical_not(has_below))
        def _():
            fill_in[0] = jnp.zeros((8, LANES), F32)
            for step in range(STEPS):
                face_in[step, 0] = jnp.zeros((192, LANES), F32)

        @pl.when(jnp.logical_not(has_above))
        def _():
            fill_in[1] = jnp.zeros((8, LANES), F32)
            for step in range(STEPS):
                face_in[step, 1] = jnp.zeros((192, LANES), F32)

        loads[0].wait()

        def dilate(i, carry):
            f = gradients(cur, i)
            det = (
                f[0][0] * (f[1][1] * f[2][2] - f[1][2] * f[2][1])
                - f[0][1] * (f[1][0] * f[2][2] - f[1][2] * f[2][0])
                + f[0][2] * (f[1][0] * f[2][1] - f[1][1] * f[2][0])
            )
            change = (det - 1.0) * filled * DILATION_SCALE
            row = pl.multiple_of(i * 64, 64)
            dil_rows[pl.ds(row, 64), :] = change.reshape(64, LANES).astype(BF16)
            return carry

        def elastic(i, carry):
            f = gradients(cur, i)
            shear, lame = slab(mat, 0, i), slab(mat, 1, i)
            c = [[None] * 3 for _ in range(3)]
            for a in range(3):
                for b in range(a, 3):
                    c[a][b] = f[0][a] * f[0][b] + f[1][a] * f[1][b] + f[2][a] * f[2][b]
                c[a][a] = c[a][a] - 1.0
            trace = (0.5 * lame) * (c[0][0] + c[1][1] + c[2][2])
            s = [[None] * 3 for _ in range(3)]
            for a in range(3):
                for b in range(a, 3):
                    s[a][b] = s[b][a] = shear * c[a][b]
            for a in range(3):
                s[a][a] = s[a][a] + trace
            for r in range(3):
                p = [f[r][0] * s[0][j] + f[r][1] * s[1][j] + f[r][2] * s[2][j] for j in range(3)]
                put_slab(piola, r, i, p[0])
                put_slab(part, r, i, along_j(p[1]) + along_k(p[2]))
            return carry

        def swell(i, carry):
            cof = cofactors(gradients(cur, i))
            row = pl.multiple_of(i * 64, 64)
            pressure = press[pl.ds(row, 64), :].reshape(8, 8, LANES)
            for r in range(3):
                p = [pressure * cof[r][j] for j in range(3)]
                put_slab(piola, r, i, slab(piola, r, i) - p[0])
                put_slab(part, r, i, slab(part, r, i) - (along_j(p[1]) + along_k(p[2])))
            return carry

        def advance(i, carry):
            below, above, scale = i_span(i)
            gain = (TIME_STEP / UNIT_LENGTH) * slab(mat, 2, i) * filled
            at_first = iota((8, 8, LANES), 1) == 0
            for r in range(3):
                s = slab(cur, r, i)
                force = slab(part, r, i) + (slab(piola, r, above) - slab(piola, r, below)) * scale
                z_below = pltpu.roll(pltpu.roll(s, 1, 1), 1, 2)
                z_above = pltpu.roll(pltpu.roll(s, 7, 1), LANES - 1, 2)
                force = force + k_weight * (jnp.where(at_first, z_below, z_above) - s)
                put_slab(cur, r, i, s + gain * force)
            return carry

        for step in range(STEPS):
            if step == 0:
                loads_done = None
            for r in range(3):

                @pl.when(has_above)
                def _():
                    send(
                        cur.at[pl.ds(r * 512 + 448, 64)],
                        face_in.at[step, 0, pl.ds(r * 64, 64)],
                        face_send_sem.at[step, 1],
                        face_sem.at[step, 0],
                        grp,
                        blk + 1,
                    )

                @pl.when(has_below)
                def _():
                    send(
                        cur.at[pl.ds(r * 512, 64)],
                        face_in.at[step, 1, pl.ds(r * 64, 64)],
                        face_send_sem.at[step, 0],
                        face_sem.at[step, 1],
                        grp,
                        blk - 1,
                    )

            lax.fori_loop(0, 8, dilate, 0)
            if step > 0:
                wait_all(dil_send, dil_send_sem.at[step - 1])
            taken = lax.dot_general(
                perm[...], dil_rows[...], (((1,), (1,)), ((), ())), preferred_element_type=F32
            )
            dil_send[...] = taken.reshape(n_blk, CAP, NODES).astype(BF16)

            def send_dilation(it, carry):
                c = lax.rem(blk + 11 * grp + it, n_blk)
                send(
                    dil_send.at[c],
                    dil_in.at[step, mine],
                    dil_send_sem.at[step],
                    dil_sem.at[step],
                    n_mech,
                    c,
                )
                return carry

            lax.fori_loop(0, n_blk, send_dilation, 0)
            if step == 0:
                loads[1].wait()
            lax.fori_loop(0, 8, elastic, 0)
            wait_all(press_in.at[step], press_sem.at[step])
            arrived = press_in[step].astype(F32).reshape(slots, NODES).astype(BF16)
            press[...] = PRESSURE_SCALE * lax.dot_general(
                arrived, perm[...], (((0,), (0,)), ((), ())), preferred_element_type=F32
            )
            lax.fori_loop(0, 8, swell, 0)
            for side, present in ((0, has_below), (1, has_above)):

                @pl.when(present)
                def _():
                    wait_all(face_in.at[step, side], face_sem.at[step, side])
                    wait_all(face_in.at[step, side], face_send_sem.at[step, side])
                    if step == 0:
                        wait_all(fill_send, fill_sem.at[side])
                        wait_all(fill_send, fill_send_sem.at[side])

                at = 7 * side
                weight = (PENALTY * UNIT_LENGTH) * fill_in[side]
                for r in range(3):
                    other = face_in[step, side, pl.ds(r * 64, 64), :].reshape(8, 8, LANES)
                    extra = weight * (other - slab(cur, r, at))
                    put_slab(part, r, at, slab(part, r, at) + extra)
            lax.fori_loop(0, 8, advance, 0)
        wait_all(oct_send, oct_send_sem)
        wait_all(dil_send, dil_send_sem.at[STEPS - 1])

    def brick():
        def greet_elements(it, carry):
            m = lax.rem(3 * blk + it, n_mech * n_blk)
            greet(m // n_blk, lax.rem(m, n_blk))
            return carry

        lax.fori_loop(0, n_mech * n_blk, greet_elements, 0)
        row = iota((768, LANES), 0)
        at_octant = row // 8 == iota((768, LANES), 1)
        for k in range(8):
            select[:, k * LANES : (k + 1) * LANES] = flag(at_octant & (row % 8 == k), BF16)
        q = iota((8, LANES), 1)
        k_at = iota((8, LANES), 0)
        inside = flag((k_at < 7) | (q < DEPTH_OCTANTS - 1))

        def split(value, row, lanes):
            high = value.astype(BF16)
            rest = value - high.astype(F32)
            middle = rest.astype(BF16)
            low = (rest - middle.astype(F32)).astype(BF16)
            for at, piece in enumerate((high, middle, low)):
                pieces[at * 256 + row : at * 256 + row + 256, lanes] = piece

        def joined(product):
            return product[0:256] + product[256:512] + product[512:768]

        def to_layers(source, target, first_row, scale):
            for zq in range(6):
                split(source[pl.ds(zq, 256, stride=6), :], 0, slice(zq * LANES, zq * LANES + LANES))
            for pair in range(4):
                lanes = slice(pair * 256, pair * 256 + 256)
                both = joined(
                    jnp.dot(pieces[:, 0:768], select[:, lanes], preferred_element_type=F32)
                )
                for half in range(2):
                    target[pl.ds(first_row + 2 * pair + half, 256, stride=8), :] = (
                        scale * both[:, half * LANES : (half + 1) * LANES]
                    )

        def from_layers(source, first_row, target):
            for k in range(8):
                lanes = slice(k * LANES, (k + 1) * LANES)
                split(source[pl.ds(first_row + k, 256, stride=8), :], 0, lanes)
            for pair in range(3):
                both = joined(
                    lax.dot_general(
                        pieces[...],
                        select[pair * 256 : pair * 256 + 256, :],
                        (((1,), (1,)), ((), ())),
                        preferred_element_type=F32,
                    )
                )
                for half in range(2):
                    target[pl.ds(2 * pair + half, 256, stride=6), :] = both[
                        :, half * LANES : (half + 1) * LANES
                    ]

        def layer(ref, at):
            return rows_of(ref, at * LAYER, LAYER).reshape(16, 8, LANES)

        def half_weight(v):
            return 0.25 + 0.5 * v * v

        def sweep(source, source_first, target, target_first, diff_first, count):
            start = layer(source, source_first)
            before = layer(source, source_first - 1)
            flux = (half_weight(start) + half_weight(before)) * (start - before)
            in_k = iota((16, 8, LANES), 1)

            def one_layer(x, carry):
                centre, entering = carry
                ahead = layer(source, source_first + 1 + x)
                weight = half_weight(centre)
                leaving = (weight + half_weight(ahead)) * (ahead - centre)
                inflow = leaving - entering
                along_y = (weight[1:] + weight[:-1]) * (centre[1:] - centre[:-1])
                none = jnp.zeros((1, 8, LANES), F32)
                inflow = inflow + (
                    jnp.concatenate([along_y, none], axis=0)
                    - jnp.concatenate([none, along_y], axis=0)
                )
                shifted = pltpu.roll(centre, 7, 1)
                upper = jnp.where(in_k == 7, pltpu.roll(shifted, LANES - 1, 2), shifted)
                along_z = inside * ((weight + half_weight(upper)) * (upper - centre))
                shifted = pltpu.roll(along_z, 1, 1)
                inflow = inflow + (
                    along_z - jnp.where(in_k == 0, pltpu.roll(shifted, 1, 2), shifted)
                )
                updated = centre + layer(diff, diff_first + x) * inflow
                at = pl.multiple_of((target_first + x) * LAYER, LAYER)
                target[pl.ds(at, LAYER), :] = updated.reshape(LAYER, LANES)
                return ahead, leaving

            lax.fori_loop(0, count, one_layer, (start, flux))

        loads[0].wait()
        to_layers(cur, phi_a.at[0], 2 * LAYER, 1.0)

        def octant_block(ref, t, first):
            x, y = 8 * (t // 2), 8 * (t % 2)
            return [rows_of(ref, ((first + x + i) * 16 + y) * 8, 64) for i in range(8)]

        def make_pressure(step):
            for t in range(4):
                value = jnp.concatenate(octant_block(phi_a.at[step], t, 2), axis=0)
                value = value + CUBIC_TERM * value * value * value
                pi_rows[:, t * LANES : (t + 1) * LANES] = value.astype(BF16)

        def send_pressure(step):
            for g in range(n_mech):
                rows = slice(g * n_blk * CAP, (g + 1) * n_blk * CAP)
                taken = lax.dot_general(
                    hits[rows, :],
                    pi_rows[...],
                    (((1,), (1,)), ((), ())),
                    preferred_element_type=F32,
                )
                press_send[step, g * n_blk : (g + 1) * n_blk] = taken.reshape(
                    n_blk, CAP, NODES
                ).astype(BF16)

                def send_one(it, carry):
                    c = lax.rem(blk + 11 * g + it, n_blk)
                    send(
                        press_send.at[step, g * n_blk + c],
                        press_in.at[step, blk],
                        press_send_sem.at[step],
                        press_sem.at[step],
                        g,
                        c,
                    )
                    return carry

                lax.fori_loop(0, n_blk, send_one, 0)

        make_pressure(0)
        pl.semaphore_wait(barrier, n_mech * n_blk + beside)
        wait_all(oct_in, oct_sem)
        wanted = oct_in[...].reshape(n_mech * n_blk * CAP, LANES)
        lane = iota(wanted.shape, 1)
        for t in range(4):
            mine = (wanted == (lane + t * DEPTH_OCTANTS).astype(F32)) & (lane < DEPTH_OCTANTS)
            hits[:, t * LANES : (t + 1) * LANES] = flag(mine, BF16)
        send_pressure(0)
        loads[1].wait()
        to_layers(mat, diff, LAYER, SWEEP_STEP)

        @pl.when(has_above)
        def _():
            send(
                diff.at[pl.ds(16 * LAYER, LAYER)],
                diff.at[pl.ds(0, LAYER)],
                rim_send_sem.at[1],
                rim_sem.at[0],
                grp,
                blk + 1,
            )

        @pl.when(has_below)
        def _():
            send(
                diff.at[pl.ds(LAYER, LAYER)],
                diff.at[pl.ds(17 * LAYER, LAYER)],
                rim_send_sem.at[0],
                rim_sem.at[1],
                grp,
                blk - 1,
            )

        @pl.when(jnp.logical_not(has_below))
        def _():
            diff[0:LAYER, :] = jnp.zeros((LAYER, LANES), F32)
            for step in range(STEPS):
                phi_a[step, 0 : 2 * LAYER, :] = jnp.zeros((2 * LAYER, LANES), F32)

        @pl.when(jnp.logical_not(has_above))
        def _():
            diff[17 * LAYER : 18 * LAYER, :] = jnp.zeros((LAYER, LANES), F32)
            for step in range(STEPS):
                phi_a[step, 18 * LAYER : 20 * LAYER, :] = jnp.zeros((2 * LAYER, LANES), F32)

        for step in range(STEPS):
            phi = phi_a.at[step]
            if step > 0:
                make_pressure(step)
                send_pressure(step)
            wait_all(dil_in.at[step], dil_sem.at[step])
            arrived = dil_in[step].astype(F32).reshape(n_mech * n_blk * CAP, NODES).astype(BF16)
            for pair in range(2):
                lanes = slice(pair * 256, pair * 256 + 256)
                total = lax.dot_general(
                    arrived, hits[:, lanes], (((0,), (0,)), ((), ())), preferred_element_type=F32
                )
                for half in range(2):
                    x, y = 8 * pair, 8 * half
                    for i in range(8):
                        at = ((2 + x + i) * 16 + y) * 8
                        phi[at : at + 64, :] = phi[at : at + 64, :] + (
                            SWEEP_STEP * SOURCE_RATE
                        ) * total[i * 64 : i * 64 + 64, half * LANES : (half + 1) * LANES]

            @pl.when(has_above)
            def _():
                send(
                    phi.at[pl.ds(16 * LAYER, 2 * LAYER)],
                    phi.at[pl.ds(0, 2 * LAYER)],
                    halo_send_sem.at[step, 1],
                    halo_sem.at[step, 0],
                    grp,
                    blk + 1,
                )

            @pl.when(has_below)
            def _():
                send(
                    phi.at[pl.ds(2 * LAYER, 2 * LAYER)],
                    phi.at[pl.ds(18 * LAYER, 2 * LAYER)],
                    halo_send_sem.at[step, 0],
                    halo_sem.at[step, 1],
                    grp,
                    blk - 1,
                )

            for side, present, first in ((0, has_below, 0), (1, has_above, 18)):

                @pl.when(present)
                def _():
                    two = phi.at[pl.ds(first * LAYER, 2 * LAYER)]
                    wait_all(two, halo_sem.at[step, side])
                    wait_all(two, halo_send_sem.at[step, side])
                    if step == 0:
                        one = diff.at[pl.ds(0, LAYER)]
                        wait_all(one, rim_sem.at[side])
                        wait_all(one, rim_send_sem.at[side])

            sweep(phi, 1, phi_b, 0, 0, 18)
            sweep(phi_b, 1, phi_a.at[(step + 1) % 2], 2, 1, 16)
            wait_all(press_send.at[step], press_send_sem.at[step])
        from_layers(phi_a.at[STEPS % 2], 2 * LAYER, cur)

    @pl.when(solvent)
    def _():
        brick()

    @pl.when(jnp.logical_not(solvent))
    def _():
        mechanics()

    store = pltpu.make_async_copy(cur, out_ref, load_sem.at[0])
    store.start()
    store.wait()


def solution(mesh):
    n_grp, n_blk = mesh.shape["grp"], mesh.shape["blk"]
    n_mech = n_grp - 1
    slots = n_blk * CAP
    dma = pltpu.SemaphoreType.DMA
    vmem = pltpu.VMEM
    whole = (1536, LANES)
    call = pl.pallas_call(
        functools.partial(kernel, n_grp, n_blk),
        out_shape=jax.ShapeDtypeStruct(whole, F32),
        in_specs=[pl.BlockSpec(memory_space=pl.ANY)] * 2 + [pl.BlockSpec(memory_space=vmem)] * 3,
        out_specs=pl.BlockSpec(memory_space=pl.ANY),
        scratch_shapes=[
            vmem(whole, F32),
            vmem(whole, F32),
            vmem((slots, LANES), BF16),
            vmem((n_blk, CAP, LANES), F32),
            vmem((n_blk, CAP, NODES), BF16),
            vmem((NODES, LANES), BF16),
            vmem((STEPS, n_blk, CAP, NODES), BF16),
            vmem((NODES, LANES), F32),
            vmem((STEPS, 2, 192, LANES), F32),
            vmem((2, 8, LANES), F32),
            vmem((8, LANES), F32),
            vmem(whole, F32),
            vmem(whole, F32),
            vmem((n_mech * n_blk, CAP, LANES), F32),
            vmem((STEPS, n_mech * n_blk, CAP, NODES), BF16),
            vmem((STEPS, n_mech * n_blk, CAP, NODES), BF16),
            vmem((n_mech * n_blk * CAP, NODES), BF16),
            vmem((768, 1024), BF16),
            vmem((768, 1024), BF16),
            vmem((2, 20 * LAYER, LANES), F32),
            vmem((18 * LAYER, LANES), F32),
            vmem((18 * LAYER, LANES), F32),
            vmem((NODES, NODES), BF16),
            dma((2,)),
            dma,
            dma,
            dma((STEPS,)),
            dma((STEPS,)),
            dma((STEPS,)),
            dma((STEPS,)),
            dma((STEPS, 2)),
            dma((STEPS, 2)),
            dma((2,)),
            dma((2,)),
            dma((STEPS, 2)),
            dma((STEPS, 2)),
            dma((2,)),
            dma((2,)),
        ],
        compiler_params=pltpu.CompilerParams(
            collective_id=0, has_side_effects=True, vmem_limit_bytes=48 << 20
        ),
    )

    def shards(state, material, occupied, brick_column, brick_octant):
        out = call(
            state.reshape(whole),
            material.reshape(whole),
            occupied.reshape(1, LANES),
            brick_column.reshape(1, LANES),
            brick_octant.reshape(1, LANES),
        )
        return out.reshape(state.shape)

    in_specs = (
        P("grp", None, None, "blk"),
        P("grp", None, None, "blk"),
        P(("grp", "blk")),
        P(("grp", "blk"), None),
        P(("grp", "blk")),
    )
    out_specs = P("grp", None, None, "blk")
    return jax.shard_map(shards, mesh=mesh, in_specs=in_specs, out_specs=out_specs, check_vma=False)
```

```python
import contextlib
import functools

import jax
import jax.numpy as jnp
from jax import lax
from jax.experimental import pallas as pl
from jax.experimental.pallas import tpu as pltpu
from jax.sharding import PartitionSpec as P

STEPS = 2
UNIT_LENGTH = 0.02
TIME_STEP = 0.1
PENALTY = 1.0
PRESSURE_SCALE = 0.05
DILATION_SCALE = 50.0
SWEEP_STEP = 0.03
SOURCE_RATE = 2.0
CUBIC_TERM = 0.3

MESH = pl.DeviceIdType.MESH
F32 = jnp.float32
BF16 = jnp.bfloat16
LANES = 128
NODES = 512
CAP = 8
DEPTH_OCTANTS = 96
CODE_SHIFT = 191.0
EMPTY_CODE = -1000.0
LAYER = 128


def phase(name):
    return contextlib.nullcontext()


def iota(shape, dim):
    return lax.broadcasted_iota(jnp.int32, shape, dim)


def flag(mask, dtype=F32):
    return jnp.where(mask, 1.0, 0.0).astype(dtype)


def wait_all(ref, sem):
    pltpu.make_async_copy(ref, ref, sem).wait()


def rows_of(ref, start, count):
    return ref[pl.ds(pl.multiple_of(start, count), count), :]


def slab(ref, r, i):
    return rows_of(ref, r * 512 + i * 64, 64).reshape(8, 8, LANES)


def put_slab(ref, r, i, value):
    ref[pl.ds(pl.multiple_of(r * 512 + i * 64, 64), 64), :] = value.reshape(64, LANES)


def along_j(s):
    return jnp.concatenate([s[1:2] - s[0:1], 0.5 * (s[2:] - s[:-2]), s[7:8] - s[6:7]], axis=0)


def along_k(s):
    k = iota(s.shape, 1)
    edge = (k == 0) | (k == 7)
    upper = jnp.where(k == 7, s, pltpu.roll(s, 7, 1))
    lower = jnp.where(k == 0, s, pltpu.roll(s, 1, 1))
    return (upper - lower) * jnp.where(edge, 1.0, 0.5)


def i_span(i):
    below, above = jnp.maximum(i - 1, 0), jnp.minimum(i + 1, 7)
    return below, above, jnp.where((i == 0) | (i == 7), 1.0, 0.5)


def gradients(cur, i):
    below, above, scale = i_span(i)
    grads = []
    for r in range(3):
        s = slab(cur, r, i)
        row = [
            (slab(cur, r, above) - slab(cur, r, below)) * (UNIT_LENGTH * scale),
            along_j(s) * UNIT_LENGTH,
            along_k(s) * UNIT_LENGTH,
        ]
        row[r] = row[r] + 1.0
        grads.append(row)
    return grads


def cofactors(f):
    return [
        [
            f[1][1] * f[2][2] - f[1][2] * f[2][1],
            f[1][2] * f[2][0] - f[1][0] * f[2][2],
            f[1][0] * f[2][1] - f[1][1] * f[2][0],
        ],
        [
            f[0][2] * f[2][1] - f[0][1] * f[2][2],
            f[0][0] * f[2][2] - f[0][2] * f[2][0],
            f[0][1] * f[2][0] - f[0][0] * f[2][1],
        ],
        [
            f[0][1] * f[1][2] - f[0][2] * f[1][1],
            f[0][2] * f[1][0] - f[0][0] * f[1][2],
            f[0][0] * f[1][1] - f[0][1] * f[1][0],
        ],
    ]


def kernel(
    n_grp,
    n_blk,
    state_ref,
    material_ref,
    occupied_ref,
    column_ref,
    octant_ref,
    cur,
    mat,
    occupied_in,
    column_in,
    octant_in,
    perm,
    oct_send,
    dil_send,
    dil_rows,
    press_in,
    press,
    face_in,
    fill_in,
    fill_send,
    piola,
    part,
    cofactor,
    oct_in,
    dil_in,
    press_send,
    hits,
    select,
    pieces,
    phi_a,
    phi_b,
    diff,
    pi_rows,
    total,
    load_sem,
    small_sem,
    oct_send_sem,
    oct_sem,
    dil_send_sem,
    dil_sem,
    press_send_sem,
    press_sem,
    face_send_sem,
    face_sem,
    fill_send_sem,
    fill_sem,
    halo_send_sem,
    halo_sem,
    rim_send_sem,
    rim_sem,
):
    grp, blk = lax.axis_index("grp"), lax.axis_index("blk")
    n_mech = n_grp - 1
    solvent = grp == n_mech
    barrier = pltpu.get_barrier_semaphore()
    has_below, has_above = blk > 0, blk < n_blk - 1
    loads = [
        pltpu.make_async_copy(state_ref, cur, load_sem.at[0]),
        pltpu.make_async_copy(material_ref, mat, load_sem.at[1]),
    ]
    for copy in loads:
        copy.start()

    def greet(g, c):
        pl.semaphore_signal(barrier, inc=1, device_id=(g, c), device_id_type=MESH)

    @pl.when(has_below)
    def _():
        greet(grp, blk - 1)

    @pl.when(has_above)
    def _():
        greet(grp, blk + 1)

    beside = jnp.where(has_below, 1, 0) + jnp.where(has_above, 1, 0)

    def send(src, dst, send_sem, recv_sem, g, c):
        copy = pltpu.make_async_remote_copy(
            src_ref=src,
            dst_ref=dst,
            send_sem=send_sem,
            recv_sem=recv_sem,
            device_id=(g, c),
            device_id_type=MESH,
        )
        copy.start()

    def mechanics():
        small = [
            pltpu.make_async_copy(source, target, small_sem.at[at])
            for at, (source, target) in enumerate(
                (
                    (occupied_ref, occupied_in),
                    (column_ref, column_in),
                    (octant_ref, octant_in),
                )
            )
        ]
        for copy in small:
            copy.start()
        with phase("m_small"):
            for copy in small:
                copy.wait()
        filled = occupied_in[...].astype(F32)
        column = column_in[...].astype(F32)
        octant = octant_in[...].astype(F32)
        square = (LANES, LANES)
        across = jnp.broadcast_to(column, square)
        diagonal = iota(square, 0) == iota(square, 1)
        down = jnp.sum(jnp.where(diagonal, across, 0.0), axis=1, keepdims=True)
        same = down == across
        rank = jnp.sum(flag(same & (iota(square, 0) < iota(square, 1))), axis=0, keepdims=True)
        rank_down = jnp.sum(
            flag(same & (iota(square, 1) < iota(square, 0))), axis=1, keepdims=True
        )
        slot = column * CAP + rank
        slots = n_blk * CAP
        hit = iota((slots, LANES), 0).astype(F32) == slot
        perm[...] = flag(hit, BF16)
        at_column = iota((n_blk, LANES), 0).astype(F32) == column
        coded = jnp.concatenate(
            [jnp.where(at_column, octant - CODE_SHIFT, 0.0), flag(at_column)], axis=0
        ).astype(BF16)
        at_rank = flag(iota(square, 1).astype(F32) == rank_down, BF16)
        placed = jnp.dot(coded, at_rank, preferred_element_type=F32)
        code = placed[0:n_blk] + EMPTY_CODE * (1.0 - placed[n_blk : 2 * n_blk])
        for c in range(n_blk):
            oct_send[c] = code[c : c + 1, :]
        fill_send[...] = jnp.broadcast_to(filled, (8, LANES))
        k = iota((8, LANES), 0)
        e = iota((8, LANES), 1)
        filled_8 = jnp.broadcast_to(filled, (8, LANES))
        fill_below = jnp.where(e == 0, 0.0, pltpu.roll(filled_8, 1, 1))
        fill_above = jnp.where(e == LANES - 1, 0.0, pltpu.roll(filled_8, LANES - 1, 1))
        k_weight = (PENALTY * UNIT_LENGTH) * jnp.where(
            k == 0, fill_below, jnp.where(k == 7, fill_above, 0.0)
        )

        with phase("m_barrier"):
            pl.semaphore_wait(barrier, n_blk + beside)

        mine = grp * n_blk + blk

        def send_octants(it, carry):
            c = lax.rem(blk + 11 * grp + it, n_blk)
            send(oct_send.at[c], oct_in.at[mine], oct_send_sem, oct_sem, n_mech, c)
            return carry

        with phase("m_send_oct"):
            lax.fori_loop(0, n_blk, send_octants, 0)

        @pl.when(jnp.logical_not(has_below))
        def _():
            fill_in[0] = jnp.zeros((8, LANES), F32)
            for step in range(STEPS):
                face_in[step, 0] = jnp.zeros((192, LANES), F32)

        @pl.when(jnp.logical_not(has_above))
        def _():
            fill_in[1] = jnp.zeros((8, LANES), F32)
            for step in range(STEPS):
                face_in[step, 1] = jnp.zeros((192, LANES), F32)

        with phase("m_load"):
            loads[0].wait()

        def dilate(i, carry):
            f = gradients(cur, i)
            det = (
                f[0][0] * (f[1][1] * f[2][2] - f[1][2] * f[2][1])
                - f[0][1] * (f[1][0] * f[2][2] - f[1][2] * f[2][0])
                + f[0][2] * (f[1][0] * f[2][1] - f[1][1] * f[2][0])
            )
            change = (det - 1.0) * filled * DILATION_SCALE
            for j in range(8):
                dil_rows[pl.ds(i * 8 + j, 8, stride=64), :] = change[j]
            return carry

        def elastic(i, carry):
            f = gradients(cur, i)
            shear, lame = slab(mat, 0, i), slab(mat, 1, i)
            c = [[None] * 3 for _ in range(3)]
            for a in range(3):
                for b in range(a, 3):
                    c[a][b] = f[0][a] * f[0][b] + f[1][a] * f[1][b] + f[2][a] * f[2][b]
                c[a][a] = c[a][a] - 1.0
            trace = (0.5 * lame) * (c[0][0] + c[1][1] + c[2][2])
            s = [[None] * 3 for _ in range(3)]
            for a in range(3):
                for b in range(a, 3):
                    s[a][b] = s[b][a] = shear * c[a][b]
            for a in range(3):
                s[a][a] = s[a][a] + trace
            for r in range(3):
                p = [f[r][0] * s[0][j] + f[r][1] * s[1][j] + f[r][2] * s[2][j] for j in range(3)]
                put_slab(piola, r, i, p[0])
                put_slab(part, r, i, along_j(p[1]) + along_k(p[2]))
            cof = cofactors(f)
            for r in range(3):
                for j in range(3):
                    put_slab(cofactor, 3 * r + j, i, cof[r][j])
            return carry

        def swell(i, carry):
            pressure = jnp.concatenate(
                [press[pl.ds(i * 8 + j, 8, stride=64), :][None] for j in range(8)], axis=0
            )
            for r in range(3):
                p = [pressure * slab(cofactor, 3 * r + j, i) for j in range(3)]
                put_slab(piola, r, i, slab(piola, r, i) - p[0])
                put_slab(part, r, i, slab(part, r, i) - (along_j(p[1]) + along_k(p[2])))
            return carry

        def advance(i, carry):
            below, above, scale = i_span(i)
            gain = (TIME_STEP / UNIT_LENGTH) * slab(mat, 2, i) * filled
            at_first = iota((8, 8, LANES), 1) == 0
            for r in range(3):
                s = slab(cur, r, i)
                force = slab(part, r, i) + (slab(piola, r, above) - slab(piola, r, below)) * scale
                z_below = pltpu.roll(pltpu.roll(s, 1, 1), 1, 2)
                z_above = pltpu.roll(pltpu.roll(s, 7, 1), LANES - 1, 2)
                force = force + k_weight * (jnp.where(at_first, z_below, z_above) - s)
                put_slab(cur, r, i, s + gain * force)
            return carry

        for step in range(STEPS):
            with phase("m_dilate"):
                lax.fori_loop(0, 8, dilate, 0)
            if step > 0:
                wait_all(dil_send, dil_send_sem.at[step - 1])
            with phase("m_take"):
                taken = lax.dot_general(
                    perm[...],
                    dil_rows[...].astype(BF16),
                    (((1,), (1,)), ((), ())),
                    preferred_element_type=F32,
                )
                dil_send[...] = taken.reshape(n_blk, CAP, NODES).astype(BF16)

            def send_dilation(it, carry):
                c = lax.rem(blk + 11 * grp + it, n_blk)
                send(
                    dil_send.at[c],
                    dil_in.at[step, mine],
                    dil_send_sem.at[step],
                    dil_sem.at[step],
                    n_mech,
                    c,
                )
                return carry

            with phase("m_send_dil"):
                lax.fori_loop(0, n_blk, send_dilation, 0)
            if step == 0:

                @pl.when(has_above)
                def _():
                    send(
                        fill_send,
                        fill_in.at[0],
                        fill_send_sem.at[1],
                        fill_sem.at[0],
                        grp,
                        blk + 1,
                    )

                @pl.when(has_below)
                def _():
                    send(
                        fill_send,
                        fill_in.at[1],
                        fill_send_sem.at[0],
                        fill_sem.at[1],
                        grp,
                        blk - 1,
                    )

            for r in range(3):

                @pl.when(has_above)
                def _():
                    send(
                        cur.at[pl.ds(r * 512 + 448, 64)],
                        face_in.at[step, 0, pl.ds(r * 64, 64)],
                        face_send_sem.at[step, 1],
                        face_sem.at[step, 0],
                        grp,
                        blk + 1,
                    )

                @pl.when(has_below)
                def _():
                    send(
                        cur.at[pl.ds(r * 512, 64)],
                        face_in.at[step, 1, pl.ds(r * 64, 64)],
                        face_send_sem.at[step, 0],
                        face_sem.at[step, 1],
                        grp,
                        blk - 1,
                    )
            if step == 0:
                loads[1].wait()
            with phase("m_elastic"):
                lax.fori_loop(0, 8, elastic, 0)
            with phase("m_wait_press"):
                wait_all(press_in.at[step], press_sem.at[step])
            with phase("m_press"):
                arrived = press_in[step].astype(F32).reshape(slots, NODES).astype(BF16)
                press[...] = PRESSURE_SCALE * lax.dot_general(
                    arrived, perm[...], (((0,), (0,)), ((), ())), preferred_element_type=F32
                )
            with phase("m_swell"):
                lax.fori_loop(0, 8, swell, 0)
            for side, present in ((0, has_below), (1, has_above)):

                @pl.when(present)
                def _():
                    wait_all(face_in.at[step, side], face_sem.at[step, side])
                    wait_all(face_in.at[step, side], face_send_sem.at[step, side])
                    if step == 0:
                        wait_all(fill_send, fill_sem.at[side])
                        wait_all(fill_send, fill_send_sem.at[side])

                at = 7 * side
                weight = (PENALTY * UNIT_LENGTH) * fill_in[side]
                for r in range(3):
                    other = face_in[step, side, pl.ds(r * 64, 64), :].reshape(8, 8, LANES)
                    extra = weight * (other - slab(cur, r, at))
                    put_slab(part, r, at, slab(part, r, at) + extra)
            with phase("m_advance"):
                lax.fori_loop(0, 8, advance, 0)
        wait_all(oct_send, oct_send_sem)
        wait_all(dil_send, dil_send_sem.at[STEPS - 1])

    def brick():
        with phase("s_greet"):
            for g in range(n_mech):

                def greet_element(it, carry):
                    greet(g, lax.rem(blk + 11 * g + it, n_blk))
                    return carry

                lax.fori_loop(0, n_blk, greet_element, 0)
        row = iota((768, LANES), 0)
        at_octant = row // 8 == iota((768, LANES), 1)
        for k in range(8):
            select[:, k * LANES : (k + 1) * LANES] = flag(at_octant & (row % 8 == k), BF16)
        def split(value, lanes):
            count = value.shape[0]
            high = value.astype(BF16)
            rest = value - high.astype(F32)
            middle = rest.astype(BF16)
            low = (rest - middle.astype(F32)).astype(BF16)
            for at, piece in enumerate((high, middle, low)):
                pieces[at * count : (at + 1) * count, lanes] = piece

        def joined(product):
            count = product.shape[0] // 3
            return product[0:count] + product[count : 2 * count] + product[2 * count : 3 * count]

        def to_layers(source, target, first, scale):
            for zq in range(6):
                split(source[pl.ds(zq, 256, stride=6), :], slice(zq * LANES, zq * LANES + LANES))
            for pair in range(4):
                lanes = slice(pair * 256, pair * 256 + 256)
                both = joined(
                    jnp.dot(pieces[:, 0:768], select[:, lanes], preferred_element_type=F32)
                )
                for half in range(2):
                    value = scale * both[:, half * LANES : (half + 1) * LANES]
                    for x in range(16):
                        at = ((first + x) * 8 + 2 * pair + half) * 16
                        target[at : at + 16, :] = value[x * 16 : x * 16 + 16]

        def from_layers(source, first, spans):
            count = 16 * sum(last - start for start, last in spans)
            for k in range(8):
                rows = [
                    source[at : at + 16, :]
                    for start, last in spans
                    for at in [((first + x) * 8 + k) * 16 for x in range(start, last)]
                ]
                split(jnp.concatenate(rows, axis=0), slice(k * LANES, (k + 1) * LANES))
            for pair in range(3):
                both = joined(
                    lax.dot_general(
                        pieces[0 : 3 * count, :],
                        select[pair * 256 : pair * 256 + 256, :],
                        (((1,), (1,)), ((), ())),
                        preferred_element_type=F32,
                    )
                )
                for half in range(2):
                    taken = 0
                    for start, last in spans:
                        more = 16 * (last - start)
                        cur[pl.ds(start * 96 + 2 * pair + half, more, stride=6), :] = both[
                            taken : taken + more, half * LANES : (half + 1) * LANES
                        ]
                        taken += more

        def half_weight(v):
            return 0.25 + 0.5 * v * v

        plane = (1, 16, LANES)
        not_first = flag(iota(plane, 1) > 0)
        not_last = flag(iota(plane, 1) < 15)
        at_start = iota(plane, 2) == 0
        at_end = iota(plane, 2) >= DEPTH_OCTANTS - 1

        def sweep(source, source_first, target, target_first, diff_first, start, last):
            source_first, target_first = source_first + start, target_first + start
            diff_first = diff_first + start

            def rows_from(row):
                return source[pl.ds(row, LAYER), :].reshape(8, 16, LANES)

            def one_layer(x, carry):
                row = pl.multiple_of((source_first + x) * LAYER, LAYER)
                centre = rows_from(row)
                x_below = rows_from(pl.multiple_of(row - LAYER, LAYER))
                x_above = rows_from(pl.multiple_of(row + LAYER, LAYER))
                y_below, y_above = rows_from(row - 1), rows_from(row + 1)
                weight = half_weight(centre)

                def flux(there):
                    return (weight + half_weight(there)) * (there - centre)

                inflow = flux(x_above) + flux(x_below)
                inflow = inflow + not_last * flux(y_above) + not_first * flux(y_below)
                after = jnp.where(at_end, centre[7:8], pltpu.roll(centre[0:1], LANES - 1, 2))
                before = jnp.where(at_start, centre[0:1], pltpu.roll(centre[7:8], 1, 2))
                inner = (weight[1:] + weight[:-1]) * (centre[1:] - centre[:-1])
                leave = (weight[7:8] + half_weight(after)) * (after - centre[7:8])
                enter = (weight[0:1] + half_weight(before)) * (before - centre[0:1])
                inflow = inflow + (
                    jnp.concatenate([inner, leave], axis=0)
                    + jnp.concatenate([enter, -inner], axis=0)
                )
                gain = rows_of(diff, (diff_first + x) * LAYER, LAYER).reshape(8, 16, LANES)
                updated = centre + gain * inflow
                at = pl.multiple_of((target_first + x) * LAYER, LAYER)
                target[pl.ds(at, LAYER), :] = updated.reshape(LAYER, LANES)
                return carry

            lax.fori_loop(0, last - start, one_layer, 0)

        with phase("s_load"):
            loads[0].wait()
        with phase("s_to_layers"):
            to_layers(cur, phi_a.at[0], 2, 1.0)

        def make_pressure(step):
            phi = phi_a.at[step]

            def one_k(k, carry):
                for t in range(4):
                    x, y = 8 * (t // 2), 8 * (t % 2)
                    value = jnp.concatenate(
                        [rows_of(phi, ((2 + x + i) * 8 + k) * 16 + y, 8) for i in range(8)], axis=0
                    )
                    value = value + CUBIC_TERM * value * value * value
                    at = pl.multiple_of(k * 64, 64)
                    pi_rows[pl.ds(at, 64), t * LANES : (t + 1) * LANES] = value.astype(BF16)
                return carry

            lax.fori_loop(0, 8, one_k, 0)

        def send_pressure(step):
            for g in range(n_mech):
                rows = slice(g * n_blk * CAP, (g + 1) * n_blk * CAP)
                taken = lax.dot_general(
                    hits[rows, :],
                    pi_rows[...],
                    (((1,), (1,)), ((), ())),
                    preferred_element_type=F32,
                )
                press_send[step, g * n_blk : (g + 1) * n_blk] = taken.reshape(
                    n_blk, CAP, NODES
                ).astype(BF16)

                def send_one(it, carry):
                    c = lax.rem(blk + 11 * g + it, n_blk)
                    send(
                        press_send.at[step, g * n_blk + c],
                        press_in.at[step, blk],
                        press_send_sem.at[step],
                        press_sem.at[step],
                        g,
                        c,
                    )
                    return carry

                lax.fori_loop(0, n_blk, send_one, 0)

        with phase("s_pi"):
            make_pressure(0)
        with phase("s_barrier"):
            pl.semaphore_wait(barrier, beside)
        with phase("s_wait_oct"):
            wait_all(oct_in, oct_sem)
        with phase("s_hits"):
            spread = (n_mech * n_blk, CAP, LANES)
            one_code = jnp.where(
                iota(spread, 1) == iota(spread, 2), jnp.broadcast_to(oct_in[...], spread), 0.0
            )
            wanted = jnp.dot(
                one_code.reshape(n_mech * n_blk * CAP, LANES).astype(BF16),
                jnp.ones((LANES, LANES), BF16),
                preferred_element_type=F32,
            )
            lane = iota(wanted.shape, 1)
            for t in range(4):
                at_octant = (lane + t * DEPTH_OCTANTS).astype(F32) - CODE_SHIFT
                mine = (wanted == at_octant) & (lane < DEPTH_OCTANTS)
                hits[:, t * LANES : (t + 1) * LANES] = flag(mine, BF16)
        with phase("s_send_press"):
            send_pressure(0)
        loads[1].wait()
        with phase("s_to_layers_d"):
            to_layers(mat, diff, 1, SWEEP_STEP)

        @pl.when(has_above)
        def _():
            send(
                diff.at[pl.ds(16 * LAYER, LAYER)],
                diff.at[pl.ds(0, LAYER)],
                rim_send_sem.at[1],
                rim_sem.at[0],
                grp,
                blk + 1,
            )

        @pl.when(has_below)
        def _():
            send(
                diff.at[pl.ds(LAYER, LAYER)],
                diff.at[pl.ds(17 * LAYER, LAYER)],
                rim_send_sem.at[0],
                rim_sem.at[1],
                grp,
                blk - 1,
            )

        @pl.when(jnp.logical_not(has_below))
        def _():
            diff[0:LAYER, :] = jnp.zeros((LAYER, LANES), F32)
            for step in range(STEPS):
                phi_a[step, 0 : 2 * LAYER, :] = jnp.zeros((2 * LAYER, LANES), F32)

        @pl.when(jnp.logical_not(has_above))
        def _():
            diff[17 * LAYER : 18 * LAYER, :] = jnp.zeros((LAYER, LANES), F32)
            for step in range(STEPS):
                phi_a[step, 18 * LAYER : 20 * LAYER, :] = jnp.zeros((2 * LAYER, LANES), F32)

        for step in range(STEPS):
            phi = phi_a.at[step]
            if step > 0:
                with phase("s_pi"):
                    make_pressure(step)
                with phase("s_send_press"):
                    send_pressure(step)
            with phase("s_wait_dil"):
                wait_all(dil_in.at[step], dil_sem.at[step])
            with phase("s_deposit"):
                arrived = dil_in[step].astype(F32).reshape(n_mech * n_blk * CAP, NODES).astype(BF16)
                total[...] = lax.dot_general(
                    arrived, hits[...], (((0,), (0,)), ((), ())), preferred_element_type=F32
                )

                def one_k(k, carry):
                    for t in range(4):
                        for i in range(8):
                            x, y = 8 * (t // 2) + i, 8 * (t % 2)
                            at = pl.multiple_of(((2 + x) * 8 + k) * 16 + y, 8)
                            more = total[
                                pl.ds(pl.multiple_of(k * 64 + i * 8, 8), 8),
                                t * LANES : (t + 1) * LANES,
                            ]
                            phi[pl.ds(at, 8), :] = (
                                phi[pl.ds(at, 8), :] + (SWEEP_STEP * SOURCE_RATE) * more
                            )
                    return carry

                lax.fori_loop(0, 8, one_k, 0)

            @pl.when(has_above)
            def _():
                send(
                    phi.at[pl.ds(16 * LAYER, 2 * LAYER)],
                    phi.at[pl.ds(0, 2 * LAYER)],
                    halo_send_sem.at[step, 1],
                    halo_sem.at[step, 0],
                    grp,
                    blk + 1,
                )

            @pl.when(has_below)
            def _():
                send(
                    phi.at[pl.ds(2 * LAYER, 2 * LAYER)],
                    phi.at[pl.ds(18 * LAYER, 2 * LAYER)],
                    halo_send_sem.at[step, 0],
                    halo_sem.at[step, 1],
                    grp,
                    blk - 1,
                )

            after = phi_a.at[(step + 1) % 2]
            with phase("s_sweep_inner"):
                sweep(phi, 2, phi_b, 1, 1, 1, 15)
                sweep(phi_b, 1, after, 2, 1, 2, 14)
            if step == STEPS - 1:
                with phase("s_from_inner"):
                    from_layers(after, 2, [(2, 14)])
            with phase("s_wait_halo"):
                for side, present, first in ((0, has_below, 0), (1, has_above, 18)):

                    @pl.when(present)
                    def _():
                        two = phi.at[pl.ds(first * LAYER, 2 * LAYER)]
                        wait_all(two, halo_sem.at[step, side])
                        wait_all(two, halo_send_sem.at[step, side])
                        if step == 0:
                            one = diff.at[pl.ds(0, LAYER)]
                            wait_all(one, rim_sem.at[side])
                            wait_all(one, rim_send_sem.at[side])

            with phase("s_sweep_edge"):
                sweep(phi, 2, phi_b, 1, 1, -1, 1)
                sweep(phi, 2, phi_b, 1, 1, 15, 17)
                sweep(phi_b, 1, after, 2, 1, 0, 2)
                sweep(phi_b, 1, after, 2, 1, 14, 16)
            with phase("s_sent"):
                wait_all(press_send.at[step], press_send_sem.at[step])
        with phase("s_from_edge"):
            from_layers(phi_a.at[STEPS % 2], 2, [(0, 2), (14, 16)])

    @pl.when(solvent)
    def _():
        brick()

    @pl.when(jnp.logical_not(solvent))
    def _():
        mechanics()


def solution(mesh):
    n_grp, n_blk = mesh.shape["grp"], mesh.shape["blk"]
    n_mech = n_grp - 1
    slots = n_blk * CAP
    dma = pltpu.SemaphoreType.DMA
    vmem = pltpu.VMEM
    whole = (1536, LANES)
    call = pl.pallas_call(
        functools.partial(kernel, n_grp, n_blk),
        out_shape=jax.ShapeDtypeStruct(whole, F32),
        in_specs=[pl.BlockSpec(memory_space=pltpu.HBM)] * 5,
        out_specs=pl.BlockSpec(memory_space=vmem),
        scratch_shapes=[
            vmem(whole, F32),
            vmem((1, LANES), jnp.int32),
            vmem((1, LANES), jnp.int32),
            vmem((1, LANES), jnp.int32),
            vmem((slots, LANES), BF16),
            vmem((n_blk, 1, LANES), F32),
            vmem((n_blk, CAP, NODES), BF16),
            vmem((NODES, LANES), F32),
            vmem((STEPS, n_blk, CAP, NODES), BF16),
            vmem((NODES, LANES), F32),
            vmem((STEPS, 2, 192, LANES), F32),
            vmem((2, 8, LANES), F32),
            vmem((8, LANES), F32),
            vmem(whole, F32),
            vmem(whole, F32),
            vmem((9 * NODES, LANES), F32),
            vmem((n_mech * n_blk, 1, LANES), F32),
            vmem((STEPS, n_mech * n_blk, CAP, NODES), BF16),
            vmem((STEPS, n_mech * n_blk, CAP, NODES), BF16),
            vmem((n_mech * n_blk * CAP, NODES), BF16),
            vmem((768, 1024), BF16),
            vmem((768, 1024), BF16),
            vmem((2, 20 * LAYER, LANES), F32),
            vmem((18 * LAYER, LANES), F32),
            vmem((18 * LAYER, LANES), F32),
            vmem((NODES, NODES), BF16),
            vmem((NODES, NODES), F32),
            dma((2,)),
            dma((3,)),
            dma,
            dma,
            dma((STEPS,)),
            dma((STEPS,)),
            dma((STEPS,)),
            dma((STEPS,)),
            dma((STEPS, 2)),
            dma((STEPS, 2)),
            dma((2,)),
            dma((2,)),
            dma((STEPS, 2)),
            dma((STEPS, 2)),
            dma((2,)),
            dma((2,)),
        ],
        compiler_params=pltpu.CompilerParams(
            collective_id=0, has_side_effects=True, vmem_limit_bytes=55 * 1000000
        ),
    )

    def shards(state, material, occupied, brick_column, brick_octant):
        out = call(
            state.reshape(whole),
            material.reshape(whole),
            occupied.reshape(1, LANES),
            brick_column.reshape(1, LANES),
            brick_octant.reshape(1, LANES),
        )
        return out.reshape(state.shape)

    in_specs = (
        P("grp", None, None, "blk"),
        P("grp", None, None, "blk"),
        P(("grp", "blk")),
        P(("grp", "blk"), None),
        P(("grp", "blk")),
    )
    out_specs = P("grp", None, None, "blk")
    return jax.shard_map(shards, mesh=mesh, in_specs=in_specs, out_specs=out_specs, check_vma=False)
```

```python
import contextlib
import functools

import jax
import jax.numpy as jnp
from jax import lax
from jax.experimental import pallas as pl
from jax.experimental.pallas import tpu as pltpu
from jax.sharding import PartitionSpec as P

STEPS = 2
UNIT_LENGTH = 0.02
TIME_STEP = 0.1
PENALTY = 1.0
PRESSURE_SCALE = 0.05
DILATION_SCALE = 50.0
SWEEP_STEP = 0.03
SOURCE_RATE = 2.0
CUBIC_TERM = 0.3

MESH = pl.DeviceIdType.MESH
F32 = jnp.float32
BF16 = jnp.bfloat16
LANES = 128
NODES = 512
CAP = 8
DEPTH_OCTANTS = 96
CODE_SHIFT = 191.0
EMPTY_CODE = -1000.0
PRESSURE_SPANS = (((0, 4), (4, 8)), ((0, 8),))
LAYER = 128


def far_first(across):
    ring = (2, 1, 3, 0)
    along_y = (2, 1) if across else (0, 1)
    shifts = [(z, x, y) for z in ring for x in ring for y in range(2)]
    return sorted(shifts, key=lambda s: -(min(s[0], 4 - s[0]) + min(s[1], 4 - s[1]) + along_y[s[2]]))


def phase(name):
    return contextlib.nullcontext()


def iota(shape, dim):
    return lax.broadcasted_iota(jnp.int32, shape, dim)


def flag(mask, dtype=F32):
    return jnp.where(mask, 1.0, 0.0).astype(dtype)


def wait_all(ref, sem):
    pltpu.make_async_copy(ref, ref, sem).wait()


def rows_of(ref, start, count):
    return ref[pl.ds(pl.multiple_of(start, count), count), :]


def slab(ref, r, i):
    return rows_of(ref, r * 512 + i * 64, 64).reshape(8, 8, LANES)


def put_slab(ref, r, i, value):
    ref[pl.ds(pl.multiple_of(r * 512 + i * 64, 64), 64), :] = value.reshape(64, LANES)


def along_j(s):
    return jnp.concatenate([s[1:2] - s[0:1], 0.5 * (s[2:] - s[:-2]), s[7:8] - s[6:7]], axis=0)


def along_k(s):
    k = iota(s.shape, 1)
    edge = (k == 0) | (k == 7)
    upper = jnp.where(k == 7, s, pltpu.roll(s, 7, 1))
    lower = jnp.where(k == 0, s, pltpu.roll(s, 1, 1))
    return (upper - lower) * jnp.where(edge, 1.0, 0.5)


def i_span(i):
    below, above = jnp.maximum(i - 1, 0), jnp.minimum(i + 1, 7)
    return below, above, jnp.where((i == 0) | (i == 7), 1.0, 0.5)


def gradients(cur, i):
    below, above, scale = i_span(i)
    grads = []
    for r in range(3):
        s = slab(cur, r, i)
        row = [
            (slab(cur, r, above) - slab(cur, r, below)) * (UNIT_LENGTH * scale),
            along_j(s) * UNIT_LENGTH,
            along_k(s) * UNIT_LENGTH,
        ]
        row[r] = row[r] + 1.0
        grads.append(row)
    return grads


def cofactors(f):
    return [
        [
            f[1][1] * f[2][2] - f[1][2] * f[2][1],
            f[1][2] * f[2][0] - f[1][0] * f[2][2],
            f[1][0] * f[2][1] - f[1][1] * f[2][0],
        ],
        [
            f[0][2] * f[2][1] - f[0][1] * f[2][2],
            f[0][0] * f[2][2] - f[0][2] * f[2][0],
            f[0][1] * f[2][0] - f[0][0] * f[2][1],
        ],
        [
            f[0][1] * f[1][2] - f[0][2] * f[1][1],
            f[0][2] * f[1][0] - f[0][0] * f[1][2],
            f[0][0] * f[1][1] - f[0][1] * f[1][0],
        ],
    ]


def kernel(
    n_grp,
    n_blk,
    state_ref,
    material_ref,
    occupied_ref,
    column_ref,
    octant_ref,
    cur,
    mat,
    occupied_in,
    column_in,
    octant_in,
    perm,
    oct_send,
    dil_send,
    dil_rows,
    press_in,
    press,
    face_in,
    fill_in,
    fill_send,
    piola,
    part,
    cofactor,
    oct_in,
    dil_in,
    press_send,
    hits,
    select,
    pieces,
    phi_a,
    phi_b,
    diff,
    pi_rows,
    total,
    load_sem,
    small_sem,
    oct_send_sem,
    oct_sem,
    dil_send_sem,
    dil_sem,
    press_send_sem,
    press_sem,
    face_send_sem,
    face_sem,
    fill_send_sem,
    fill_sem,
    halo_send_sem,
    halo_sem,
    rim_send_sem,
    rim_sem,
):
    grp, blk = lax.axis_index("grp"), lax.axis_index("blk")
    n_mech = n_grp - 1
    solvent = grp == n_mech
    barrier = pltpu.get_barrier_semaphore()
    has_below, has_above = blk > 0, blk < n_blk - 1
    loads = [
        pltpu.make_async_copy(state_ref, cur, load_sem.at[0]),
        pltpu.make_async_copy(material_ref, mat, load_sem.at[1]),
    ]
    for copy in loads:
        copy.start()

    def greet(g, c):
        pl.semaphore_signal(barrier, inc=1, device_id=(g, c), device_id_type=MESH)

    @pl.when(has_below)
    def _():
        greet(grp, blk - 1)

    @pl.when(has_above)
    def _():
        greet(grp, blk + 1)

    def column_at(shift):
        z, x, y = blk // 8 + shift[0], blk // 2 + shift[1], blk + shift[2]
        return lax.rem(z, 4) * 8 + lax.rem(x, 4) * 2 + lax.rem(y, 2)

    columns = {shift: column_at(shift) for shift in far_first(True)}
    beside = jnp.where(has_below, 1, 0) + jnp.where(has_above, 1, 0)

    def send(src, dst, send_sem, recv_sem, g, c):
        copy = pltpu.make_async_remote_copy(
            src_ref=src,
            dst_ref=dst,
            send_sem=send_sem,
            recv_sem=recv_sem,
            device_id=(g, c),
            device_id_type=MESH,
        )
        copy.start()

    def mechanics():
        small = [
            pltpu.make_async_copy(source, target, small_sem.at[at])
            for at, (source, target) in enumerate(
                (
                    (occupied_ref, occupied_in),
                    (column_ref, column_in),
                    (octant_ref, octant_in),
                )
            )
        ]
        for copy in small:
            copy.start()
        with phase("m_small"):
            for copy in small:
                copy.wait()
        filled = occupied_in[...].astype(F32)
        column = column_in[...].astype(F32)
        octant = octant_in[...].astype(F32)
        square = (LANES, LANES)
        across = jnp.broadcast_to(column, square)
        diagonal = iota(square, 0) == iota(square, 1)
        down = jnp.sum(jnp.where(diagonal, across, 0.0), axis=1, keepdims=True)
        same = down == across
        rank = jnp.sum(flag(same & (iota(square, 0) < iota(square, 1))), axis=0, keepdims=True)
        rank_down = jnp.sum(
            flag(same & (iota(square, 1) < iota(square, 0))), axis=1, keepdims=True
        )
        slot = column * CAP + rank
        slots = n_blk * CAP
        hit = iota((slots, LANES), 0).astype(F32) == slot
        perm[...] = flag(hit, BF16)
        at_column = iota((n_blk, LANES), 0).astype(F32) == column
        coded = jnp.concatenate(
            [jnp.where(at_column, octant - CODE_SHIFT, 0.0), flag(at_column)], axis=0
        ).astype(BF16)
        at_rank = flag(iota(square, 1).astype(F32) == rank_down, BF16)
        placed = jnp.dot(coded, at_rank, preferred_element_type=F32)
        code = placed[0:n_blk] + EMPTY_CODE * (1.0 - placed[n_blk : 2 * n_blk])
        for c in range(n_blk):
            oct_send[c] = code[c : c + 1, :]
        fill_send[...] = jnp.broadcast_to(filled, (8, LANES))
        k = iota((8, LANES), 0)
        e = iota((8, LANES), 1)
        filled_8 = jnp.broadcast_to(filled, (8, LANES))
        fill_below = jnp.where(e == 0, 0.0, pltpu.roll(filled_8, 1, 1))
        fill_above = jnp.where(e == LANES - 1, 0.0, pltpu.roll(filled_8, LANES - 1, 1))
        k_weight = (PENALTY * UNIT_LENGTH) * jnp.where(
            k == 0, fill_below, jnp.where(k == 7, fill_above, 0.0)
        )

        @pl.when(jnp.logical_not(has_below))
        def _():
            fill_in[0] = jnp.zeros((8, LANES), F32)
            for step in range(STEPS):
                face_in[step, 0] = jnp.zeros((192, LANES), F32)

        @pl.when(jnp.logical_not(has_above))
        def _():
            fill_in[1] = jnp.zeros((8, LANES), F32)
            for step in range(STEPS):
                face_in[step, 1] = jnp.zeros((192, LANES), F32)

        def dilate(i, carry):
            f = gradients(cur, i)
            det = (
                f[0][0] * (f[1][1] * f[2][2] - f[1][2] * f[2][1])
                - f[0][1] * (f[1][0] * f[2][2] - f[1][2] * f[2][0])
                + f[0][2] * (f[1][0] * f[2][1] - f[1][1] * f[2][0])
            )
            change = (det - 1.0) * filled * DILATION_SCALE
            for j in range(8):
                dil_rows[pl.ds(i * 64 + j, 8, stride=8), :] = change[j]
            return carry

        def elastic(i, carry):
            f = gradients(cur, i)
            shear, lame = slab(mat, 0, i), slab(mat, 1, i)
            c = [[None] * 3 for _ in range(3)]
            for a in range(3):
                for b in range(a, 3):
                    c[a][b] = f[0][a] * f[0][b] + f[1][a] * f[1][b] + f[2][a] * f[2][b]
                c[a][a] = c[a][a] - 1.0
            trace = (0.5 * lame) * (c[0][0] + c[1][1] + c[2][2])
            s = [[None] * 3 for _ in range(3)]
            for a in range(3):
                for b in range(a, 3):
                    s[a][b] = s[b][a] = shear * c[a][b]
            for a in range(3):
                s[a][a] = s[a][a] + trace
            for r in range(3):
                p = [f[r][0] * s[0][j] + f[r][1] * s[1][j] + f[r][2] * s[2][j] for j in range(3)]
                put_slab(piola, r, i, p[0])
                own = slab(cur, r, i)
                z_below = pltpu.roll(pltpu.roll(own, 1, 1), 1, 2)
                z_above = pltpu.roll(pltpu.roll(own, 7, 1), LANES - 1, 2)
                pull = k_weight * (jnp.where(iota(own.shape, 1) == 0, z_below, z_above) - own)
                put_slab(part, r, i, along_j(p[1]) + along_k(p[2]) + pull)
            cof = cofactors(f)
            for r in range(3):
                for j in range(3):
                    put_slab(cofactor, 3 * r + j, i, cof[r][j])
            return carry

        def swell(i, carry):
            pressure = jnp.concatenate(
                [press[pl.ds(i * 64 + j, 8, stride=8), :][None] for j in range(8)], axis=0
            )
            for r in range(3):
                p = [pressure * slab(cofactor, 3 * r + j, i) for j in range(3)]
                put_slab(piola, r, i, slab(piola, r, i) - p[0])
                put_slab(part, r, i, slab(part, r, i) - (along_j(p[1]) + along_k(p[2])))
            return carry

        def advance(i, carry):
            below, above, scale = i_span(i)
            gain = (TIME_STEP / UNIT_LENGTH) * slab(mat, 2, i) * filled
            for r in range(3):
                s = slab(cur, r, i)
                force = slab(part, r, i) + (slab(piola, r, above) - slab(piola, r, below)) * scale
                put_slab(cur, r, i, s + gain * force)
            return carry

        def take(first, last):
            lanes = slice(first * 64, last * 64)
            lax.fori_loop(first, last, dilate, 0)
            taken = lax.dot_general(
                perm[...],
                dil_rows[lanes, :].astype(BF16),
                (((1,), (1,)), ((), ())),
                preferred_element_type=F32,
            )
            dil_send[:, :, lanes] = taken.reshape(n_blk, CAP, (last - first) * 64).astype(BF16)

        def send_taken(step, first, last):
            lanes = pl.ds(first * 64, (last - first) * 64)

            for shift in far_first(True):
                c = columns[shift]
                send(
                    dil_send.at[c, :, lanes],
                    dil_in.at[step, mine, :, lanes],
                    dil_send_sem.at[step],
                    dil_sem.at[step, grp],
                    n_mech,
                    c,
                )

        def send_faces(step):
            for r in range(3):

                @pl.when(has_above)
                def _():
                    send(
                        cur.at[pl.ds(r * 512 + 448, 64)],
                        face_in.at[step, 0, pl.ds(r * 64, 64)],
                        face_send_sem.at[step, 1],
                        face_sem.at[step, 0],
                        grp,
                        blk + 1,
                    )

                @pl.when(has_below)
                def _():
                    send(
                        cur.at[pl.ds(r * 512, 64)],
                        face_in.at[step, 1, pl.ds(r * 64, 64)],
                        face_send_sem.at[step, 0],
                        face_sem.at[step, 1],
                        grp,
                        blk - 1,
                    )

        with phase("m_load"):
            loads[0].wait()
        with phase("m_take"):
            take(0, 8)

        with phase("m_barrier"):
            pl.semaphore_wait(barrier, n_blk + beside)

        mine = grp * n_blk + blk

        with phase("m_send_oct"):
            for shift in far_first(True):
                c = columns[shift]
                send(oct_send.at[c], oct_in.at[mine], oct_send_sem, oct_sem, n_mech, c)

        loads[1].wait()
        for step in range(STEPS):
            with phase("m_elastic"):
                lax.fori_loop(0, 8, elastic, 0)
            if step == 0:
                with phase("m_send_dil"):
                    send_taken(0, 0, 8)

                @pl.when(has_above)
                def _():
                    send(fill_send, fill_in.at[0], fill_send_sem.at[1], fill_sem.at[0], grp, blk + 1)

                @pl.when(has_below)
                def _():
                    send(fill_send, fill_in.at[1], fill_send_sem.at[0], fill_sem.at[1], grp, blk - 1)

                send_faces(0)
            with phase("m_faces"):
                for side, present in ((0, has_below), (1, has_above)):

                    @pl.when(present)
                    def _():
                        wait_all(face_in.at[step, side], face_sem.at[step, side])
                        wait_all(face_in.at[step, side], face_send_sem.at[step, side])
                        if step == 0:
                            wait_all(fill_send, fill_sem.at[side])
                            wait_all(fill_send, fill_send_sem.at[side])

                    at = 7 * side
                    weight = (PENALTY * UNIT_LENGTH) * fill_in[side]
                    for r in range(3):
                        other = face_in[step, side, pl.ds(r * 64, 64), :].reshape(8, 8, LANES)
                        extra = weight * (other - slab(cur, r, at))
                        put_slab(part, r, at, slab(part, r, at) + extra)
            for at, (first, last) in enumerate(PRESSURE_SPANS[step]):
                lanes = slice(first * 64, last * 64)
                with phase("m_wait_press"):
                    wait_all(
                        press_in.at[step, :, :, pl.ds(first * 64, (last - first) * 64)],
                        press_sem.at[step, at],
                    )
                with phase("m_press"):
                    arrived = press_in[step, :, :, lanes].astype(F32)
                    press[lanes, :] = PRESSURE_SCALE * lax.dot_general(
                        arrived.reshape(slots, (last - first) * 64).astype(BF16),
                        perm[...],
                        (((0,), (0,)), ((), ())),
                        preferred_element_type=F32,
                    )
                with phase("m_swell"):
                    lax.fori_loop(first, last, swell, 0)
                with phase("m_advance"):
                    lax.fori_loop(max(first - 1, 0), last - 1 if last < 8 else 8, advance, 0)
                if step + 1 < STEPS:
                    if at == 0:
                        wait_all(dil_send, dil_send_sem.at[step])
                    ready = (max(first - 2, 0), last - 2 if last < 8 else 8)
                    with phase("m_take"):
                        take(*ready)
                    with phase("m_send_dil"):
                        send_taken(step + 1, *ready)
            if step + 1 < STEPS:
                send_faces(step + 1)
        wait_all(oct_send, oct_send_sem)
        wait_all(dil_send, dil_send_sem.at[STEPS - 1])

    def brick():
        with phase("s_greet"):
            for g in range(n_mech):

                for shift in far_first(g < 2):
                    greet(g, columns[shift])
        row = iota((768, LANES), 0)
        at_octant = row // 8 == iota((768, LANES), 1)
        for k in range(8):
            select[:, k * LANES : (k + 1) * LANES] = flag(at_octant & (row % 8 == k), BF16)
        def split(value, lanes, parts):
            count = value.shape[0]
            high = value.astype(BF16)
            rest = value - high.astype(F32)
            middle = rest.astype(BF16)
            low = (rest - middle.astype(F32)).astype(BF16)
            for at, piece in enumerate((high, middle, low)[0:parts]):
                pieces[at * count : (at + 1) * count, lanes] = piece

        def joined(product, parts):
            count = product.shape[0] // parts
            return sum(product[at * count : (at + 1) * count] for at in range(parts))

        def to_layers(source, target, first, scale):
            for zq in range(6):
                split(source[pl.ds(zq, 256, stride=6), :], slice(zq * LANES, zq * LANES + LANES), 3)
            for pair in range(4):
                lanes = slice(pair * 256, pair * 256 + 256)
                both = joined(
                    jnp.dot(pieces[:, 0:768], select[:, lanes], preferred_element_type=F32), 3
                )
                for half in range(2):
                    value = scale * both[:, half * LANES : (half + 1) * LANES]
                    for x in range(16):
                        at = ((first + x) * 8 + 2 * pair + half) * 16
                        target[at : at + 16, :] = value[x * 16 : x * 16 + 16]

        def from_layers(source, first, spans):
            count = 16 * sum(last - start for start, last in spans)
            for k in range(8):
                rows = [
                    source[at : at + 16, :]
                    for start, last in spans
                    for at in [((first + x) * 8 + k) * 16 for x in range(start, last)]
                ]
                split(jnp.concatenate(rows, axis=0), slice(k * LANES, (k + 1) * LANES), 2)
            for pair in range(3):
                both = joined(
                    lax.dot_general(
                        pieces[0 : 2 * count, :],
                        select[pair * 256 : pair * 256 + 256, :],
                        (((1,), (1,)), ((), ())),
                        preferred_element_type=F32,
                    ),
                    2,
                )
                for half in range(2):
                    taken = 0
                    for start, last in spans:
                        more = 16 * (last - start)
                        cur[pl.ds(start * 96 + 2 * pair + half, more, stride=6), :] = both[
                            taken : taken + more, half * LANES : (half + 1) * LANES
                        ]
                        taken += more

        plane = (1, 16, LANES)
        not_first = flag(iota(plane, 1) > 0)
        not_last = flag(iota(plane, 1) < 15)
        at_start = iota(plane, 2) == 0
        at_end = iota(plane, 2) >= DEPTH_OCTANTS - 1

        def sweep(source, source_first, target, target_first, diff_first, start, last):
            source_first, target_first = source_first + start, target_first + start
            diff_first = diff_first + start

            def rows_from(row):
                return source[pl.ds(row, LAYER), :].reshape(8, 16, LANES)

            below = rows_from((source_first - 1) * LAYER)
            first = rows_from(source_first * LAYER)
            entering = (below * below + (first * first + 1.0)) * (first - below)

            def one_layer(x, carry):
                centre, entering = carry
                row = pl.multiple_of((source_first + x) * LAYER, LAYER)
                x_above = rows_from(pl.multiple_of(row + LAYER, LAYER))
                y_below, y_above = rows_from(row - 1), rows_from(row + 1)
                square = centre * centre
                weight = square + 1.0

                def flux(there):
                    return (weight + there * there) * (there - centre)

                leaving = flux(x_above)
                inflow = leaving - entering
                inflow = inflow + not_last * flux(y_above) + not_first * flux(y_below)
                after = jnp.where(at_end, centre[7:8], pltpu.roll(centre[0:1], LANES - 1, 2))
                before = jnp.where(at_start, centre[0:1], pltpu.roll(centre[7:8], 1, 2))
                inner = (weight[1:] + square[:-1]) * (centre[1:] - centre[:-1])
                leave = (weight[7:8] + after * after) * (after - centre[7:8])
                enter = (weight[0:1] + before * before) * (before - centre[0:1])
                inflow = inflow + (
                    jnp.concatenate([inner, leave], axis=0)
                    - jnp.concatenate([-enter, inner], axis=0)
                )
                gain = rows_of(diff, (diff_first + x) * LAYER, LAYER).reshape(8, 16, LANES)
                updated = centre + gain * inflow
                at = pl.multiple_of((target_first + x) * LAYER, LAYER)
                target[pl.ds(at, LAYER), :] = updated.reshape(LAYER, LANES)
                return x_above, leaving

            lax.fori_loop(0, last - start, one_layer, (first, entering))

        with phase("s_load"):
            loads[0].wait()
        with phase("s_to_layers"):
            to_layers(cur, phi_a.at[0], 2, 1.0)

        def make_pressure(step):
            phi = phi_a.at[step]

            def one_i(i, carry):
                for t in range(4):
                    x, y = 8 * (t // 2), 8 * (t % 2)
                    value = jnp.concatenate(
                        [rows_of(phi, ((2 + x + i) * 8 + k) * 16 + y, 8) for k in range(8)], axis=0
                    )
                    value = value + CUBIC_TERM * value * value * value
                    at = pl.multiple_of(i * 64, 64)
                    pi_rows[pl.ds(at, 64), t * LANES : (t + 1) * LANES] = value.astype(BF16)
                return carry

            lax.fori_loop(0, 8, one_i, 0)

        def send_pressure(step):
            for at, (first, last) in enumerate(PRESSURE_SPANS[step]):
                wide = slice(first * 64, last * 64)
                lanes = pl.ds(first * 64, (last - first) * 64)
                for g in range(n_mech):
                    taken = lax.dot_general(
                        hits[g * n_blk * CAP : (g + 1) * n_blk * CAP, :],
                        pi_rows[wide, :],
                        (((1,), (1,)), ((), ())),
                        preferred_element_type=F32,
                    )
                    press_send[step, g * n_blk : (g + 1) * n_blk, :, wide] = taken.reshape(
                        n_blk, CAP, (last - first) * 64
                    ).astype(BF16)

                    for shift in far_first(g < 2):
                        c = columns[shift]
                        send(
                            press_send.at[step, g * n_blk + c, :, lanes],
                            press_in.at[step, blk, :, lanes],
                            press_send_sem.at[step],
                            press_sem.at[step, at],
                            g,
                            c,
                        )

        with phase("s_pi"):
            make_pressure(0)
        loads[1].wait()
        with phase("s_to_layers_d"):
            to_layers(mat, diff, 1, 0.5 * SWEEP_STEP)
        with phase("s_barrier"):
            pl.semaphore_wait(barrier, beside)

        @pl.when(has_above)
        def _():
            send(
                diff.at[pl.ds(16 * LAYER, LAYER)],
                diff.at[pl.ds(0, LAYER)],
                rim_send_sem.at[1],
                rim_sem.at[0],
                grp,
                blk + 1,
            )

        @pl.when(has_below)
        def _():
            send(
                diff.at[pl.ds(LAYER, LAYER)],
                diff.at[pl.ds(17 * LAYER, LAYER)],
                rim_send_sem.at[0],
                rim_sem.at[1],
                grp,
                blk - 1,
            )

        with phase("s_wait_oct"):
            wait_all(oct_in, oct_sem)
        with phase("s_hits"):
            spread = (n_mech * n_blk, CAP, LANES)
            one_code = jnp.where(
                iota(spread, 1) == iota(spread, 2), jnp.broadcast_to(oct_in[...], spread), 0.0
            )
            wanted = jnp.dot(
                one_code.reshape(n_mech * n_blk * CAP, LANES).astype(BF16),
                jnp.ones((LANES, LANES), BF16),
                preferred_element_type=F32,
            )
            lane = iota(wanted.shape, 1)
            for t in range(4):
                at_octant = (lane + t * DEPTH_OCTANTS).astype(F32) - CODE_SHIFT
                mine = (wanted == at_octant) & (lane < DEPTH_OCTANTS)
                hits[:, t * LANES : (t + 1) * LANES] = flag(mine, BF16)
        with phase("s_send_press"):
            send_pressure(0)
        @pl.when(jnp.logical_not(has_below))
        def _():
            diff[0:LAYER, :] = jnp.zeros((LAYER, LANES), F32)
            for step in range(STEPS):
                phi_a[step, 0 : 2 * LAYER, :] = jnp.zeros((2 * LAYER, LANES), F32)

        @pl.when(jnp.logical_not(has_above))
        def _():
            diff[17 * LAYER : 18 * LAYER, :] = jnp.zeros((LAYER, LANES), F32)
            for step in range(STEPS):
                phi_a[step, 18 * LAYER : 20 * LAYER, :] = jnp.zeros((2 * LAYER, LANES), F32)

        for step in range(STEPS):
            phi = phi_a.at[step]
            if step > 0:
                with phase("s_pi"):
                    make_pressure(step)
                with phase("s_send_press"):
                    send_pressure(step)
            for g in (2, 0, 1):
                span = slice(g * n_blk, (g + 1) * n_blk)
                rows = slice(g * n_blk * CAP, (g + 1) * n_blk * CAP)
                with phase("s_wait_dil"):
                    wait_all(dil_in.at[step, span], dil_sem.at[step, g])
                arrived = dil_in[step, span].astype(F32)
                arrived = arrived.reshape(n_blk * CAP, NODES).astype(BF16)
                if g != 1:
                    with phase("s_collect"):
                        share = lax.dot_general(
                            arrived,
                            hits[rows, :],
                            (((0,), (0,)), ((), ())),
                            preferred_element_type=F32,
                        )
                        total[...] = share if g == 2 else total[...] + share

            def finish(ox, first, last):
                taken = slice(first * 64, last * 64)
                lanes = slice(ox * 256, ox * 256 + 256)
                total[taken, lanes] = total[taken, lanes] + lax.dot_general(
                    arrived[:, taken],
                    hits[rows, lanes],
                    (((0,), (0,)), ((), ())),
                    preferred_element_type=F32,
                )

                def one_i(i, carry):
                    for oy in range(2):
                        for k in range(8):
                            at = pl.multiple_of(((2 + 8 * ox + i) * 8 + k) * 16 + 8 * oy, 8)
                            octant = 2 * ox + oy
                            more = total[
                                pl.ds(pl.multiple_of(i * 64 + k * 8, 8), 8),
                                octant * LANES : (octant + 1) * LANES,
                            ]
                            phi[pl.ds(at, 8), :] = (
                                phi[pl.ds(at, 8), :] + (SWEEP_STEP * SOURCE_RATE) * more
                            )
                    return carry

                lax.fori_loop(first, last, one_i, 0)

            with phase("s_deposit_edge"):
                finish(0, 0, 2)
                finish(1, 6, 8)

            @pl.when(has_above)
            def _():
                send(
                    phi.at[pl.ds(16 * LAYER, 2 * LAYER)],
                    phi.at[pl.ds(0, 2 * LAYER)],
                    halo_send_sem.at[step, 1],
                    halo_sem.at[step, 0],
                    grp,
                    blk + 1,
                )

            @pl.when(has_below)
            def _():
                send(
                    phi.at[pl.ds(2 * LAYER, 2 * LAYER)],
                    phi.at[pl.ds(18 * LAYER, 2 * LAYER)],
                    halo_send_sem.at[step, 0],
                    halo_sem.at[step, 1],
                    grp,
                    blk - 1,
                )

            with phase("s_deposit"):
                finish(0, 2, 8)
                finish(1, 0, 6)
            after = phi_a.at[(step + 1) % 2]
            with phase("s_sweep_inner"):
                sweep(phi, 2, phi_b, 1, 1, 1, 15)
                sweep(phi_b, 1, after, 2, 1, 2, 14)
            if step == STEPS - 1:
                with phase("s_from_inner"):
                    from_layers(after, 2, [(2, 14)])
            with phase("s_wait_halo"):
                for side, present, first in ((0, has_below, 0), (1, has_above, 18)):

                    @pl.when(present)
                    def _():
                        two = phi.at[pl.ds(first * LAYER, 2 * LAYER)]
                        wait_all(two, halo_sem.at[step, side])
                        wait_all(two, halo_send_sem.at[step, side])
                        if step == 0:
                            one = diff.at[pl.ds(0, LAYER)]
                            wait_all(one, rim_sem.at[side])
                            wait_all(one, rim_send_sem.at[side])

            with phase("s_sweep_edge"):
                sweep(phi, 2, phi_b, 1, 1, -1, 1)
                sweep(phi, 2, phi_b, 1, 1, 15, 17)
                sweep(phi_b, 1, after, 2, 1, 0, 2)
                sweep(phi_b, 1, after, 2, 1, 14, 16)
            with phase("s_sent"):
                wait_all(press_send.at[step], press_send_sem.at[step])
        with phase("s_from_edge"):
            from_layers(phi_a.at[STEPS % 2], 2, [(0, 2), (14, 16)])

    @pl.when(solvent)
    def _():
        brick()

    @pl.when(jnp.logical_not(solvent))
    def _():
        mechanics()


def solution(mesh):
    n_grp, n_blk = mesh.shape["grp"], mesh.shape["blk"]
    n_mech = n_grp - 1
    slots = n_blk * CAP
    dma = pltpu.SemaphoreType.DMA
    vmem = pltpu.VMEM
    whole = (1536, LANES)
    call = pl.pallas_call(
        functools.partial(kernel, n_grp, n_blk),
        out_shape=jax.ShapeDtypeStruct(whole, F32),
        in_specs=[pl.BlockSpec(memory_space=pltpu.HBM)] * 5,
        out_specs=pl.BlockSpec(memory_space=vmem),
        scratch_shapes=[
            vmem(whole, F32),
            vmem((1, LANES), jnp.int32),
            vmem((1, LANES), jnp.int32),
            vmem((1, LANES), jnp.int32),
            vmem((slots, LANES), BF16),
            vmem((n_blk, 1, LANES), F32),
            vmem((n_blk, CAP, NODES), BF16),
            vmem((NODES, LANES), F32),
            vmem((STEPS, n_blk, CAP, NODES), BF16),
            vmem((NODES, LANES), F32),
            vmem((STEPS, 2, 192, LANES), F32),
            vmem((2, 8, LANES), F32),
            vmem((8, LANES), F32),
            vmem(whole, F32),
            vmem(whole, F32),
            vmem((9 * NODES, LANES), F32),
            vmem((n_mech * n_blk, 1, LANES), F32),
            vmem((STEPS, n_mech * n_blk, CAP, NODES), BF16),
            vmem((STEPS, n_mech * n_blk, CAP, NODES), BF16),
            vmem((n_mech * n_blk * CAP, NODES), BF16),
            vmem((768, 1024), BF16),
            vmem((768, 1024), BF16),
            vmem((2, 20 * LAYER, LANES), F32),
            vmem((18 * LAYER, LANES), F32),
            vmem((18 * LAYER, LANES), F32),
            vmem((NODES, NODES), BF16),
            vmem((NODES, NODES), F32),
            dma((2,)),
            dma((3,)),
            dma,
            dma,
            dma((STEPS,)),
            dma((STEPS, n_mech)),
            dma((STEPS,)),
            dma((STEPS, 2)),
            dma((STEPS, 2)),
            dma((STEPS, 2)),
            dma((2,)),
            dma((2,)),
            dma((STEPS, 2)),
            dma((STEPS, 2)),
            dma((2,)),
            dma((2,)),
        ],
        compiler_params=pltpu.CompilerParams(
            collective_id=0, has_side_effects=True, vmem_limit_bytes=55 * 1000000
        ),
    )

    def shards(state, material, occupied, brick_column, brick_octant):
        out = call(
            state.reshape(whole),
            material.reshape(whole),
            occupied.reshape(1, LANES),
            brick_column.reshape(1, LANES),
            brick_octant.reshape(1, LANES),
        )
        return out.reshape(state.shape)

    in_specs = (
        P("grp", None, None, "blk"),
        P("grp", None, None, "blk"),
        P(("grp", "blk")),
        P(("grp", "blk"), None),
        P(("grp", "blk")),
    )
    out_specs = P("grp", None, None, "blk")
    return jax.shard_map(shards, mesh=mesh, in_specs=in_specs, out_specs=out_specs, check_vma=False)
```

```python
import contextlib
import functools

import jax
import jax.numpy as jnp
from jax import lax
from jax.experimental import pallas as pl
from jax.experimental.pallas import tpu as pltpu
from jax.sharding import PartitionSpec as P

STEPS = 2
UNIT_LENGTH = 0.02
TIME_STEP = 0.1
PENALTY = 1.0
PRESSURE_SCALE = 0.05
DILATION_SCALE = 50.0
SWEEP_STEP = 0.03
SOURCE_RATE = 2.0
CUBIC_TERM = 0.3

MESH = pl.DeviceIdType.MESH
F32 = jnp.float32
BF16 = jnp.bfloat16
LANES = 128
NODES = 512
CAP = 8
HALO_PIECE = 64
DEPTH_OCTANTS = 96
CODE_SHIFT = 191.0
EMPTY_CODE = -1000.0
PRESSURE_SPANS = (((0, 4), (4, 6), (6, 8)), ((0, 8),))
LAYER = 128


def far_first(across):
    ring = (2, 1, 3, 0)
    along_y = (2, 1) if across else (0, 1)
    shifts = [(z, x, y) for z in ring for x in ring for y in range(2)]
    return sorted(shifts, key=lambda s: -(min(s[0], 4 - s[0]) + min(s[1], 4 - s[1]) + along_y[s[2]]))


def phase(name):
    return contextlib.nullcontext()


def iota(shape, dim):
    return lax.broadcasted_iota(jnp.int32, shape, dim)


def flag(mask, dtype=F32):
    return jnp.where(mask, 1.0, 0.0).astype(dtype)


def aligned(start, count):
    return start if isinstance(start, int) else pl.multiple_of(start, count)


def wait_all(ref, sem):
    pltpu.make_async_copy(ref, ref, sem).wait()


def rows_of(ref, start, count):
    return ref[pl.ds(aligned(start, count), count), :]


def slab(ref, r, i):
    return rows_of(ref, r * 512 + i * 64, 64).reshape(8, 8, LANES)


def put_slab(ref, r, i, value):
    ref[pl.ds(aligned(r * 512 + i * 64, 64), 64), :] = value.reshape(64, LANES)


def along_j(s):
    return jnp.concatenate([s[1:2] - s[0:1], 0.5 * (s[2:] - s[:-2]), s[7:8] - s[6:7]], axis=0)


def along_k(s):
    k = iota(s.shape, 1)
    edge = (k == 0) | (k == 7)
    upper = jnp.where(k == 7, s, pltpu.roll(s, 7, 1))
    lower = jnp.where(k == 0, s, pltpu.roll(s, 1, 1))
    return (upper - lower) * jnp.where(edge, 1.0, 0.5)


def i_span(i):
    if isinstance(i, int):
        return max(i - 1, 0), min(i + 1, 7), 1.0 if i in (0, 7) else 0.5
    below, above = jnp.maximum(i - 1, 0), jnp.minimum(i + 1, 7)
    return below, above, jnp.where((i == 0) | (i == 7), 1.0, 0.5)


def gradients(cur, i):
    below, above, scale = i_span(i)
    grads = []
    for r in range(3):
        s = slab(cur, r, i)
        row = [
            (slab(cur, r, above) - slab(cur, r, below)) * (UNIT_LENGTH * scale),
            along_j(s) * UNIT_LENGTH,
            along_k(s) * UNIT_LENGTH,
        ]
        row[r] = row[r] + 1.0
        grads.append(row)
    return grads


def cofactors(f):
    return [
        [
            f[1][1] * f[2][2] - f[1][2] * f[2][1],
            f[1][2] * f[2][0] - f[1][0] * f[2][2],
            f[1][0] * f[2][1] - f[1][1] * f[2][0],
        ],
        [
            f[0][2] * f[2][1] - f[0][1] * f[2][2],
            f[0][0] * f[2][2] - f[0][2] * f[2][0],
            f[0][1] * f[2][0] - f[0][0] * f[2][1],
        ],
        [
            f[0][1] * f[1][2] - f[0][2] * f[1][1],
            f[0][2] * f[1][0] - f[0][0] * f[1][2],
            f[0][0] * f[1][1] - f[0][1] * f[1][0],
        ],
    ]


def kernel(
    n_grp,
    n_blk,
    state_ref,
    material_ref,
    occupied_ref,
    column_ref,
    octant_ref,
    cur,
    mat,
    occupied_in,
    column_in,
    octant_in,
    perm,
    oct_send,
    dil_send,
    dil_rows,
    press_in,
    press,
    face_in,
    fill_in,
    fill_send,
    piola,
    part,
    cofactor,
    oct_in,
    dil_in,
    press_send,
    hits,
    select,
    pieces,
    phi_a,
    phi_b,
    diff,
    halo_send,
    halo_in,
    pick,
    packed,
    pi_rows,
    total,
    local_sem,
    send_sem,
    recv_sem,
):
    grp, blk = lax.axis_index("grp"), lax.axis_index("blk")
    sent, got = send_sem, recv_sem
    n_mech = n_grp - 1
    solvent = grp == n_mech
    barrier = pltpu.get_barrier_semaphore()
    has_below, has_above = blk > 0, blk < n_blk - 1
    loads = [
        pltpu.make_async_copy(state_ref, cur, local_sem.at[0]),
        pltpu.make_async_copy(material_ref, mat, local_sem.at[1]),
    ]
    for copy in loads:
        copy.start()

    def greet(g, c):
        pl.semaphore_signal(barrier, inc=1, device_id=(g, c), device_id_type=MESH)

    @pl.when(has_below)
    def _():
        greet(grp, blk - 1)

    @pl.when(has_above)
    def _():
        greet(grp, blk + 1)

    def column_at(shift):
        z, x, y = blk // 8 + shift[0], blk // 2 + shift[1], blk + shift[2]
        return lax.rem(z, 4) * 8 + lax.rem(x, 4) * 2 + lax.rem(y, 2)

    columns = {shift: column_at(shift) for shift in far_first(True)}
    beside = jnp.where(has_below, 1, 0) + jnp.where(has_above, 1, 0)

    def send(src, dst, send_sem, recv_sem, g, c):
        copy = pltpu.make_async_remote_copy(
            src_ref=src,
            dst_ref=dst,
            send_sem=send_sem,
            recv_sem=recv_sem,
            device_id=(g, c),
            device_id_type=MESH,
        )
        copy.start()

    def send_pieces(source, first, target, there, count, send_sem, recv_sem, g, c):
        for at in range(0, count, HALO_PIECE):
            send(
                source.at[pl.ds(first + at, HALO_PIECE)],
                target.at[pl.ds(there + at, HALO_PIECE)],
                send_sem,
                recv_sem,
                g,
                c,
            )

    def mechanics():
        small = [
            pltpu.make_async_copy(source, target, local_sem.at[2 + at])
            for at, (source, target) in enumerate(
                (
                    (occupied_ref, occupied_in),
                    (column_ref, column_in),
                    (octant_ref, octant_in),
                )
            )
        ]
        for copy in small:
            copy.start()
        with phase("m_small"):
            for copy in small:
                copy.wait()
        filled = occupied_in[...].astype(F32)
        column = column_in[...].astype(F32)
        octant = octant_in[...].astype(F32)
        square = (LANES, LANES)
        across = jnp.broadcast_to(column, square)
        diagonal = iota(square, 0) == iota(square, 1)
        down = jnp.sum(jnp.where(diagonal, across, 0.0), axis=1, keepdims=True)
        same = down == across
        rank = jnp.sum(flag(same & (iota(square, 0) < iota(square, 1))), axis=0, keepdims=True)
        rank_down = jnp.sum(
            flag(same & (iota(square, 1) < iota(square, 0))), axis=1, keepdims=True
        )
        slot = column * CAP + rank
        slots = n_blk * CAP
        hit = iota((slots, LANES), 0).astype(F32) == slot
        perm[...] = flag(hit, BF16)
        at_column = iota((n_blk, LANES), 0).astype(F32) == column
        coded = jnp.concatenate(
            [jnp.where(at_column, octant - CODE_SHIFT, 0.0), flag(at_column)], axis=0
        ).astype(BF16)
        at_rank = flag(iota(square, 1).astype(F32) == rank_down, BF16)
        placed = jnp.dot(coded, at_rank, preferred_element_type=F32)
        code = placed[0:n_blk] + EMPTY_CODE * (1.0 - placed[n_blk : 2 * n_blk])
        for c in range(n_blk):
            oct_send[c] = code[c : c + 1, :]
        fill_send[...] = jnp.broadcast_to(filled, (8, LANES))
        k = iota((8, LANES), 0)
        e = iota((8, LANES), 1)
        filled_8 = jnp.broadcast_to(filled, (8, LANES))
        fill_below = jnp.where(e == 0, 0.0, pltpu.roll(filled_8, 1, 1))
        fill_above = jnp.where(e == LANES - 1, 0.0, pltpu.roll(filled_8, LANES - 1, 1))
        k_weight = (PENALTY * UNIT_LENGTH) * jnp.where(
            k == 0, fill_below, jnp.where(k == 7, fill_above, 0.0)
        )

        @pl.when(jnp.logical_not(has_below))
        def _():
            fill_in[0] = jnp.zeros((8, LANES), F32)
            for step in range(STEPS):
                face_in[step, 0] = jnp.zeros((192, LANES), F32)

        @pl.when(jnp.logical_not(has_above))
        def _():
            fill_in[1] = jnp.zeros((8, LANES), F32)
            for step in range(STEPS):
                face_in[step, 1] = jnp.zeros((192, LANES), F32)

        def dilate(i, carry):
            f = gradients(cur, i)
            det = (
                f[0][0] * (f[1][1] * f[2][2] - f[1][2] * f[2][1])
                - f[0][1] * (f[1][0] * f[2][2] - f[1][2] * f[2][0])
                + f[0][2] * (f[1][0] * f[2][1] - f[1][1] * f[2][0])
            )
            change = (det - 1.0) * filled * DILATION_SCALE
            for j in range(8):
                dil_rows[pl.ds(i * 64 + j, 8, stride=8), :] = change[j]
            return carry

        def elastic(i, carry):
            f = gradients(cur, i)
            shear, lame = slab(mat, 0, i), slab(mat, 1, i)
            c = [[None] * 3 for _ in range(3)]
            for a in range(3):
                for b in range(a, 3):
                    c[a][b] = f[0][a] * f[0][b] + f[1][a] * f[1][b] + f[2][a] * f[2][b]
                c[a][a] = c[a][a] - 1.0
            trace = (0.5 * lame) * (c[0][0] + c[1][1] + c[2][2])
            s = [[None] * 3 for _ in range(3)]
            for a in range(3):
                for b in range(a, 3):
                    s[a][b] = s[b][a] = shear * c[a][b]
            for a in range(3):
                s[a][a] = s[a][a] + trace
            for r in range(3):
                p = [f[r][0] * s[0][j] + f[r][1] * s[1][j] + f[r][2] * s[2][j] for j in range(3)]
                put_slab(piola, r, i, p[0])
                own = slab(cur, r, i)
                z_below = pltpu.roll(pltpu.roll(own, 1, 1), 1, 2)
                z_above = pltpu.roll(pltpu.roll(own, 7, 1), LANES - 1, 2)
                pull = k_weight * (jnp.where(iota(own.shape, 1) == 0, z_below, z_above) - own)
                put_slab(part, r, i, along_j(p[1]) + along_k(p[2]) + pull)
            cof = cofactors(f)
            for r in range(3):
                for j in range(3):
                    put_slab(cofactor, 3 * r + j, i, cof[r][j])
            return carry

        def swell(i, carry):
            pressure = jnp.concatenate(
                [press[pl.ds(i * 64 + j, 8, stride=8), :][None] for j in range(8)], axis=0
            )
            for r in range(3):
                p = [pressure * slab(cofactor, 3 * r + j, i) for j in range(3)]
                put_slab(piola, r, i, slab(piola, r, i) - p[0])
                put_slab(part, r, i, slab(part, r, i) - (along_j(p[1]) + along_k(p[2])))
            return carry

        def advance(i, carry):
            below, above, scale = i_span(i)
            gain = (TIME_STEP / UNIT_LENGTH) * slab(mat, 2, i) * filled
            for r in range(3):
                s = slab(cur, r, i)
                force = slab(part, r, i) + (slab(piola, r, above) - slab(piola, r, below)) * scale
                put_slab(cur, r, i, s + gain * force)
            return carry

        def take(first, last):
            lanes = slice(first * 64, last * 64)
            for i in range(first, last):
                dilate(i, 0)
            taken = lax.dot_general(
                perm[...],
                dil_rows[lanes, :].astype(BF16),
                (((1,), (1,)), ((), ())),
                preferred_element_type=F32,
            )
            dil_send[:, :, lanes] = taken.reshape(n_blk, CAP, (last - first) * 64).astype(BF16)

        def send_taken(step, first, last):
            lanes = pl.ds(first * 64, (last - first) * 64)

            for shift in far_first(True):
                c = columns[shift]
                send(
                    dil_send.at[c, :, lanes],
                    dil_in.at[step, mine, :, lanes],
                    sent.at[1 + step],
                    got.at[1 + n_mech * step + grp],
                    n_mech,
                    c,
                )

        def send_faces(step):
            for r in range(3):

                @pl.when(has_above)
                def _():
                    send(
                        cur.at[pl.ds(r * 512 + 448, 64)],
                        face_in.at[step, 0, pl.ds(r * 64, 64)],
                        sent.at[3 + 2 * step + 1],
                        got.at[4 + 2 * step + 0],
                        grp,
                        blk + 1,
                    )

                @pl.when(has_below)
                def _():
                    send(
                        cur.at[pl.ds(r * 512, 64)],
                        face_in.at[step, 1, pl.ds(r * 64, 64)],
                        sent.at[3 + 2 * step + 0],
                        got.at[4 + 2 * step + 1],
                        grp,
                        blk - 1,
                    )

        with phase("m_load"):
            loads[0].wait()
        with phase("m_take"):
            take(0, 8)

        with phase("m_barrier"):
            pl.semaphore_wait(barrier, n_blk + beside)

        mine = grp * n_blk + blk

        with phase("m_send_oct"):
            for shift in far_first(True):
                c = columns[shift]
                send(oct_send.at[c], oct_in.at[mine], sent.at[0], got.at[0], n_mech, c)

        @pl.when(has_above)
        def _():
            send(fill_send, fill_in.at[0], sent.at[7 + 1], got.at[8 + 0], grp, blk + 1)

        @pl.when(has_below)
        def _():
            send(fill_send, fill_in.at[1], sent.at[7 + 0], got.at[8 + 1], grp, blk - 1)

        send_faces(0)
        loads[1].wait()
        for step in range(STEPS):
            with phase("m_elastic"):
                lax.fori_loop(0, 8, elastic, 0)
            if step == 0:
                with phase("m_send_dil"):
                    send_taken(0, 0, 8)
            if step > 0:
                send_faces(step)
            with phase("m_faces"):
                for side, present in ((0, has_below), (1, has_above)):

                    @pl.when(present)
                    def _():
                        wait_all(face_in.at[step, side], got.at[4 + 2 * step + side])
                        wait_all(face_in.at[step, side], sent.at[3 + 2 * step + side])
                        if step == 0:
                            wait_all(fill_send, got.at[8 + side])
                            wait_all(fill_send, sent.at[7 + side])

                    at = 7 * side
                    weight = (PENALTY * UNIT_LENGTH) * fill_in[side]
                    for r in range(3):
                        other = face_in[step, side, pl.ds(r * 64, 64), :].reshape(8, 8, LANES)
                        extra = weight * (other - slab(cur, r, at))
                        put_slab(part, r, at, slab(part, r, at) + extra)
            for at, (first, last) in enumerate(PRESSURE_SPANS[step]):
                lanes = slice(first * 64, last * 64)
                with phase("m_wait_press"):
                    wait_all(
                        press_in.at[step, :, :, pl.ds(first * 64, (last - first) * 64)],
                        got.at[3 * step + at],
                    )
                with phase("m_press"):
                    arrived = press_in[step, :, :, lanes].astype(F32)
                    press[lanes, :] = PRESSURE_SCALE * lax.dot_general(
                        arrived.reshape(slots, (last - first) * 64).astype(BF16),
                        perm[...],
                        (((0,), (0,)), ((), ())),
                        preferred_element_type=F32,
                    )
                with phase("m_swell"):
                    for i in range(first, last):
                        swell(i, 0)
                with phase("m_advance"):
                    for i in range(max(first - 1, 0), last - 1 if last < 8 else 8):
                        advance(i, 0)
                if step + 1 < STEPS:
                    if at == 0:
                        wait_all(dil_send, sent.at[1 + step])
                    ready = (max(first - 2, 0), last - 2 if last < 8 else 8)
                    with phase("m_take"):
                        take(*ready)
                    with phase("m_send_dil"):
                        send_taken(step + 1, *ready)
        wait_all(oct_send, sent.at[0])
        wait_all(dil_send, sent.at[1 + STEPS - 1])

    def brick():
        with phase("s_greet"):
            for g in range(n_mech):

                for shift in far_first(g < 2):
                    greet(g, columns[shift])
        row = iota((768, LANES), 0)
        at_octant = row // 8 == iota((768, LANES), 1)
        for k in range(8):
            select[:, k * LANES : (k + 1) * LANES] = flag(at_octant & (row % 8 == k), BF16)
        def split(value, lanes):
            count = value.shape[0]
            high = value.astype(BF16)
            rest = value - high.astype(F32)
            middle = rest.astype(BF16)
            low = (rest - middle.astype(F32)).astype(BF16)
            for at, piece in enumerate((high, middle, low)):
                pieces[at * count : (at + 1) * count, lanes] = piece

        def joined(product):
            return product[0:256] + product[256:512] + product[512:768]

        def to_layers(source, target, first, scale):
            for zq in range(6):
                split(source[pl.ds(zq, 256, stride=6), :], slice(zq * LANES, zq * LANES + LANES))
            for pair in range(4):
                lanes = slice(pair * 256, pair * 256 + 256)
                both = joined(
                    jnp.dot(pieces[...], select[:, lanes], preferred_element_type=F32)
                )
                for half in range(2):
                    value = scale * both[:, half * LANES : (half + 1) * LANES]
                    for x in range(16):
                        at = ((first + x) * 8 + 2 * pair + half) * 16
                        target[at : at + 16, :] = value[x * 16 : x * 16 + 16]

        k_row, column_256 = iota((256, 256), 0), iota((256, 256), 1)
        for block in range(3):
            k_held = k_row // LANES * 4 + (k_row // 32 + 4 - block) % 4
            chosen = (k_row % 32 == column_256 // 8) & (k_held == column_256 % 8)
            pick[block] = flag(chosen, BF16)

        def from_layers(source, first, spans):
            count = 16 * sum(last - start for start, last in spans)
            place = iota((count, LANES), 1) // 32
            for half in range(2):
                lanes = slice(half * LANES, (half + 1) * LANES)
                turned = []
                for k in range(4 * half, 4 * half + 4):
                    rows = [
                        source[at : at + 16, :]
                        for start, last in spans
                        for at in [((first + x) * 8 + k) * 16 for x in range(start, last)]
                    ]
                    rows = jnp.concatenate(rows, axis=0)
                    turned.append(pltpu.roll(rows, 32 * (k % 4), 1) if k % 4 else rows)
                for block in range(3):
                    value = turned[(3 - block) % 4]
                    for at in range(3):
                        value = jnp.where(place == at, turned[(at - block) % 4], value)
                    high = value.astype(BF16)
                    packed[block, 0:count, lanes] = high
                    packed[block, count : 2 * count, lanes] = (
                        value - high.astype(F32)
                    ).astype(BF16)
            for block in range(3):
                both = jnp.dot(
                    packed[block, 0 : 2 * count, :], pick[block], preferred_element_type=F32
                )
                both = both[0:count] + both[count : 2 * count]
                for half in range(2):
                    taken = 0
                    for start, last in spans:
                        more = 16 * (last - start)
                        cur[pl.ds(start * 96 + 2 * block + half, more, stride=6), :] = both[
                            taken : taken + more, half * LANES : (half + 1) * LANES
                        ]
                        taken += more

        plane = (1, 16, LANES)
        not_first = flag(iota(plane, 1) > 0)
        not_last = flag(iota(plane, 1) < 15)
        at_start = iota(plane, 2) == 0
        at_end = iota(plane, 2) >= DEPTH_OCTANTS - 1

        def sweep(source, source_first, target, target_first, diff_first, start, last):
            source_first, target_first = source_first + start, target_first + start
            diff_first = diff_first + start

            def rows_from(row):
                return source[pl.ds(row, LAYER), :].reshape(8, 16, LANES)

            below = rows_from((source_first - 1) * LAYER)
            first = rows_from(source_first * LAYER)
            entering = (below * below + (first * first + 1.0)) * (first - below)

            def one_layer(x, carry):
                centre, entering = carry
                row = pl.multiple_of((source_first + x) * LAYER, LAYER)
                x_above = rows_from(pl.multiple_of(row + LAYER, LAYER))
                y_below, y_above = rows_from(row - 1), rows_from(row + 1)
                square = centre * centre
                weight = square + 1.0

                def flux(there):
                    return (weight + there * there) * (there - centre)

                leaving = flux(x_above)
                inflow = leaving - entering
                inflow = inflow + not_last * flux(y_above) + not_first * flux(y_below)
                after = jnp.where(at_end, centre[7:8], pltpu.roll(centre[0:1], LANES - 1, 2))
                before = jnp.where(at_start, centre[0:1], pltpu.roll(centre[7:8], 1, 2))
                inner = (weight[1:] + square[:-1]) * (centre[1:] - centre[:-1])
                leave = (weight[7:8] + after * after) * (after - centre[7:8])
                enter = (weight[0:1] + before * before) * (before - centre[0:1])
                inflow = inflow + (
                    jnp.concatenate([inner, leave], axis=0)
                    - jnp.concatenate([-enter, inner], axis=0)
                )
                gain = rows_of(diff, (diff_first + x) * LAYER, LAYER).reshape(8, 16, LANES)
                updated = centre + gain * inflow
                at = pl.multiple_of((target_first + x) * LAYER, LAYER)
                target[pl.ds(at, LAYER), :] = updated.reshape(LAYER, LANES)
                return x_above, leaving

            lax.fori_loop(0, last - start, one_layer, (first, entering), unroll=2)

        with phase("s_load"):
            loads[0].wait()
        with phase("s_to_layers"):
            to_layers(cur, phi_a.at[0], 2, 1.0)

        def make_pressure(step):
            phi = phi_a.at[step]

            def one_i(i, carry):
                for t in range(4):
                    x, y = 8 * (t // 2), 8 * (t % 2)
                    value = jnp.concatenate(
                        [rows_of(phi, ((2 + x + i) * 8 + k) * 16 + y, 8) for k in range(8)], axis=0
                    )
                    value = value + CUBIC_TERM * value * value * value
                    at = pl.multiple_of(i * 64, 64)
                    pi_rows[pl.ds(at, 64), t * LANES : (t + 1) * LANES] = value.astype(BF16)
                return carry

            lax.fori_loop(0, 8, one_i, 0)

        def send_pressure(step):
            for at, (first, last) in enumerate(PRESSURE_SPANS[step]):
                wide = slice(first * 64, last * 64)
                lanes = pl.ds(first * 64, (last - first) * 64)
                for g in range(n_mech):
                    taken = lax.dot_general(
                        hits[g * n_blk * CAP : (g + 1) * n_blk * CAP, :],
                        pi_rows[wide, :],
                        (((1,), (1,)), ((), ())),
                        preferred_element_type=F32,
                    )
                    press_send[step, g * n_blk : (g + 1) * n_blk, :, wide] = taken.reshape(
                        n_blk, CAP, (last - first) * 64
                    ).astype(BF16)

                    for shift in far_first(g < 2):
                        c = columns[shift]
                        send(
                            press_send.at[step, g * n_blk + c, :, lanes],
                            press_in.at[step, blk, :, lanes],
                            sent.at[step],
                            got.at[3 * step + at],
                            g,
                            c,
                        )

        with phase("s_pi"):
            make_pressure(0)
        loads[1].wait()
        with phase("s_to_layers_d"):
            to_layers(mat, diff, 1, 0.5 * SWEEP_STEP)
        with phase("s_barrier"):
            pl.semaphore_wait(barrier, beside)

        @pl.when(has_above)
        def _():
            rim = (sent.at[6 + 1], got.at[11 + 0])
            send_pieces(diff, 16 * LAYER, diff, 0, LAYER, *rim, grp, blk + 1)

        @pl.when(has_below)
        def _():
            rim = (sent.at[6 + 0], got.at[11 + 1])
            send_pieces(diff, LAYER, diff, 17 * LAYER, LAYER, *rim, grp, blk - 1)

        with phase("s_wait_oct"):
            wait_all(oct_in, got.at[0])
        with phase("s_hits"):
            spread = (n_mech * n_blk, CAP, LANES)
            one_code = jnp.where(
                iota(spread, 1) == iota(spread, 2), jnp.broadcast_to(oct_in[...], spread), 0.0
            )
            wanted = jnp.dot(
                one_code.reshape(n_mech * n_blk * CAP, LANES).astype(BF16),
                jnp.ones((LANES, LANES), BF16),
                preferred_element_type=F32,
            )
            lane = iota(wanted.shape, 1)
            for t in range(4):
                at_octant = (lane + t * DEPTH_OCTANTS).astype(F32) - CODE_SHIFT
                mine = (wanted == at_octant) & (lane < DEPTH_OCTANTS)
                hits[:, t * LANES : (t + 1) * LANES] = flag(mine, BF16)
        with phase("s_send_press"):
            send_pressure(0)
        @pl.when(jnp.logical_not(has_below))
        def _():
            diff[0:LAYER, :] = jnp.zeros((LAYER, LANES), F32)
            for step in range(STEPS):
                phi_a[step, 0 : 2 * LAYER, :] = jnp.zeros((2 * LAYER, LANES), F32)

        @pl.when(jnp.logical_not(has_above))
        def _():
            diff[17 * LAYER : 18 * LAYER, :] = jnp.zeros((LAYER, LANES), F32)
            for step in range(STEPS):
                phi_a[step, 18 * LAYER : 20 * LAYER, :] = jnp.zeros((2 * LAYER, LANES), F32)

        for step in range(STEPS):
            phi = phi_a.at[step]
            if step > 0:
                with phase("s_pi"):
                    make_pressure(step)
                with phase("s_send_press"):
                    send_pressure(step)
            for g in (2, 0, 1):
                span = slice(g * n_blk, (g + 1) * n_blk)
                rows = slice(g * n_blk * CAP, (g + 1) * n_blk * CAP)
                with phase("s_wait_dil"):
                    wait_all(dil_in.at[step, span], got.at[1 + n_mech * step + g])
                arrived = dil_in[step, span].astype(F32)
                arrived = arrived.reshape(n_blk * CAP, NODES).astype(BF16)
                if g != 1:
                    with phase("s_collect"):
                        share = lax.dot_general(
                            arrived,
                            hits[rows, :],
                            (((0,), (0,)), ((), ())),
                            preferred_element_type=F32,
                        )
                        total[...] = share if g == 2 else total[...] + share

            def finish(ox, first, last):
                taken = slice(first * 64, last * 64)
                lanes = slice(ox * 256, ox * 256 + 256)
                share = lax.dot_general(
                    arrived[:, taken],
                    hits[rows, lanes],
                    (((0,), (0,)), ((), ())),
                    preferred_element_type=F32,
                )
                source = (SWEEP_STEP * SOURCE_RATE) * (total[taken, lanes] + share)
                for i in range(first, last):
                    for k in range(8):
                        at, row = ((2 + 8 * ox + i) * 8 + k) * 16, (i - first) * 64 + k * 8
                        for oy in range(2):
                            cells = slice(at + 8 * oy, at + 8 * oy + 8)
                            more = source[row : row + 8, oy * LANES : (oy + 1) * LANES]
                            phi[cells, :] = phi[cells, :] + more

            with phase("s_deposit_edge"):
                finish(0, 0, 2)
                finish(1, 6, 8)

            @pl.when(has_above)
            def _():
                halo_send[1] = phi[16 * LAYER : 18 * LAYER, :].astype(BF16)
                halo = (sent.at[2 + 2 * step + 1], got.at[7 + 2 * step + 0])
                target = halo_in.at[step, 0]
                send_pieces(halo_send.at[1], 0, target, 0, 2 * LAYER, *halo, grp, blk + 1)

            @pl.when(has_below)
            def _():
                halo_send[0] = phi[2 * LAYER : 4 * LAYER, :].astype(BF16)
                halo = (sent.at[2 + 2 * step + 0], got.at[7 + 2 * step + 1])
                target = halo_in.at[step, 1]
                send_pieces(halo_send.at[0], 0, target, 0, 2 * LAYER, *halo, grp, blk - 1)

            with phase("s_deposit"):
                finish(0, 2, 8)
                finish(1, 0, 6)
            after = phi_a.at[(step + 1) % 2]
            with phase("s_sweep_inner"):
                sweep(phi, 2, phi_b, 1, 1, 1, 15)
                sweep(phi_b, 1, after, 2, 1, 2, 14)
            if step == STEPS - 1:
                with phase("s_from_inner"):
                    from_layers(after, 2, [(2, 14)])
            with phase("s_wait_halo"):
                for side, present, first in ((0, has_below, 0), (1, has_above, 18)):

                    @pl.when(present)
                    def _():
                        two = halo_in.at[step, side]
                        wait_all(two, got.at[7 + 2 * step + side])
                        wait_all(two, sent.at[2 + 2 * step + side])
                        phi[first * LAYER : (first + 2) * LAYER, :] = two[...].astype(F32)
                        if step == 0:
                            one = diff.at[pl.ds(0, LAYER)]
                            wait_all(one, got.at[11 + side])
                            wait_all(one, sent.at[6 + side])

            with phase("s_sweep_edge"):
                sweep(phi, 2, phi_b, 1, 1, -1, 1)
                sweep(phi, 2, phi_b, 1, 1, 15, 17)
                sweep(phi_b, 1, after, 2, 1, 0, 2)
                sweep(phi_b, 1, after, 2, 1, 14, 16)
            with phase("s_sent"):
                wait_all(press_send.at[step], sent.at[step])
        with phase("s_from_edge"):
            from_layers(phi_a.at[STEPS % 2], 2, [(0, 2), (14, 16)])

    @pl.when(solvent)
    def _():
        brick()

    @pl.when(jnp.logical_not(solvent))
    def _():
        mechanics()


def solution(mesh):
    n_grp, n_blk = mesh.shape["grp"], mesh.shape["blk"]
    n_mech = n_grp - 1
    slots = n_blk * CAP
    dma = pltpu.SemaphoreType.DMA
    vmem = pltpu.VMEM
    whole = (1536, LANES)
    call = pl.pallas_call(
        functools.partial(kernel, n_grp, n_blk),
        out_shape=jax.ShapeDtypeStruct(whole, F32),
        in_specs=[pl.BlockSpec(memory_space=pltpu.HBM)] * 5,
        out_specs=pl.BlockSpec(memory_space=vmem),
        scratch_shapes=[
            vmem(whole, F32),
            vmem((1, LANES), jnp.int32),
            vmem((1, LANES), jnp.int32),
            vmem((1, LANES), jnp.int32),
            vmem((slots, LANES), BF16),
            vmem((n_blk, 1, LANES), F32),
            vmem((n_blk, CAP, NODES), BF16),
            vmem((NODES, LANES), F32),
            vmem((STEPS, n_blk, CAP, NODES), BF16),
            vmem((NODES, LANES), F32),
            vmem((STEPS, 2, 192, LANES), F32),
            vmem((2, 8, LANES), F32),
            vmem((8, LANES), F32),
            vmem(whole, F32),
            vmem(whole, F32),
            vmem((9 * NODES, LANES), F32),
            vmem((n_mech * n_blk, 1, LANES), F32),
            vmem((STEPS, n_mech * n_blk, CAP, NODES), BF16),
            vmem((STEPS, n_mech * n_blk, CAP, NODES), BF16),
            vmem((n_mech * n_blk * CAP, NODES), BF16),
            vmem((768, 1024), BF16),
            vmem((768, 768), BF16),
            vmem((2, 20 * LAYER, LANES), F32),
            vmem((18 * LAYER, LANES), F32),
            vmem((18 * LAYER, LANES), F32),
            vmem((2, 2 * LAYER, LANES), BF16),
            vmem((STEPS, 2, 2 * LAYER, LANES), BF16),
            vmem((3, 256, 256), BF16),
            vmem((3, 384, 256), BF16),
            vmem((NODES, NODES), BF16),
            vmem((NODES, NODES), F32),
            dma((5,)),
            dma((9,)),
            dma((13,)),
        ],
        compiler_params=pltpu.CompilerParams(
            collective_id=0, has_side_effects=True, vmem_limit_bytes=55 * 1000000
        ),
    )

    def shards(state, material, occupied, brick_column, brick_octant):
        operands = (
            state.reshape(whole),
            material.reshape(whole),
            occupied.reshape(1, LANES),
            brick_column.reshape(1, LANES),
            brick_octant.reshape(1, LANES),
        )
        out = call(*(pltpu.with_memory_space_constraint(x, pltpu.HBM) for x in operands))
        return out.reshape(state.shape)

    in_specs = (
        P("grp", None, None, "blk"),
        P("grp", None, None, "blk"),
        P(("grp", "blk")),
        P(("grp", "blk"), None),
        P(("grp", "blk")),
    )
    out_specs = P("grp", None, None, "blk")
    return jax.shard_map(shards, mesh=mesh, in_specs=in_specs, out_specs=out_specs, check_vma=False)
```

```python
import contextlib
import functools

import jax
import jax.numpy as jnp
from jax import lax
from jax.experimental import pallas as pl
from jax.experimental.pallas import tpu as pltpu
from jax.sharding import PartitionSpec as P

STEPS = 2
UNIT_LENGTH = 0.02
TIME_STEP = 0.1
PENALTY = 1.0
PRESSURE_SCALE = 0.05
DILATION_SCALE = 50.0
SWEEP_STEP = 0.03
SOURCE_RATE = 2.0
CUBIC_TERM = 0.3

MESH = pl.DeviceIdType.MESH
F32 = jnp.float32
BF16 = jnp.bfloat16
LANES = 128
NODES = 512
CAP = 8
HALO_PIECE = 64
DEPTH_OCTANTS = 96
CODE_SHIFT = 191.0
EMPTY_CODE = -1000.0
PRESSURE_SPANS = (((0, 4), (4, 6), (6, 8)), ((0, 8),))
LAYER = 128


def far_first(across):
    ring = (2, 1, 3, 0)
    along_y = (2, 1) if across else (0, 1)
    shifts = [(z, x, y) for z in ring for x in ring for y in range(2)]
    return sorted(shifts, key=lambda s: -(min(s[0], 4 - s[0]) + min(s[1], 4 - s[1]) + along_y[s[2]]))


def phase(name):
    return contextlib.nullcontext()


def iota(shape, dim):
    return lax.broadcasted_iota(jnp.int32, shape, dim)


def flag(mask, dtype=F32):
    return jnp.where(mask, 1.0, 0.0).astype(dtype)


def aligned(start, count):
    return start if isinstance(start, int) else pl.multiple_of(start, count)


def wait_all(ref, sem):
    pltpu.make_async_copy(ref, ref, sem).wait()


def rows_of(ref, start, count):
    return ref[pl.ds(aligned(start, count), count), :]


def slab(ref, r, i):
    return rows_of(ref, r * 512 + i * 64, 64).reshape(8, 8, LANES)


def put_slab(ref, r, i, value):
    ref[pl.ds(aligned(r * 512 + i * 64, 64), 64), :] = value.reshape(64, LANES)


def along_j(s):
    return jnp.concatenate([s[1:2] - s[0:1], 0.5 * (s[2:] - s[:-2]), s[7:8] - s[6:7]], axis=0)


def along_k(s):
    k = iota(s.shape, 1)
    edge = (k == 0) | (k == 7)
    upper = jnp.where(k == 7, s, pltpu.roll(s, 7, 1))
    lower = jnp.where(k == 0, s, pltpu.roll(s, 1, 1))
    return (upper - lower) * jnp.where(edge, 1.0, 0.5)


def i_span(i):
    if isinstance(i, int):
        return max(i - 1, 0), min(i + 1, 7), 1.0 if i in (0, 7) else 0.5
    below, above = jnp.maximum(i - 1, 0), jnp.minimum(i + 1, 7)
    return below, above, jnp.where((i == 0) | (i == 7), 1.0, 0.5)


def gradients(cur, i):
    below, above, scale = i_span(i)
    grads = []
    for r in range(3):
        s = slab(cur, r, i)
        row = [
            (slab(cur, r, above) - slab(cur, r, below)) * (UNIT_LENGTH * scale),
            along_j(s) * UNIT_LENGTH,
            along_k(s) * UNIT_LENGTH,
        ]
        row[r] = row[r] + 1.0
        grads.append(row)
    return grads


def cofactors(f):
    return [
        [
            f[1][1] * f[2][2] - f[1][2] * f[2][1],
            f[1][2] * f[2][0] - f[1][0] * f[2][2],
            f[1][0] * f[2][1] - f[1][1] * f[2][0],
        ],
        [
            f[0][2] * f[2][1] - f[0][1] * f[2][2],
            f[0][0] * f[2][2] - f[0][2] * f[2][0],
            f[0][1] * f[2][0] - f[0][0] * f[2][1],
        ],
        [
            f[0][1] * f[1][2] - f[0][2] * f[1][1],
            f[0][2] * f[1][0] - f[0][0] * f[1][2],
            f[0][0] * f[1][1] - f[0][1] * f[1][0],
        ],
    ]


def kernel(
    n_grp,
    n_blk,
    state_ref,
    material_ref,
    occupied_ref,
    column_ref,
    octant_ref,
    cur,
    mat,
    occupied_in,
    column_in,
    octant_in,
    perm,
    oct_send,
    dil_send,
    dil_rows,
    press_in,
    press,
    face_in,
    face_send,
    fill_in,
    fill_send,
    piola,
    part,
    cofactor,
    oct_in,
    dil_in,
    press_send,
    hits,
    select,
    pieces,
    phi_a,
    phi_b,
    diff,
    halo_send,
    halo_in,
    pick,
    packed,
    pi_rows,
    total,
    local_sem,
    send_sem,
    recv_sem,
):
    grp, blk = lax.axis_index("grp"), lax.axis_index("blk")
    sent, got = send_sem, recv_sem
    n_mech = n_grp - 1
    solvent = grp == n_mech
    barrier = pltpu.get_barrier_semaphore()
    has_below, has_above = blk > 0, blk < n_blk - 1
    loads = [
        pltpu.make_async_copy(state_ref, cur, local_sem.at[0]),
        pltpu.make_async_copy(material_ref, mat, local_sem.at[1]),
    ]
    for copy in loads:
        copy.start()

    def greet(g, c):
        pl.semaphore_signal(barrier, inc=1, device_id=(g, c), device_id_type=MESH)

    @pl.when(has_below)
    def _():
        greet(grp, blk - 1)

    @pl.when(has_above)
    def _():
        greet(grp, blk + 1)

    def column_at(shift):
        z, x, y = blk // 8 + shift[0], blk // 2 + shift[1], blk + shift[2]
        return lax.rem(z, 4) * 8 + lax.rem(x, 4) * 2 + lax.rem(y, 2)

    columns = {shift: column_at(shift) for shift in far_first(True)}
    beside = jnp.where(has_below, 1, 0) + jnp.where(has_above, 1, 0)

    def send(src, dst, send_sem, recv_sem, g, c):
        copy = pltpu.make_async_remote_copy(
            src_ref=src,
            dst_ref=dst,
            send_sem=send_sem,
            recv_sem=recv_sem,
            device_id=(g, c),
            device_id_type=MESH,
        )
        copy.start()

    def send_pieces(source, first, target, there, count, send_sem, recv_sem, g, c):
        for at in range(0, count, HALO_PIECE):
            send(
                source.at[pl.ds(first + at, HALO_PIECE)],
                target.at[pl.ds(there + at, HALO_PIECE)],
                send_sem,
                recv_sem,
                g,
                c,
            )

    def mechanics():
        small = [
            pltpu.make_async_copy(source, target, local_sem.at[2 + at])
            for at, (source, target) in enumerate(
                (
                    (occupied_ref, occupied_in),
                    (column_ref, column_in),
                    (octant_ref, octant_in),
                )
            )
        ]
        for copy in small:
            copy.start()
        with phase("m_small"):
            for copy in small:
                copy.wait()
        filled = occupied_in[...].astype(F32)
        column = column_in[...].astype(F32)
        octant = octant_in[...].astype(F32)
        square = (LANES, LANES)
        across = jnp.broadcast_to(column, square)
        diagonal = iota(square, 0) == iota(square, 1)
        down = jnp.sum(jnp.where(diagonal, across, 0.0), axis=1, keepdims=True)
        same = down == across
        rank = jnp.sum(flag(same & (iota(square, 0) < iota(square, 1))), axis=0, keepdims=True)
        rank_down = jnp.sum(
            flag(same & (iota(square, 1) < iota(square, 0))), axis=1, keepdims=True
        )
        slot = column * CAP + rank
        slots = n_blk * CAP
        hit = iota((slots, LANES), 0).astype(F32) == slot
        perm[...] = flag(hit, BF16)
        at_column = iota((n_blk, LANES), 0).astype(F32) == column
        coded = jnp.concatenate(
            [jnp.where(at_column, octant - CODE_SHIFT, 0.0), flag(at_column)], axis=0
        ).astype(BF16)
        at_rank = flag(iota(square, 1).astype(F32) == rank_down, BF16)
        placed = jnp.dot(coded, at_rank, preferred_element_type=F32)
        code = placed[0:n_blk] + EMPTY_CODE * (1.0 - placed[n_blk : 2 * n_blk])
        for c in range(n_blk):
            oct_send[c] = code[c : c + 1, :]
        fill_send[...] = jnp.broadcast_to(filled, (8, LANES))
        k = iota((8, LANES), 0)
        e = iota((8, LANES), 1)
        filled_8 = jnp.broadcast_to(filled, (8, LANES))
        fill_below = jnp.where(e == 0, 0.0, pltpu.roll(filled_8, 1, 1))
        fill_above = jnp.where(e == LANES - 1, 0.0, pltpu.roll(filled_8, LANES - 1, 1))
        k_weight = (PENALTY * UNIT_LENGTH) * jnp.where(
            k == 0, fill_below, jnp.where(k == 7, fill_above, 0.0)
        )

        @pl.when(jnp.logical_not(has_below))
        def _():
            fill_in[0] = jnp.zeros((8, LANES), F32)
            for step in range(STEPS):
                face_in[step, 0] = jnp.zeros((192, LANES), BF16)

        @pl.when(jnp.logical_not(has_above))
        def _():
            fill_in[1] = jnp.zeros((8, LANES), F32)
            for step in range(STEPS):
                face_in[step, 1] = jnp.zeros((192, LANES), BF16)

        def dilate(i, carry):
            f = gradients(cur, i)
            det = (
                f[0][0] * (f[1][1] * f[2][2] - f[1][2] * f[2][1])
                - f[0][1] * (f[1][0] * f[2][2] - f[1][2] * f[2][0])
                + f[0][2] * (f[1][0] * f[2][1] - f[1][1] * f[2][0])
            )
            change = (det - 1.0) * filled * DILATION_SCALE
            for j in range(8):
                dil_rows[pl.ds(i * 64 + j, 8, stride=8), :] = change[j]
            return carry

        def elastic(i, carry):
            f = gradients(cur, i)
            shear, lame = slab(mat, 0, i), slab(mat, 1, i)
            c = [[None] * 3 for _ in range(3)]
            for a in range(3):
                for b in range(a, 3):
                    c[a][b] = f[0][a] * f[0][b] + f[1][a] * f[1][b] + f[2][a] * f[2][b]
                c[a][a] = c[a][a] - 1.0
            trace = (0.5 * lame) * (c[0][0] + c[1][1] + c[2][2])
            s = [[None] * 3 for _ in range(3)]
            for a in range(3):
                for b in range(a, 3):
                    s[a][b] = s[b][a] = shear * c[a][b]
            for a in range(3):
                s[a][a] = s[a][a] + trace
            for r in range(3):
                p = [f[r][0] * s[0][j] + f[r][1] * s[1][j] + f[r][2] * s[2][j] for j in range(3)]
                put_slab(piola, r, i, p[0])
                own = slab(cur, r, i)
                z_below = pltpu.roll(pltpu.roll(own, 1, 1), 1, 2)
                z_above = pltpu.roll(pltpu.roll(own, 7, 1), LANES - 1, 2)
                pull = k_weight * (jnp.where(iota(own.shape, 1) == 0, z_below, z_above) - own)
                put_slab(part, r, i, along_j(p[1]) + along_k(p[2]) + pull)
            cof = cofactors(f)
            for r in range(3):
                for j in range(3):
                    put_slab(cofactor, 3 * r + j, i, cof[r][j])
            return carry

        def swell(i, carry):
            pressure = jnp.concatenate(
                [press[pl.ds(i * 64 + j, 8, stride=8), :][None] for j in range(8)], axis=0
            )
            for r in range(3):
                p = [pressure * slab(cofactor, 3 * r + j, i) for j in range(3)]
                put_slab(piola, r, i, slab(piola, r, i) - p[0])
                put_slab(part, r, i, slab(part, r, i) - (along_j(p[1]) + along_k(p[2])))
            return carry

        def advance(i, carry):
            below, above, scale = i_span(i)
            gain = (TIME_STEP / UNIT_LENGTH) * slab(mat, 2, i) * filled
            for r in range(3):
                s = slab(cur, r, i)
                force = slab(part, r, i) + (slab(piola, r, above) - slab(piola, r, below)) * scale
                put_slab(cur, r, i, s + gain * force)
            return carry

        def take(first, last):
            lanes = slice(first * 64, last * 64)
            for i in range(first, last):
                dilate(i, 0)
            taken = lax.dot_general(
                perm[...],
                dil_rows[lanes, :].astype(BF16),
                (((1,), (1,)), ((), ())),
                preferred_element_type=F32,
            )
            dil_send[:, :, lanes] = taken.reshape(n_blk, CAP, (last - first) * 64).astype(BF16)

        def send_taken(step, first, last):
            lanes = pl.ds(first * 64, (last - first) * 64)

            for shift in far_first(True):
                c = columns[shift]
                send(
                    dil_send.at[c, :, lanes],
                    dil_in.at[step, mine, :, lanes],
                    sent.at[1 + step],
                    got.at[1 + n_mech * step + grp],
                    n_mech,
                    c,
                )

        def send_faces(step):
            for r in range(3):
                face_send[0, r * 64 : r * 64 + 64] = cur[r * 512 : r * 512 + 64, :].astype(BF16)
                face_send[1, r * 64 : r * 64 + 64] = cur[
                    r * 512 + 448 : r * 512 + 512, :
                ].astype(BF16)

            @pl.when(has_above)
            def _():
                face = (sent.at[3 + 2 * step + 1], got.at[4 + 2 * step + 0])
                send_pieces(face_send.at[1], 0, face_in.at[step, 0], 0, 192, *face, grp, blk + 1)

            @pl.when(has_below)
            def _():
                face = (sent.at[3 + 2 * step + 0], got.at[4 + 2 * step + 1])
                send_pieces(face_send.at[0], 0, face_in.at[step, 1], 0, 192, *face, grp, blk - 1)

        def meet_faces(step):
            with phase("m_faces"):
                for side, present in ((0, has_below), (1, has_above)):

                    @pl.when(present)
                    def _():
                        wait_all(face_in.at[step, side], got.at[4 + 2 * step + side])
                        wait_all(face_in.at[step, side], sent.at[3 + 2 * step + side])
                        if step == 0:
                            wait_all(fill_send, got.at[8 + side])
                            wait_all(fill_send, sent.at[7 + side])

                    at = 7 * side
                    weight = (PENALTY * UNIT_LENGTH) * fill_in[side]
                    for r in range(3):
                        other = face_in[step, side, r * 64 : r * 64 + 64, :].astype(F32).reshape(8, 8, LANES)
                        extra = weight * (other - slab(cur, r, at))
                        put_slab(part, r, at, slab(part, r, at) + extra)

        with phase("m_load"):
            loads[0].wait()
        with phase("m_take"):
            take(0, 8)

        with phase("m_barrier"):
            pl.semaphore_wait(barrier, n_blk + beside)

        mine = grp * n_blk + blk

        with phase("m_send_oct"):
            for shift in far_first(True):
                c = columns[shift]
                send(oct_send.at[c], oct_in.at[mine], sent.at[0], got.at[0], n_mech, c)

        @pl.when(has_above)
        def _():
            send(fill_send, fill_in.at[0], sent.at[7 + 1], got.at[8 + 0], grp, blk + 1)

        @pl.when(has_below)
        def _():
            send(fill_send, fill_in.at[1], sent.at[7 + 0], got.at[8 + 1], grp, blk - 1)

        loads[1].wait()
        for step in range(STEPS):
            with phase("m_elastic"):
                lax.fori_loop(0, 8, elastic, 0)
            if step == 0:
                with phase("m_send_dil"):
                    send_taken(0, 0, 8)
            if step == 0:
                send_faces(0)
            if step > 0:
                send_faces(step)
            if step + 1 < STEPS:
                meet_faces(step)
            for at, (first, last) in enumerate(PRESSURE_SPANS[step]):
                lanes = slice(first * 64, last * 64)
                with phase("m_wait_press"):
                    wait_all(
                        press_in.at[step, :, :, pl.ds(first * 64, (last - first) * 64)],
                        got.at[3 * step + at],
                    )
                with phase("m_press"):
                    arrived = press_in[step, :, :, lanes].astype(F32)
                    press[lanes, :] = PRESSURE_SCALE * lax.dot_general(
                        arrived.reshape(slots, (last - first) * 64).astype(BF16),
                        perm[...],
                        (((0,), (0,)), ((), ())),
                        preferred_element_type=F32,
                    )
                with phase("m_swell"):
                    for i in range(first, last):
                        swell(i, 0)
                if step + 1 == STEPS:
                    meet_faces(step)
                with phase("m_advance"):
                    for i in range(max(first - 1, 0), last - 1 if last < 8 else 8):
                        advance(i, 0)
                if step + 1 < STEPS:
                    if at == 0:
                        wait_all(dil_send, sent.at[1 + step])
                    ready = (max(first - 2, 0), last - 2 if last < 8 else 8)
                    with phase("m_take"):
                        take(*ready)
                    with phase("m_send_dil"):
                        send_taken(step + 1, *ready)
        wait_all(oct_send, sent.at[0])
        wait_all(dil_send, sent.at[1 + STEPS - 1])

    def brick():
        with phase("s_greet"):
            for g in range(n_mech):

                for shift in far_first(g < 2):
                    greet(g, columns[shift])
        row = iota((768, LANES), 0)
        at_octant = row // 8 == iota((768, LANES), 1)
        for k in range(8):
            select[:, k * LANES : (k + 1) * LANES] = flag(at_octant & (row % 8 == k), BF16)
        def split(value, lanes):
            count = value.shape[0]
            high = value.astype(BF16)
            rest = value - high.astype(F32)
            middle = rest.astype(BF16)
            low = (rest - middle.astype(F32)).astype(BF16)
            for at, piece in enumerate((high, middle, low)):
                pieces[at * count : (at + 1) * count, lanes] = piece

        def joined(product):
            return product[0:256] + product[256:512] + product[512:768]

        def to_layers(source, target, first, scale):
            for zq in range(6):
                split(source[pl.ds(zq, 256, stride=6), :], slice(zq * LANES, zq * LANES + LANES))
            for pair in range(4):
                lanes = slice(pair * 256, pair * 256 + 256)
                both = joined(
                    jnp.dot(pieces[...], select[:, lanes], preferred_element_type=F32)
                )
                for half in range(2):
                    value = scale * both[:, half * LANES : (half + 1) * LANES]
                    for x in range(16):
                        at = ((first + x) * 8 + 2 * pair + half) * 16
                        target[at : at + 16, :] = value[x * 16 : x * 16 + 16]

        k_row, column_256 = iota((256, 256), 0), iota((256, 256), 1)
        for block in range(3):
            k_held = k_row // LANES * 4 + (k_row // 32 + 4 - block) % 4
            chosen = (k_row % 32 == column_256 // 8) & (k_held == column_256 % 8)
            pick[block] = flag(chosen, BF16)

        def from_layers(source, first, spans):
            count = 16 * sum(last - start for start, last in spans)
            place = iota((count, LANES), 1) // 32
            for half in range(2):
                lanes = slice(half * LANES, (half + 1) * LANES)
                turned = []
                for k in range(4 * half, 4 * half + 4):
                    rows = [
                        source[at : at + 16, :]
                        for start, last in spans
                        for at in [((first + x) * 8 + k) * 16 for x in range(start, last)]
                    ]
                    rows = jnp.concatenate(rows, axis=0)
                    turned.append(pltpu.roll(rows, 32 * (k % 4), 1) if k % 4 else rows)
                for block in range(3):
                    value = turned[(3 - block) % 4]
                    for at in range(3):
                        value = jnp.where(place == at, turned[(at - block) % 4], value)
                    high = value.astype(BF16)
                    packed[block, 0:count, lanes] = high
                    packed[block, count : 2 * count, lanes] = (
                        value - high.astype(F32)
                    ).astype(BF16)
            for block in range(3):
                both = jnp.dot(
                    packed[block, 0 : 2 * count, :], pick[block], preferred_element_type=F32
                )
                both = both[0:count] + both[count : 2 * count]
                for half in range(2):
                    taken = 0
                    for start, last in spans:
                        more = 16 * (last - start)
                        cur[pl.ds(start * 96 + 2 * block + half, more, stride=6), :] = both[
                            taken : taken + more, half * LANES : (half + 1) * LANES
                        ]
                        taken += more

        plane = (1, 16, LANES)
        not_first = flag(iota(plane, 1) > 0)
        not_last = flag(iota(plane, 1) < 15)
        at_start = iota(plane, 2) == 0
        at_end = iota(plane, 2) >= DEPTH_OCTANTS - 1

        def sweep(source, source_first, target, target_first, diff_first, start, last):
            source_first, target_first = source_first + start, target_first + start
            diff_first = diff_first + start

            def rows_from(row):
                return source[pl.ds(row, LAYER), :].reshape(8, 16, LANES)

            below = rows_from((source_first - 1) * LAYER)
            first = rows_from(source_first * LAYER)
            entering = (below * below + (first * first + 1.0)) * (first - below)

            def one_layer(x, carry):
                centre, entering = carry
                row = pl.multiple_of((source_first + x) * LAYER, LAYER)
                x_above = rows_from(pl.multiple_of(row + LAYER, LAYER))
                y_below, y_above = rows_from(row - 1), rows_from(row + 1)
                square = centre * centre
                weight = square + 1.0

                def flux(there):
                    return (weight + there * there) * (there - centre)

                leaving = flux(x_above)
                inflow = leaving - entering
                inflow = inflow + not_last * flux(y_above) + not_first * flux(y_below)
                after = jnp.where(at_end, centre[7:8], pltpu.roll(centre[0:1], LANES - 1, 2))
                before = jnp.where(at_start, centre[0:1], pltpu.roll(centre[7:8], 1, 2))
                inner = (weight[1:] + square[:-1]) * (centre[1:] - centre[:-1])
                leave = (weight[7:8] + after * after) * (after - centre[7:8])
                enter = (weight[0:1] + before * before) * (before - centre[0:1])
                inflow = inflow + (
                    jnp.concatenate([inner, leave], axis=0)
                    - jnp.concatenate([-enter, inner], axis=0)
                )
                gain = rows_of(diff, (diff_first + x) * LAYER, LAYER).reshape(8, 16, LANES)
                updated = centre + gain * inflow
                at = pl.multiple_of((target_first + x) * LAYER, LAYER)
                target[pl.ds(at, LAYER), :] = updated.reshape(LAYER, LANES)
                return x_above, leaving

            lax.fori_loop(0, last - start, one_layer, (first, entering), unroll=2)

        with phase("s_load"):
            loads[0].wait()
        with phase("s_to_layers"):
            to_layers(cur, phi_a.at[0], 2, 1.0)

        def make_pressure(step):
            phi = phi_a.at[step]

            def one_i(i, carry):
                for t in range(4):
                    x, y = 8 * (t // 2), 8 * (t % 2)
                    value = jnp.concatenate(
                        [rows_of(phi, ((2 + x + i) * 8 + k) * 16 + y, 8) for k in range(8)], axis=0
                    )
                    value = value + CUBIC_TERM * value * value * value
                    at = pl.multiple_of(i * 64, 64)
                    pi_rows[pl.ds(at, 64), t * LANES : (t + 1) * LANES] = value.astype(BF16)
                return carry

            lax.fori_loop(0, 8, one_i, 0)

        def send_pressure(step, span, g):
            first, last = PRESSURE_SPANS[step][span]
            wide = slice(first * 64, last * 64)
            lanes = pl.ds(first * 64, (last - first) * 64)
            taken = lax.dot_general(
                hits[g * n_blk * CAP : (g + 1) * n_blk * CAP, :],
                pi_rows[wide, :],
                (((1,), (1,)), ((), ())),
                preferred_element_type=F32,
            )
            press_send[step, g * n_blk : (g + 1) * n_blk, :, wide] = taken.reshape(
                n_blk, CAP, (last - first) * 64
            ).astype(BF16)
            for shift in far_first(g < 2):
                c = columns[shift]
                send(
                    press_send.at[step, g * n_blk + c, :, lanes],
                    press_in.at[step, blk, :, lanes],
                    sent.at[step],
                    got.at[3 * step + span],
                    g,
                    c,
                )

        with phase("s_pi"):
            make_pressure(0)
        loads[1].wait()
        with phase("s_to_layers_d"):
            to_layers(mat, diff, 1, 0.5 * SWEEP_STEP)
        with phase("s_barrier"):
            pl.semaphore_wait(barrier, beside)

        @pl.when(has_above)
        def _():
            rim = (sent.at[6 + 1], got.at[11 + 0])
            send_pieces(diff, 16 * LAYER, diff, 0, LAYER, *rim, grp, blk + 1)

        @pl.when(has_below)
        def _():
            rim = (sent.at[6 + 0], got.at[11 + 1])
            send_pieces(diff, LAYER, diff, 17 * LAYER, LAYER, *rim, grp, blk - 1)

        with phase("s_wait_oct"):
            wait_all(oct_in, got.at[0])
        def find_hits(g):
            spread = (n_blk, CAP, LANES)
            codes = jnp.broadcast_to(oct_in[g * n_blk : (g + 1) * n_blk], spread)
            one_code = jnp.where(iota(spread, 1) == iota(spread, 2), codes, 0.0)
            wanted = jnp.dot(
                one_code.reshape(n_blk * CAP, LANES).astype(BF16),
                jnp.ones((LANES, LANES), BF16),
                preferred_element_type=F32,
            )
            lane = iota(wanted.shape, 1)
            rows = slice(g * n_blk * CAP, (g + 1) * n_blk * CAP)
            for t in range(4):
                at_octant = (lane + t * DEPTH_OCTANTS).astype(F32) - CODE_SHIFT
                found = (wanted == at_octant) & (lane < DEPTH_OCTANTS)
                hits[rows, t * LANES : (t + 1) * LANES] = flag(found, BF16)

        with phase("s_send_press"):
            find_hits(0)
            send_pressure(0, 0, 0)
            find_hits(1)
            send_pressure(0, 0, 1)
            find_hits(2)
            send_pressure(0, 0, 2)
            send_pressure(0, 1, 0)
            send_pressure(0, 1, 1)
            send_pressure(0, 1, 2)
            send_pressure(0, 2, 0)
            send_pressure(0, 2, 1)
            send_pressure(0, 2, 2)
        @pl.when(jnp.logical_not(has_below))
        def _():
            diff[0:LAYER, :] = jnp.zeros((LAYER, LANES), F32)
            for step in range(STEPS):
                phi_a[step, 0 : 2 * LAYER, :] = jnp.zeros((2 * LAYER, LANES), F32)

        @pl.when(jnp.logical_not(has_above))
        def _():
            diff[17 * LAYER : 18 * LAYER, :] = jnp.zeros((LAYER, LANES), F32)
            for step in range(STEPS):
                phi_a[step, 18 * LAYER : 20 * LAYER, :] = jnp.zeros((2 * LAYER, LANES), F32)

        for step in range(STEPS):
            phi = phi_a.at[step]
            if step > 0:
                with phase("s_pi"):
                    make_pressure(step)
                with phase("s_send_press"):
                    for g in range(n_mech):
                        send_pressure(step, 0, g)
            for g in (2, 0, 1):
                span = slice(g * n_blk, (g + 1) * n_blk)
                rows = slice(g * n_blk * CAP, (g + 1) * n_blk * CAP)
                with phase("s_wait_dil"):
                    wait_all(dil_in.at[step, span], got.at[1 + n_mech * step + g])
                arrived = dil_in[step, span].astype(F32)
                arrived = arrived.reshape(n_blk * CAP, NODES).astype(BF16)
                if g != 1:
                    with phase("s_collect"):
                        share = lax.dot_general(
                            arrived,
                            hits[rows, :],
                            (((0,), (0,)), ((), ())),
                            preferred_element_type=F32,
                        )
                        total[...] = share if g == 2 else total[...] + share

            def finish(ox, first, last):
                taken = slice(first * 64, last * 64)
                lanes = slice(ox * 256, ox * 256 + 256)
                share = lax.dot_general(
                    arrived[:, taken],
                    hits[rows, lanes],
                    (((0,), (0,)), ((), ())),
                    preferred_element_type=F32,
                )
                source = (SWEEP_STEP * SOURCE_RATE) * (total[taken, lanes] + share)
                for i in range(first, last):
                    for k in range(8):
                        at, row = ((2 + 8 * ox + i) * 8 + k) * 16, (i - first) * 64 + k * 8
                        for oy in range(2):
                            cells = slice(at + 8 * oy, at + 8 * oy + 8)
                            more = source[row : row + 8, oy * LANES : (oy + 1) * LANES]
                            phi[cells, :] = phi[cells, :] + more

            with phase("s_deposit_edge"):
                finish(0, 0, 2)
                finish(1, 6, 8)

            @pl.when(has_above)
            def _():
                halo_send[1] = phi[16 * LAYER : 18 * LAYER, :].astype(BF16)
                halo = (sent.at[2 + 2 * step + 1], got.at[7 + 2 * step + 0])
                target = halo_in.at[step, 0]
                send_pieces(halo_send.at[1], 0, target, 0, 2 * LAYER, *halo, grp, blk + 1)

            @pl.when(has_below)
            def _():
                halo_send[0] = phi[2 * LAYER : 4 * LAYER, :].astype(BF16)
                halo = (sent.at[2 + 2 * step + 0], got.at[7 + 2 * step + 1])
                target = halo_in.at[step, 1]
                send_pieces(halo_send.at[0], 0, target, 0, 2 * LAYER, *halo, grp, blk - 1)

            with phase("s_deposit"):
                finish(0, 2, 8)
                finish(1, 0, 6)
            after = phi_a.at[(step + 1) % 2]
            with phase("s_sweep_inner"):
                sweep(phi, 2, phi_b, 1, 1, 1, 15)
                sweep(phi_b, 1, after, 2, 1, 2, 14)
            if step == STEPS - 1:
                with phase("s_from_inner"):
                    from_layers(after, 2, [(2, 14)])
            with phase("s_wait_halo"):
                for side, present, first in ((0, has_below, 0), (1, has_above, 18)):

                    @pl.when(present)
                    def _():
                        two = halo_in.at[step, side]
                        wait_all(two, got.at[7 + 2 * step + side])
                        wait_all(two, sent.at[2 + 2 * step + side])
                        phi[first * LAYER : (first + 2) * LAYER, :] = two[...].astype(F32)
                        if step == 0:
                            one = diff.at[pl.ds(0, LAYER)]
                            wait_all(one, got.at[11 + side])
                            wait_all(one, sent.at[6 + side])

            with phase("s_sweep_edge"):
                sweep(phi, 2, phi_b, 1, 1, -1, 1)
                sweep(phi, 2, phi_b, 1, 1, 15, 17)
                sweep(phi_b, 1, after, 2, 1, 0, 2)
                sweep(phi_b, 1, after, 2, 1, 14, 16)
            with phase("s_sent"):
                wait_all(press_send.at[step], sent.at[step])
        with phase("s_from_edge"):
            from_layers(phi_a.at[STEPS % 2], 2, [(0, 2), (14, 16)])

    @pl.when(solvent)
    def _():
        brick()

    @pl.when(jnp.logical_not(solvent))
    def _():
        mechanics()


def solution(mesh):
    n_grp, n_blk = mesh.shape["grp"], mesh.shape["blk"]
    n_mech = n_grp - 1
    slots = n_blk * CAP
    dma = pltpu.SemaphoreType.DMA
    vmem = pltpu.VMEM
    whole = (1536, LANES)
    call = pl.pallas_call(
        functools.partial(kernel, n_grp, n_blk),
        out_shape=jax.ShapeDtypeStruct(whole, F32),
        in_specs=[pl.BlockSpec(memory_space=pltpu.HBM)] * 5,
        out_specs=pl.BlockSpec(memory_space=vmem),
        scratch_shapes=[
            vmem(whole, F32),
            vmem((1, LANES), jnp.int32),
            vmem((1, LANES), jnp.int32),
            vmem((1, LANES), jnp.int32),
            vmem((slots, LANES), BF16),
            vmem((n_blk, 1, LANES), F32),
            vmem((n_blk, CAP, NODES), BF16),
            vmem((NODES, LANES), F32),
            vmem((STEPS, n_blk, CAP, NODES), BF16),
            vmem((NODES, LANES), F32),
            vmem((STEPS, 2, 192, LANES), BF16),
            vmem((2, 192, LANES), BF16),
            vmem((2, 8, LANES), F32),
            vmem((8, LANES), F32),
            vmem(whole, F32),
            vmem(whole, F32),
            vmem((9 * NODES, LANES), F32),
            vmem((n_mech * n_blk, 1, LANES), F32),
            vmem((STEPS, n_mech * n_blk, CAP, NODES), BF16),
            vmem((STEPS, n_mech * n_blk, CAP, NODES), BF16),
            vmem((n_mech * n_blk * CAP, NODES), BF16),
            vmem((768, 1024), BF16),
            vmem((768, 768), BF16),
            vmem((2, 20 * LAYER, LANES), F32),
            vmem((18 * LAYER, LANES), F32),
            vmem((18 * LAYER, LANES), F32),
            vmem((2, 2 * LAYER, LANES), BF16),
            vmem((STEPS, 2, 2 * LAYER, LANES), BF16),
            vmem((3, 256, 256), BF16),
            vmem((3, 384, 256), BF16),
            vmem((NODES, NODES), BF16),
            vmem((NODES, NODES), F32),
            dma((5,)),
            dma((9,)),
            dma((13,)),
        ],
        compiler_params=pltpu.CompilerParams(
            collective_id=0, has_side_effects=True, vmem_limit_bytes=55 * 1000000
        ),
    )

    def shards(state, material, occupied, brick_column, brick_octant):
        operands = (
            state.reshape(whole),
            material.reshape(whole),
            occupied.reshape(1, LANES),
            brick_column.reshape(1, LANES),
            brick_octant.reshape(1, LANES),
        )
        out = call(*(pltpu.with_memory_space_constraint(x, pltpu.HBM) for x in operands))
        return out.reshape(state.shape)

    in_specs = (
        P("grp", None, None, "blk"),
        P("grp", None, None, "blk"),
        P(("grp", "blk")),
        P(("grp", "blk"), None),
        P(("grp", "blk")),
    )
    out_specs = P("grp", None, None, "blk")
    return jax.shard_map(shards, mesh=mesh, in_specs=in_specs, out_specs=out_specs, check_vma=False)
```

```python
import contextlib
import functools

import jax
import jax.numpy as jnp
from jax import lax
from jax.experimental import pallas as pl
from jax.experimental.pallas import tpu as pltpu
from jax.sharding import PartitionSpec as P

STEPS = 2
UNIT_LENGTH = 0.02
TIME_STEP = 0.1
PENALTY = 1.0
PRESSURE_SCALE = 0.05
DILATION_SCALE = 50.0
SWEEP_STEP = 0.03
SOURCE_RATE = 2.0
CUBIC_TERM = 0.3

MESH = pl.DeviceIdType.MESH
F32 = jnp.float32
BF16 = jnp.bfloat16
LANES = 128
NODES = 512
CAP = 8
HALO_PIECE = 64
DEPTH_OCTANTS = 96
CODE_SHIFT = 191.0
EMPTY_CODE = -1000.0
PRESSURE_SPANS = (((0, 4), (4, 6), (6, 8)), ((0, 8),))
LAYER = 128


def far_first(across):
    ring = (2, 1, 3, 0)
    along_y = (2, 1) if across else (0, 1)
    shifts = [(z, x, y) for z in ring for x in ring for y in range(2)]
    return sorted(shifts, key=lambda s: -(min(s[0], 4 - s[0]) + min(s[1], 4 - s[1]) + along_y[s[2]]))


def phase(name):
    return contextlib.nullcontext()


def iota(shape, dim):
    return lax.broadcasted_iota(jnp.int32, shape, dim)


def flag(mask, dtype=F32):
    return jnp.where(mask, 1.0, 0.0).astype(dtype)


def aligned(start, count):
    return start if isinstance(start, int) else pl.multiple_of(start, count)


def wait_all(ref, sem):
    pltpu.make_async_copy(ref, ref, sem).wait()


def rows_of(ref, start, count):
    return ref[pl.ds(aligned(start, count), count), :]


def slab(ref, r, i):
    return rows_of(ref, r * 512 + i * 64, 64).reshape(8, 8, LANES)


def put_slab(ref, r, i, value):
    ref[pl.ds(aligned(r * 512 + i * 64, 64), 64), :] = value.reshape(64, LANES)


def along_j(s, scale=1.0):
    first, last = s[1:2] - s[0:1], s[7:8] - s[6:7]
    if scale != 1.0:
        first, last = scale * first, scale * last
    return jnp.concatenate([first, (0.5 * scale) * (s[2:] - s[:-2]), last], axis=0)


def along_k(s, scale=1.0):
    k = iota(s.shape, 1)
    edge = (k == 0) | (k == 7)
    upper = jnp.where(k == 7, s, pltpu.roll(s, 7, 1))
    lower = jnp.where(k == 0, s, pltpu.roll(s, 1, 1))
    return (upper - lower) * jnp.where(edge, scale, 0.5 * scale)


def i_span(i):
    if isinstance(i, int):
        return max(i - 1, 0), min(i + 1, 7), 1.0 if i in (0, 7) else 0.5
    below, above = jnp.maximum(i - 1, 0), jnp.minimum(i + 1, 7)
    return below, above, jnp.where((i == 0) | (i == 7), 1.0, 0.5)


def gradients(cur, i):
    below, above, scale = i_span(i)
    grads = []
    for r in range(3):
        s = slab(cur, r, i)
        row = [
            (slab(cur, r, above) - slab(cur, r, below)) * (UNIT_LENGTH * scale),
            along_j(s, UNIT_LENGTH),
            along_k(s, UNIT_LENGTH),
        ]
        row[r] = row[r] + 1.0
        grads.append(row)
    return grads


def cofactors(f):
    return [
        [
            f[1][1] * f[2][2] - f[1][2] * f[2][1],
            f[1][2] * f[2][0] - f[1][0] * f[2][2],
            f[1][0] * f[2][1] - f[1][1] * f[2][0],
        ],
        [
            f[0][2] * f[2][1] - f[0][1] * f[2][2],
            f[0][0] * f[2][2] - f[0][2] * f[2][0],
            f[0][1] * f[2][0] - f[0][0] * f[2][1],
        ],
        [
            f[0][1] * f[1][2] - f[0][2] * f[1][1],
            f[0][2] * f[1][0] - f[0][0] * f[1][2],
            f[0][0] * f[1][1] - f[0][1] * f[1][0],
        ],
    ]


def kernel(
    n_grp,
    n_blk,
    state_ref,
    material_ref,
    occupied_ref,
    column_ref,
    octant_ref,
    cur,
    mat,
    occupied_in,
    column_in,
    octant_in,
    perm,
    oct_send,
    dil_send,
    dil_rows,
    press_in,
    press,
    face_in,
    face_send,
    fill_in,
    fill_send,
    piola,
    part,
    cofactor,
    oct_in,
    dil_in,
    press_send,
    hits,
    select,
    pieces,
    phi_a,
    phi_b,
    diff,
    halo_send,
    halo_in,
    pick,
    packed,
    pi_rows,
    total,
    local_sem,
    send_sem,
    recv_sem,
):
    grp, blk = lax.axis_index("grp"), lax.axis_index("blk")
    sent, got = send_sem, recv_sem
    n_mech = n_grp - 1
    solvent = grp == n_mech
    barrier = pltpu.get_barrier_semaphore()
    has_below, has_above = blk > 0, blk < n_blk - 1
    loads = [
        pltpu.make_async_copy(state_ref, cur, local_sem.at[0]),
        pltpu.make_async_copy(material_ref, mat, local_sem.at[1]),
    ]
    for copy in loads:
        copy.start()

    def greet(g, c):
        pl.semaphore_signal(barrier, inc=1, device_id=(g, c), device_id_type=MESH)

    @pl.when(has_below)
    def _():
        greet(grp, blk - 1)

    @pl.when(has_above)
    def _():
        greet(grp, blk + 1)

    def column_at(shift):
        z, x, y = blk // 8 + shift[0], blk // 2 + shift[1], blk + shift[2]
        return lax.rem(z, 4) * 8 + lax.rem(x, 4) * 2 + lax.rem(y, 2)

    columns = {shift: column_at(shift) for shift in far_first(True)}
    beside = jnp.where(has_below, 1, 0) + jnp.where(has_above, 1, 0)

    def send(src, dst, send_sem, recv_sem, g, c):
        copy = pltpu.make_async_remote_copy(
            src_ref=src,
            dst_ref=dst,
            send_sem=send_sem,
            recv_sem=recv_sem,
            device_id=(g, c),
            device_id_type=MESH,
        )
        copy.start()

    def send_pieces(source, first, target, there, count, send_sem, recv_sem, g, c):
        for at in range(0, count, HALO_PIECE):
            send(
                source.at[pl.ds(first + at, HALO_PIECE)],
                target.at[pl.ds(there + at, HALO_PIECE)],
                send_sem,
                recv_sem,
                g,
                c,
            )

    def mechanics():
        small = [
            pltpu.make_async_copy(source, target, local_sem.at[2 + at])
            for at, (source, target) in enumerate(
                (
                    (occupied_ref, occupied_in),
                    (column_ref, column_in),
                    (octant_ref, octant_in),
                )
            )
        ]
        for copy in small:
            copy.start()
        with phase("m_small"):
            for copy in small:
                copy.wait()
        filled = occupied_in[...].astype(F32)
        column = column_in[...].astype(F32)
        octant = octant_in[...].astype(F32)
        square = (LANES, LANES)
        across = jnp.broadcast_to(column, square)
        diagonal = iota(square, 0) == iota(square, 1)
        down = jnp.sum(jnp.where(diagonal, across, 0.0), axis=1, keepdims=True)
        same = down == across
        rank = jnp.sum(flag(same & (iota(square, 0) < iota(square, 1))), axis=0, keepdims=True)
        rank_down = jnp.sum(
            flag(same & (iota(square, 1) < iota(square, 0))), axis=1, keepdims=True
        )
        slot = column * CAP + rank
        slots = n_blk * CAP
        hit = iota((slots, LANES), 0).astype(F32) == slot
        perm[...] = flag(hit, BF16)
        at_column = iota((n_blk, LANES), 0).astype(F32) == column
        coded = jnp.concatenate(
            [jnp.where(at_column, octant - CODE_SHIFT, 0.0), flag(at_column)], axis=0
        ).astype(BF16)
        at_rank = flag(iota(square, 1).astype(F32) == rank_down, BF16)
        placed = jnp.dot(coded, at_rank, preferred_element_type=F32)
        code = placed[0:n_blk] + EMPTY_CODE * (1.0 - placed[n_blk : 2 * n_blk])
        for c in range(n_blk):
            oct_send[c] = code[c : c + 1, :]
        fill_send[...] = jnp.broadcast_to(filled, (8, LANES))
        k = iota((8, LANES), 0)
        e = iota((8, LANES), 1)
        filled_8 = jnp.broadcast_to(filled, (8, LANES))
        fill_below = jnp.where(e == 0, 0.0, pltpu.roll(filled_8, 1, 1))
        fill_above = jnp.where(e == LANES - 1, 0.0, pltpu.roll(filled_8, LANES - 1, 1))
        k_weight = (PENALTY * UNIT_LENGTH) * jnp.where(
            k == 0, fill_below, jnp.where(k == 7, fill_above, 0.0)
        )

        @pl.when(jnp.logical_not(has_below))
        def _():
            fill_in[0] = jnp.zeros((8, LANES), F32)
            for step in range(STEPS):
                face_in[step, 0] = jnp.zeros((192, LANES), BF16)

        @pl.when(jnp.logical_not(has_above))
        def _():
            fill_in[1] = jnp.zeros((8, LANES), F32)
            for step in range(STEPS):
                face_in[step, 1] = jnp.zeros((192, LANES), BF16)

        swelling = filled * DILATION_SCALE

        def dilate(i, carry):
            f = gradients(cur, i)
            det = (
                f[0][0] * (f[1][1] * f[2][2] - f[1][2] * f[2][1])
                - f[0][1] * (f[1][0] * f[2][2] - f[1][2] * f[2][0])
                + f[0][2] * (f[1][0] * f[2][1] - f[1][1] * f[2][0])
            )
            change = (det - 1.0) * swelling
            for j in range(8):
                dil_rows[pl.ds(i * 64 + j, 8, stride=8), :] = change[j]
            return carry

        def elastic(i, carry):
            f = gradients(cur, i)
            shear, lame = slab(mat, 0, i), slab(mat, 1, i)
            c = [[None] * 3 for _ in range(3)]
            for a in range(3):
                for b in range(a, 3):
                    c[a][b] = f[0][a] * f[0][b] + f[1][a] * f[1][b] + f[2][a] * f[2][b]
                c[a][a] = c[a][a] - 1.0
            trace = (0.5 * lame) * (c[0][0] + c[1][1] + c[2][2])
            s = [[None] * 3 for _ in range(3)]
            for a in range(3):
                for b in range(a, 3):
                    s[a][b] = s[b][a] = shear * c[a][b]
            for a in range(3):
                s[a][a] = s[a][a] + trace
            for r in range(3):
                p = [f[r][0] * s[0][j] + f[r][1] * s[1][j] + f[r][2] * s[2][j] for j in range(3)]
                put_slab(piola, r, i, p[0])
                own = slab(cur, r, i)
                z_below = pltpu.roll(pltpu.roll(own, 1, 1), 1, 2)
                z_above = pltpu.roll(pltpu.roll(own, 7, 1), LANES - 1, 2)
                pull = k_weight * (jnp.where(iota(own.shape, 1) == 0, z_below, z_above) - own)
                put_slab(part, r, i, along_j(p[1]) + along_k(p[2]) + pull)
            cof = cofactors(f)
            for r in range(3):
                for j in range(3):
                    put_slab(cofactor, 3 * r + j, i, cof[r][j])
            return carry

        def swell(i, carry):
            pressure = jnp.concatenate(
                [press[pl.ds(i * 64 + j, 8, stride=8), :][None] for j in range(8)], axis=0
            )
            for r in range(3):
                p = [pressure * slab(cofactor, 3 * r + j, i) for j in range(3)]
                put_slab(piola, r, i, slab(piola, r, i) - p[0])
                put_slab(part, r, i, slab(part, r, i) - (along_j(p[1]) + along_k(p[2])))
            return carry

        def advance(i, carry):
            below, above, scale = i_span(i)
            gain = (TIME_STEP / UNIT_LENGTH) * slab(mat, 2, i) * filled
            for r in range(3):
                s = slab(cur, r, i)
                force = slab(part, r, i) + (slab(piola, r, above) - slab(piola, r, below)) * scale
                put_slab(cur, r, i, s + gain * force)
            return carry

        def take(first, last):
            lanes = slice(first * 64, last * 64)
            for i in range(first, last):
                dilate(i, 0)
            taken = lax.dot_general(
                perm[...],
                dil_rows[lanes, :].astype(BF16),
                (((1,), (1,)), ((), ())),
                preferred_element_type=F32,
            )
            dil_send[:, :, lanes] = taken.reshape(n_blk, CAP, (last - first) * 64).astype(BF16)

        def send_taken(step, first, last):
            lanes = pl.ds(first * 64, (last - first) * 64)

            for shift in far_first(True):
                c = columns[shift]
                send(
                    dil_send.at[c, :, lanes],
                    dil_in.at[step, mine, :, lanes],
                    sent.at[1 + step],
                    got.at[1 + n_mech * step + grp],
                    n_mech,
                    c,
                )

        def send_faces(step):
            for r in range(3):
                face_send[0, r * 64 : r * 64 + 64] = cur[r * 512 : r * 512 + 64, :].astype(BF16)
                face_send[1, r * 64 : r * 64 + 64] = cur[
                    r * 512 + 448 : r * 512 + 512, :
                ].astype(BF16)

            @pl.when(has_above)
            def _():
                face = (sent.at[3 + 2 * step + 1], got.at[4 + 2 * step + 0])
                send_pieces(face_send.at[1], 0, face_in.at[step, 0], 0, 192, *face, grp, blk + 1)

            @pl.when(has_below)
            def _():
                face = (sent.at[3 + 2 * step + 0], got.at[4 + 2 * step + 1])
                send_pieces(face_send.at[0], 0, face_in.at[step, 1], 0, 192, *face, grp, blk - 1)

        def meet_faces(step):
            with phase("m_faces"):
                for side, present in ((0, has_below), (1, has_above)):

                    @pl.when(present)
                    def _():
                        wait_all(face_in.at[step, side], got.at[4 + 2 * step + side])
                        wait_all(face_in.at[step, side], sent.at[3 + 2 * step + side])
                        if step == 0:
                            wait_all(fill_send, got.at[8 + side])
                            wait_all(fill_send, sent.at[7 + side])

                    at = 7 * side
                    weight = (PENALTY * UNIT_LENGTH) * fill_in[side]
                    for r in range(3):
                        other = face_in[step, side, r * 64 : r * 64 + 64, :].astype(F32).reshape(8, 8, LANES)
                        extra = weight * (other - slab(cur, r, at))
                        put_slab(part, r, at, slab(part, r, at) + extra)

        with phase("m_load"):
            loads[0].wait()
        with phase("m_take"):
            take(0, 8)

        with phase("m_barrier"):
            pl.semaphore_wait(barrier, n_blk + beside)

        mine = grp * n_blk + blk

        with phase("m_send_oct"):
            for shift in far_first(True):
                c = columns[shift]
                send(oct_send.at[c], oct_in.at[mine], sent.at[0], got.at[0], n_mech, c)

        @pl.when(has_above)
        def _():
            send(fill_send, fill_in.at[0], sent.at[7 + 1], got.at[8 + 0], grp, blk + 1)

        @pl.when(has_below)
        def _():
            send(fill_send, fill_in.at[1], sent.at[7 + 0], got.at[8 + 1], grp, blk - 1)

        loads[1].wait()
        for step in range(STEPS):
            with phase("m_elastic"):
                lax.fori_loop(0, 8, elastic, 0)
            if step == 0:
                with phase("m_send_dil"):
                    send_taken(0, 0, 8)
            if step == 0:
                send_faces(0)
            if step > 0:
                send_faces(step)
            if step + 1 < STEPS:
                meet_faces(step)
            for at, (first, last) in enumerate(PRESSURE_SPANS[step]):
                lanes = slice(first * 64, last * 64)
                with phase("m_wait_press"):
                    wait_all(
                        press_in.at[step, :, :, pl.ds(first * 64, (last - first) * 64)],
                        got.at[3 * step + at],
                    )
                with phase("m_press"):
                    arrived = press_in[step, :, :, lanes].astype(F32)
                    press[lanes, :] = PRESSURE_SCALE * lax.dot_general(
                        arrived.reshape(slots, (last - first) * 64).astype(BF16),
                        perm[...],
                        (((0,), (0,)), ((), ())),
                        preferred_element_type=F32,
                    )
                with phase("m_swell"):
                    for i in range(first, last):
                        swell(i, 0)
                if step + 1 == STEPS:
                    meet_faces(step)
                with phase("m_advance"):
                    for i in range(max(first - 1, 0), last - 1 if last < 8 else 8):
                        advance(i, 0)
                if step + 1 < STEPS:
                    if at == 0:
                        wait_all(dil_send, sent.at[1 + step])
                    ready = (max(first - 2, 0), last - 2 if last < 8 else 8)
                    with phase("m_take"):
                        take(*ready)
                    with phase("m_send_dil"):
                        send_taken(step + 1, *ready)
        wait_all(oct_send, sent.at[0])
        wait_all(dil_send, sent.at[1 + STEPS - 1])

    def brick():
        with phase("s_greet"):
            for g in range(n_mech):

                for shift in far_first(g < 2):
                    greet(g, columns[shift])
        row = iota((768, LANES), 0)
        at_octant = row // 8 == iota((768, LANES), 1)
        for k in range(8):
            select[:, k * LANES : (k + 1) * LANES] = flag(at_octant & (row % 8 == k), BF16)
        def split(value, lanes):
            count = value.shape[0]
            high = value.astype(BF16)
            rest = value - high.astype(F32)
            middle = rest.astype(BF16)
            low = (rest - middle.astype(F32)).astype(BF16)
            for at, piece in enumerate((high, middle, low)):
                pieces[at * count : (at + 1) * count, lanes] = piece

        def joined(product):
            return product[0:256] + product[256:512] + product[512:768]

        def to_layers(source, target, first, scale):
            for zq in range(6):
                split(source[pl.ds(zq, 256, stride=6), :], slice(zq * LANES, zq * LANES + LANES))
            for pair in range(4):
                lanes = slice(pair * 256, pair * 256 + 256)
                both = joined(
                    jnp.dot(pieces[...], select[:, lanes], preferred_element_type=F32)
                )
                for half in range(2):
                    value = scale * both[:, half * LANES : (half + 1) * LANES]
                    for x in range(16):
                        at = ((first + x) * 8 + 2 * pair + half) * 16
                        target[at : at + 16, :] = value[x * 16 : x * 16 + 16]

        k_row, column_256 = iota((256, 256), 0), iota((256, 256), 1)
        for block in range(3):
            k_held = k_row // LANES * 4 + (k_row // 32 + 4 - block) % 4
            chosen = (k_row % 32 == column_256 // 8) & (k_held == column_256 % 8)
            pick[block] = flag(chosen, BF16)

        def from_layers(source, first, spans):
            count = 16 * sum(last - start for start, last in spans)
            place = iota((count, LANES), 1) // 32
            for half in range(2):
                lanes = slice(half * LANES, (half + 1) * LANES)
                turned = []
                for k in range(4 * half, 4 * half + 4):
                    rows = [
                        source[at : at + 16, :]
                        for start, last in spans
                        for at in [((first + x) * 8 + k) * 16 for x in range(start, last)]
                    ]
                    rows = jnp.concatenate(rows, axis=0)
                    turned.append(pltpu.roll(rows, 32 * (k % 4), 1) if k % 4 else rows)
                for block in range(3):
                    value = turned[(3 - block) % 4]
                    for at in range(3):
                        value = jnp.where(place == at, turned[(at - block) % 4], value)
                    high = value.astype(BF16)
                    packed[block, 0:count, lanes] = high
                    packed[block, count : 2 * count, lanes] = (
                        value - high.astype(F32)
                    ).astype(BF16)
            for block in range(3):
                both = jnp.dot(
                    packed[block, 0 : 2 * count, :], pick[block], preferred_element_type=F32
                )
                both = both[0:count] + both[count : 2 * count]
                for half in range(2):
                    taken = 0
                    for start, last in spans:
                        more = 16 * (last - start)
                        cur[pl.ds(start * 96 + 2 * block + half, more, stride=6), :] = both[
                            taken : taken + more, half * LANES : (half + 1) * LANES
                        ]
                        taken += more

        plane = (1, 16, LANES)
        not_first = flag(iota(plane, 1) > 0)
        not_last = flag(iota(plane, 1) < 15)
        at_start = iota(plane, 2) == 0
        at_end = iota(plane, 2) >= DEPTH_OCTANTS - 1

        def sweep(source, source_first, target, target_first, diff_first, start, last):
            source_first, target_first = source_first + start, target_first + start
            diff_first = diff_first + start

            def rows_from(row):
                return source[pl.ds(row, LAYER), :].reshape(8, 16, LANES)

            below = rows_from((source_first - 1) * LAYER)
            first = rows_from(source_first * LAYER)
            entering = (below * below + (first * first + 1.0)) * (first - below)

            def one_layer(x, carry):
                centre, entering = carry
                row = pl.multiple_of((source_first + x) * LAYER, LAYER)
                x_above = rows_from(pl.multiple_of(row + LAYER, LAYER))
                y_below, y_above = rows_from(row - 1), rows_from(row + 1)
                square = centre * centre
                weight = square + 1.0

                def flux(there):
                    return (weight + there * there) * (there - centre)

                leaving = flux(x_above)
                inflow = leaving - entering
                inflow = inflow + not_last * flux(y_above) + not_first * flux(y_below)
                after = jnp.where(at_end, centre[7:8], pltpu.roll(centre[0:1], LANES - 1, 2))
                before = jnp.where(at_start, centre[0:1], pltpu.roll(centre[7:8], 1, 2))
                inner = (weight[1:] + square[:-1]) * (centre[1:] - centre[:-1])
                leave = (weight[7:8] + after * after) * (after - centre[7:8])
                enter = (weight[0:1] + before * before) * (before - centre[0:1])
                inflow = inflow + (
                    jnp.concatenate([inner, leave], axis=0)
                    - jnp.concatenate([-enter, inner], axis=0)
                )
                gain = rows_of(diff, (diff_first + x) * LAYER, LAYER).reshape(8, 16, LANES)
                updated = centre + gain * inflow
                at = pl.multiple_of((target_first + x) * LAYER, LAYER)
                target[pl.ds(at, LAYER), :] = updated.reshape(LAYER, LANES)
                return x_above, leaving

            lax.fori_loop(0, last - start, one_layer, (first, entering), unroll=2)

        with phase("s_load"):
            loads[0].wait()
        with phase("s_to_layers"):
            to_layers(cur, phi_a.at[0], 2, 1.0)

        def make_pressure(step):
            phi = phi_a.at[step]

            def one_i(i, carry):
                for t in range(4):
                    x, y = 8 * (t // 2), 8 * (t % 2)
                    value = jnp.concatenate(
                        [rows_of(phi, ((2 + x + i) * 8 + k) * 16 + y, 8) for k in range(8)], axis=0
                    )
                    value = value + CUBIC_TERM * value * value * value
                    at = pl.multiple_of(i * 64, 64)
                    pi_rows[pl.ds(at, 64), t * LANES : (t + 1) * LANES] = value.astype(BF16)
                return carry

            lax.fori_loop(0, 8, one_i, 0)

        def send_pressure(step, span, g):
            first, last = PRESSURE_SPANS[step][span]
            wide = slice(first * 64, last * 64)
            lanes = pl.ds(first * 64, (last - first) * 64)
            taken = lax.dot_general(
                hits[g * n_blk * CAP : (g + 1) * n_blk * CAP, :],
                pi_rows[wide, :],
                (((1,), (1,)), ((), ())),
                preferred_element_type=F32,
            )
            press_send[step, g * n_blk : (g + 1) * n_blk, :, wide] = taken.reshape(
                n_blk, CAP, (last - first) * 64
            ).astype(BF16)
            for shift in far_first(g < 2):
                c = columns[shift]
                send(
                    press_send.at[step, g * n_blk + c, :, lanes],
                    press_in.at[step, blk, :, lanes],
                    sent.at[step],
                    got.at[3 * step + span],
                    g,
                    c,
                )

        with phase("s_pi"):
            make_pressure(0)
        loads[1].wait()
        with phase("s_to_layers_d"):
            to_layers(mat, diff, 1, 0.5 * SWEEP_STEP)
        with phase("s_barrier"):
            pl.semaphore_wait(barrier, beside)

        @pl.when(has_above)
        def _():
            rim = (sent.at[6 + 1], got.at[11 + 0])
            send_pieces(diff, 16 * LAYER, diff, 0, LAYER, *rim, grp, blk + 1)

        @pl.when(has_below)
        def _():
            rim = (sent.at[6 + 0], got.at[11 + 1])
            send_pieces(diff, LAYER, diff, 17 * LAYER, LAYER, *rim, grp, blk - 1)

        with phase("s_wait_oct"):
            wait_all(oct_in, got.at[0])
        def find_hits(g):
            spread = (n_blk, CAP, LANES)
            codes = jnp.broadcast_to(oct_in[g * n_blk : (g + 1) * n_blk], spread)
            one_code = jnp.where(iota(spread, 1) == iota(spread, 2), codes, 0.0)
            wanted = jnp.dot(
                one_code.reshape(n_blk * CAP, LANES).astype(BF16),
                jnp.ones((LANES, LANES), BF16),
                preferred_element_type=F32,
            )
            lane = iota(wanted.shape, 1)
            rows = slice(g * n_blk * CAP, (g + 1) * n_blk * CAP)
            for t in range(4):
                at_octant = (lane + t * DEPTH_OCTANTS).astype(F32) - CODE_SHIFT
                found = (wanted == at_octant) & (lane < DEPTH_OCTANTS)
                hits[rows, t * LANES : (t + 1) * LANES] = flag(found, BF16)

        with phase("s_send_press"):
            find_hits(0)
            send_pressure(0, 0, 0)
            find_hits(1)
            send_pressure(0, 0, 1)
            find_hits(2)
            send_pressure(0, 0, 2)
            send_pressure(0, 1, 0)
            send_pressure(0, 1, 1)
            send_pressure(0, 1, 2)
            send_pressure(0, 2, 0)
            send_pressure(0, 2, 1)
            send_pressure(0, 2, 2)
        @pl.when(jnp.logical_not(has_below))
        def _():
            diff[0:LAYER, :] = jnp.zeros((LAYER, LANES), F32)
            for step in range(STEPS):
                phi_a[step, 0 : 2 * LAYER, :] = jnp.zeros((2 * LAYER, LANES), F32)

        @pl.when(jnp.logical_not(has_above))
        def _():
            diff[17 * LAYER : 18 * LAYER, :] = jnp.zeros((LAYER, LANES), F32)
            for step in range(STEPS):
                phi_a[step, 18 * LAYER : 20 * LAYER, :] = jnp.zeros((2 * LAYER, LANES), F32)

        for step in range(STEPS):
            phi = phi_a.at[step]
            if step > 0:
                with phase("s_pi"):
                    make_pressure(step)
                with phase("s_send_press"):
                    for g in range(n_mech):
                        send_pressure(step, 0, g)
            for g in (2, 0, 1):
                span = slice(g * n_blk, (g + 1) * n_blk)
                rows = slice(g * n_blk * CAP, (g + 1) * n_blk * CAP)
                with phase("s_wait_dil"):
                    wait_all(dil_in.at[step, span], got.at[1 + n_mech * step + g])
                arrived = dil_in[step, span].astype(F32)
                arrived = arrived.reshape(n_blk * CAP, NODES).astype(BF16)
                if g != 1:
                    with phase("s_collect"):
                        share = lax.dot_general(
                            arrived,
                            hits[rows, :],
                            (((0,), (0,)), ((), ())),
                            preferred_element_type=F32,
                        )
                        total[...] = share if g == 2 else total[...] + share

            def finish(ox, first, last):
                taken = slice(first * 64, last * 64)
                lanes = slice(ox * 256, ox * 256 + 256)
                share = lax.dot_general(
                    arrived[:, taken],
                    hits[rows, lanes],
                    (((0,), (0,)), ((), ())),
                    preferred_element_type=F32,
                )
                source = (SWEEP_STEP * SOURCE_RATE) * (total[taken, lanes] + share)
                for i in range(first, last):
                    for k in range(8):
                        at, row = ((2 + 8 * ox + i) * 8 + k) * 16, (i - first) * 64 + k * 8
                        for oy in range(2):
                            cells = slice(at + 8 * oy, at + 8 * oy + 8)
                            more = source[row : row + 8, oy * LANES : (oy + 1) * LANES]
                            phi[cells, :] = phi[cells, :] + more

            with phase("s_deposit_edge"):
                finish(0, 0, 2)
                finish(1, 6, 8)

            @pl.when(has_above)
            def _():
                halo_send[1] = phi[16 * LAYER : 18 * LAYER, :].astype(BF16)
                halo = (sent.at[2 + 2 * step + 1], got.at[7 + 2 * step + 0])
                target = halo_in.at[step, 0]
                send_pieces(halo_send.at[1], 0, target, 0, 2 * LAYER, *halo, grp, blk + 1)

            @pl.when(has_below)
            def _():
                halo_send[0] = phi[2 * LAYER : 4 * LAYER, :].astype(BF16)
                halo = (sent.at[2 + 2 * step + 0], got.at[7 + 2 * step + 1])
                target = halo_in.at[step, 1]
                send_pieces(halo_send.at[0], 0, target, 0, 2 * LAYER, *halo, grp, blk - 1)

            with phase("s_deposit"):
                finish(0, 2, 8)
                finish(1, 0, 6)
            after = phi_a.at[(step + 1) % 2]
            with phase("s_sweep_inner"):
                sweep(phi, 2, phi_b, 1, 1, 1, 15)
                sweep(phi_b, 1, after, 2, 1, 2, 14)
            if step == STEPS - 1:
                with phase("s_from_inner"):
                    from_layers(after, 2, [(2, 14)])
            with phase("s_wait_halo"):
                for side, present, first in ((0, has_below, 0), (1, has_above, 18)):

                    @pl.when(present)
                    def _():
                        two = halo_in.at[step, side]
                        wait_all(two, got.at[7 + 2 * step + side])
                        wait_all(two, sent.at[2 + 2 * step + side])
                        phi[first * LAYER : (first + 2) * LAYER, :] = two[...].astype(F32)
                        if step == 0:
                            one = diff.at[pl.ds(0, LAYER)]
                            wait_all(one, got.at[11 + side])
                            wait_all(one, sent.at[6 + side])

            with phase("s_sweep_edge"):
                sweep(phi, 2, phi_b, 1, 1, -1, 1)
                sweep(phi, 2, phi_b, 1, 1, 15, 17)
                sweep(phi_b, 1, after, 2, 1, 0, 2)
                sweep(phi_b, 1, after, 2, 1, 14, 16)
            with phase("s_sent"):
                wait_all(press_send.at[step], sent.at[step])
        with phase("s_from_edge"):
            from_layers(phi_a.at[STEPS % 2], 2, [(0, 2), (14, 16)])

    @pl.when(solvent)
    def _():
        brick()

    @pl.when(jnp.logical_not(solvent))
    def _():
        mechanics()


def solution(mesh):
    n_grp, n_blk = mesh.shape["grp"], mesh.shape["blk"]
    n_mech = n_grp - 1
    slots = n_blk * CAP
    dma = pltpu.SemaphoreType.DMA
    vmem = pltpu.VMEM
    whole = (1536, LANES)
    call = pl.pallas_call(
        functools.partial(kernel, n_grp, n_blk),
        out_shape=jax.ShapeDtypeStruct(whole, F32),
        in_specs=[pl.BlockSpec(memory_space=pltpu.HBM)] * 5,
        out_specs=pl.BlockSpec(memory_space=vmem),
        scratch_shapes=[
            vmem(whole, F32),
            vmem((1, LANES), jnp.int32),
            vmem((1, LANES), jnp.int32),
            vmem((1, LANES), jnp.int32),
            vmem((slots, LANES), BF16),
            vmem((n_blk, 1, LANES), F32),
            vmem((n_blk, CAP, NODES), BF16),
            vmem((NODES, LANES), F32),
            vmem((STEPS, n_blk, CAP, NODES), BF16),
            vmem((NODES, LANES), F32),
            vmem((STEPS, 2, 192, LANES), BF16),
            vmem((2, 192, LANES), BF16),
            vmem((2, 8, LANES), F32),
            vmem((8, LANES), F32),
            vmem(whole, F32),
            vmem(whole, F32),
            vmem((9 * NODES, LANES), F32),
            vmem((n_mech * n_blk, 1, LANES), F32),
            vmem((STEPS, n_mech * n_blk, CAP, NODES), BF16),
            vmem((STEPS, n_mech * n_blk, CAP, NODES), BF16),
            vmem((n_mech * n_blk * CAP, NODES), BF16),
            vmem((768, 1024), BF16),
            vmem((768, 768), BF16),
            vmem((2, 20 * LAYER, LANES), F32),
            vmem((18 * LAYER, LANES), F32),
            vmem((18 * LAYER, LANES), F32),
            vmem((2, 2 * LAYER, LANES), BF16),
            vmem((STEPS, 2, 2 * LAYER, LANES), BF16),
            vmem((3, 256, 256), BF16),
            vmem((3, 384, 256), BF16),
            vmem((NODES, NODES), BF16),
            vmem((NODES, NODES), F32),
            dma((5,)),
            dma((9,)),
            dma((13,)),
        ],
        compiler_params=pltpu.CompilerParams(
            collective_id=0, has_side_effects=True, vmem_limit_bytes=55 * 1000000
        ),
    )

    def shards(state, material, occupied, brick_column, brick_octant):
        operands = (
            state.reshape(whole),
            material.reshape(whole),
            occupied.reshape(1, LANES),
            brick_column.reshape(1, LANES),
            brick_octant.reshape(1, LANES),
        )
        out = call(*(pltpu.with_memory_space_constraint(x, pltpu.HBM) for x in operands))
        return out.reshape(state.shape)

    in_specs = (
        P("grp", None, None, "blk"),
        P("grp", None, None, "blk"),
        P(("grp", "blk")),
        P(("grp", "blk"), None),
        P(("grp", "blk")),
    )
    out_specs = P("grp", None, None, "blk")
    return jax.shard_map(shards, mesh=mesh, in_specs=in_specs, out_specs=out_specs, check_vma=False)
```

```python
import contextlib
import functools

import jax
import jax.numpy as jnp
from jax import lax
from jax.experimental import pallas as pl
from jax.experimental.pallas import tpu as pltpu
from jax.sharding import PartitionSpec as P

STEPS = 2
UNIT_LENGTH = 0.02
TIME_STEP = 0.1
PENALTY = 1.0
PRESSURE_SCALE = 0.05
DILATION_SCALE = 50.0
SWEEP_STEP = 0.03
SOURCE_RATE = 2.0
CUBIC_TERM = 0.3

MESH = pl.DeviceIdType.MESH
F32 = jnp.float32
BF16 = jnp.bfloat16
LANES = 128
NODES = 512
CAP = 8
HALO_PIECE = 32
DEPTH_OCTANTS = 96
CODE_SHIFT = 191.0
EMPTY_CODE = -1000.0
PRESSURE_SPANS = (((0, 4), (4, 6), (6, 8)), ((0, 8),))
LAYER = 128


def far_first(across):
    ring = (2, 1, 3, 0)
    along_y = (2, 1) if across else (0, 1)
    shifts = [(z, x, y) for z in ring for x in ring for y in range(2)]
    return sorted(shifts, key=lambda s: -(min(s[0], 4 - s[0]) + min(s[1], 4 - s[1]) + along_y[s[2]]))


def phase(name):
    return contextlib.nullcontext()


def iota(shape, dim):
    return lax.broadcasted_iota(jnp.int32, shape, dim)


def flag(mask, dtype=F32):
    return jnp.where(mask, 1.0, 0.0).astype(dtype)


def aligned(start, count):
    return start if isinstance(start, int) else pl.multiple_of(start, count)


def wait_all(ref, sem):
    pltpu.make_async_copy(ref, ref, sem).wait()


def rows_of(ref, start, count):
    return ref[pl.ds(aligned(start, count), count), :]


def slab(ref, r, i):
    return rows_of(ref, r * 512 + i * 64, 64).reshape(8, 8, LANES)


def put_slab(ref, r, i, value):
    ref[pl.ds(aligned(r * 512 + i * 64, 64), 64), :] = value.reshape(64, LANES)


def along_j(s, scale=1.0):
    first, last = s[1:2] - s[0:1], s[7:8] - s[6:7]
    if scale != 1.0:
        first, last = scale * first, scale * last
    return jnp.concatenate([first, (0.5 * scale) * (s[2:] - s[:-2]), last], axis=0)


def along_k(s, scale=1.0):
    k = iota(s.shape, 1)
    edge = (k == 0) | (k == 7)
    upper = jnp.where(k == 7, s, pltpu.roll(s, 7, 1))
    lower = jnp.where(k == 0, s, pltpu.roll(s, 1, 1))
    return (upper - lower) * jnp.where(edge, scale, 0.5 * scale)


def i_span(i):
    if isinstance(i, int):
        return max(i - 1, 0), min(i + 1, 7), 1.0 if i in (0, 7) else 0.5
    below, above = jnp.maximum(i - 1, 0), jnp.minimum(i + 1, 7)
    return below, above, jnp.where((i == 0) | (i == 7), 1.0, 0.5)


def gradients(cur, i):
    below, above, scale = i_span(i)
    grads = []
    for r in range(3):
        s = slab(cur, r, i)
        row = [
            (slab(cur, r, above) - slab(cur, r, below)) * (UNIT_LENGTH * scale),
            along_j(s, UNIT_LENGTH),
            along_k(s, UNIT_LENGTH),
        ]
        row[r] = row[r] + 1.0
        grads.append(row)
    return grads


def cofactors(f):
    return [
        [
            f[1][1] * f[2][2] - f[1][2] * f[2][1],
            f[1][2] * f[2][0] - f[1][0] * f[2][2],
            f[1][0] * f[2][1] - f[1][1] * f[2][0],
        ],
        [
            f[0][2] * f[2][1] - f[0][1] * f[2][2],
            f[0][0] * f[2][2] - f[0][2] * f[2][0],
            f[0][1] * f[2][0] - f[0][0] * f[2][1],
        ],
        [
            f[0][1] * f[1][2] - f[0][2] * f[1][1],
            f[0][2] * f[1][0] - f[0][0] * f[1][2],
            f[0][0] * f[1][1] - f[0][1] * f[1][0],
        ],
    ]


def kernel(
    n_grp,
    n_blk,
    state_ref,
    material_ref,
    occupied_ref,
    column_ref,
    octant_ref,
    cur,
    mat,
    occupied_in,
    column_in,
    octant_in,
    perm,
    oct_send,
    dil_send,
    dil_rows,
    press_in,
    press,
    face_in,
    face_send,
    fill_in,
    fill_send,
    piola,
    part,
    cofactor,
    oct_in,
    dil_in,
    press_send,
    hits,
    select,
    pieces,
    phi_a,
    phi_b,
    diff,
    halo_send,
    halo_in,
    pick,
    packed,
    pi_rows,
    total,
    local_sem,
    send_sem,
    recv_sem,
):
    grp, blk = lax.axis_index("grp"), lax.axis_index("blk")
    sent, got = send_sem, recv_sem
    n_mech = n_grp - 1
    solvent = grp == n_mech
    barrier = pltpu.get_barrier_semaphore()
    has_below, has_above = blk > 0, blk < n_blk - 1
    loads = [
        pltpu.make_async_copy(state_ref, cur, local_sem.at[0]),
        pltpu.make_async_copy(material_ref, mat, local_sem.at[1]),
    ]
    for copy in loads:
        copy.start()

    def greet(g, c):
        pl.semaphore_signal(barrier, inc=1, device_id=(g, c), device_id_type=MESH)

    @pl.when(has_below)
    def _():
        greet(grp, blk - 1)

    @pl.when(has_above)
    def _():
        greet(grp, blk + 1)

    def column_at(shift):
        z, x, y = blk // 8 + shift[0], blk // 2 + shift[1], blk + shift[2]
        return lax.rem(z, 4) * 8 + lax.rem(x, 4) * 2 + lax.rem(y, 2)

    columns = {shift: column_at(shift) for shift in far_first(True)}
    beside = jnp.where(has_below, 1, 0) + jnp.where(has_above, 1, 0)

    def send(src, dst, send_sem, recv_sem, g, c):
        copy = pltpu.make_async_remote_copy(
            src_ref=src,
            dst_ref=dst,
            send_sem=send_sem,
            recv_sem=recv_sem,
            device_id=(g, c),
            device_id_type=MESH,
        )
        copy.start()

    def send_pieces(source, first, target, there, count, send_sem, recv_sem, g, c):
        for at in range(0, count, HALO_PIECE):
            send(
                source.at[pl.ds(first + at, HALO_PIECE)],
                target.at[pl.ds(there + at, HALO_PIECE)],
                send_sem,
                recv_sem,
                g,
                c,
            )

    def mechanics():
        small = [
            pltpu.make_async_copy(source, target, local_sem.at[2 + at])
            for at, (source, target) in enumerate(
                (
                    (occupied_ref, occupied_in),
                    (column_ref, column_in),
                    (octant_ref, octant_in),
                )
            )
        ]
        for copy in small:
            copy.start()
        with phase("m_small"):
            for copy in small:
                copy.wait()
        filled = occupied_in[...].astype(F32)
        column = column_in[...].astype(F32)
        octant = octant_in[...].astype(F32)
        square = (LANES, LANES)
        across = jnp.broadcast_to(column, square)
        diagonal = iota(square, 0) == iota(square, 1)
        down = jnp.sum(jnp.where(diagonal, across, 0.0), axis=1, keepdims=True)
        same = down == across
        rank = jnp.sum(flag(same & (iota(square, 0) < iota(square, 1))), axis=0, keepdims=True)
        rank_down = jnp.sum(
            flag(same & (iota(square, 1) < iota(square, 0))), axis=1, keepdims=True
        )
        slot = column * CAP + rank
        slots = n_blk * CAP
        hit = iota((slots, LANES), 0).astype(F32) == slot
        perm[...] = flag(hit, BF16)
        at_column = iota((n_blk, LANES), 0).astype(F32) == column
        coded = jnp.concatenate(
            [jnp.where(at_column, octant - CODE_SHIFT, 0.0), flag(at_column)], axis=0
        ).astype(BF16)
        at_rank = flag(iota(square, 1).astype(F32) == rank_down, BF16)
        placed = jnp.dot(coded, at_rank, preferred_element_type=F32)
        code = placed[0:n_blk] + EMPTY_CODE * (1.0 - placed[n_blk : 2 * n_blk])
        for c in range(n_blk):
            oct_send[c] = code[c : c + 1, :]
        fill_send[...] = jnp.broadcast_to(filled, (8, LANES))
        k = iota((8, LANES), 0)
        e = iota((8, LANES), 1)
        filled_8 = jnp.broadcast_to(filled, (8, LANES))
        fill_below = jnp.where(e == 0, 0.0, pltpu.roll(filled_8, 1, 1))
        fill_above = jnp.where(e == LANES - 1, 0.0, pltpu.roll(filled_8, LANES - 1, 1))
        k_weight = (PENALTY * UNIT_LENGTH) * jnp.where(
            k == 0, fill_below, jnp.where(k == 7, fill_above, 0.0)
        )

        @pl.when(jnp.logical_not(has_below))
        def _():
            fill_in[0] = jnp.zeros((8, LANES), F32)
            for step in range(STEPS):
                face_in[step, 0] = jnp.zeros((192, LANES), BF16)

        @pl.when(jnp.logical_not(has_above))
        def _():
            fill_in[1] = jnp.zeros((8, LANES), F32)
            for step in range(STEPS):
                face_in[step, 1] = jnp.zeros((192, LANES), BF16)

        swelling = filled * DILATION_SCALE

        def dilate(i, carry):
            f = gradients(cur, i)
            det = (
                f[0][0] * (f[1][1] * f[2][2] - f[1][2] * f[2][1])
                - f[0][1] * (f[1][0] * f[2][2] - f[1][2] * f[2][0])
                + f[0][2] * (f[1][0] * f[2][1] - f[1][1] * f[2][0])
            )
            change = (det - 1.0) * swelling
            for j in range(8):
                dil_rows[pl.ds(i * 64 + j, 8, stride=8), :] = change[j]
            return carry

        def elastic(i, carry):
            f = gradients(cur, i)
            shear, lame = slab(mat, 0, i), slab(mat, 1, i)
            c = [[None] * 3 for _ in range(3)]
            for a in range(3):
                for b in range(a, 3):
                    c[a][b] = f[0][a] * f[0][b] + f[1][a] * f[1][b] + f[2][a] * f[2][b]
                c[a][a] = c[a][a] - 1.0
            trace = (0.5 * lame) * (c[0][0] + c[1][1] + c[2][2])
            s = [[None] * 3 for _ in range(3)]
            for a in range(3):
                for b in range(a, 3):
                    s[a][b] = s[b][a] = shear * c[a][b]
            for a in range(3):
                s[a][a] = s[a][a] + trace
            for r in range(3):
                p = [f[r][0] * s[0][j] + f[r][1] * s[1][j] + f[r][2] * s[2][j] for j in range(3)]
                put_slab(piola, r, i, p[0])
                own = slab(cur, r, i)
                z_below = pltpu.roll(pltpu.roll(own, 1, 1), 1, 2)
                z_above = pltpu.roll(pltpu.roll(own, 7, 1), LANES - 1, 2)
                pull = k_weight * (jnp.where(iota(own.shape, 1) == 0, z_below, z_above) - own)
                put_slab(part, r, i, along_j(p[1]) + along_k(p[2]) + pull)
            cof = cofactors(f)
            for r in range(3):
                for j in range(3):
                    put_slab(cofactor, 3 * r + j, i, cof[r][j])
            return carry

        def swell(i, carry):
            pressure = jnp.concatenate(
                [press[pl.ds(i * 64 + j, 8, stride=8), :][None] for j in range(8)], axis=0
            )
            for r in range(3):
                p = [pressure * slab(cofactor, 3 * r + j, i) for j in range(3)]
                put_slab(piola, r, i, slab(piola, r, i) - p[0])
                put_slab(part, r, i, slab(part, r, i) - (along_j(p[1]) + along_k(p[2])))
            return carry

        def advance(i, carry):
            below, above, scale = i_span(i)
            gain = (TIME_STEP / UNIT_LENGTH) * slab(mat, 2, i) * filled
            for r in range(3):
                s = slab(cur, r, i)
                force = slab(part, r, i) + (slab(piola, r, above) - slab(piola, r, below)) * scale
                put_slab(cur, r, i, s + gain * force)
            return carry

        def take(first, last):
            lanes = slice(first * 64, last * 64)
            for i in range(first, last):
                dilate(i, 0)
            taken = lax.dot_general(
                perm[...],
                dil_rows[lanes, :].astype(BF16),
                (((1,), (1,)), ((), ())),
                preferred_element_type=F32,
            )
            dil_send[:, :, lanes] = taken.reshape(n_blk, CAP, (last - first) * 64).astype(BF16)

        def send_taken(step, first, last):
            lanes = pl.ds(first * 64, (last - first) * 64)

            for shift in far_first(True):
                c = columns[shift]
                send(
                    dil_send.at[c, :, lanes],
                    dil_in.at[step, mine, :, lanes],
                    sent.at[1 + step],
                    got.at[1 + n_mech * step + grp],
                    n_mech,
                    c,
                )

        def send_faces(step):
            for r in range(3):
                face_send[0, r * 64 : r * 64 + 64] = cur[r * 512 : r * 512 + 64, :].astype(BF16)
                face_send[1, r * 64 : r * 64 + 64] = cur[
                    r * 512 + 448 : r * 512 + 512, :
                ].astype(BF16)

            @pl.when(has_above)
            def _():
                face = (sent.at[3 + 2 * step + 1], got.at[4 + 2 * step + 0])
                send_pieces(face_send.at[1], 0, face_in.at[step, 0], 0, 192, *face, grp, blk + 1)

            @pl.when(has_below)
            def _():
                face = (sent.at[3 + 2 * step + 0], got.at[4 + 2 * step + 1])
                send_pieces(face_send.at[0], 0, face_in.at[step, 1], 0, 192, *face, grp, blk - 1)

        def meet_faces(step):
            with phase("m_faces"):
                for side, present in ((0, has_below), (1, has_above)):

                    @pl.when(present)
                    def _():
                        wait_all(face_in.at[step, side], got.at[4 + 2 * step + side])
                        wait_all(face_in.at[step, side], sent.at[3 + 2 * step + side])
                        if step == 0:
                            wait_all(fill_send, got.at[8 + side])
                            wait_all(fill_send, sent.at[7 + side])

                    at = 7 * side
                    weight = (PENALTY * UNIT_LENGTH) * fill_in[side]
                    for r in range(3):
                        other = face_in[step, side, r * 64 : r * 64 + 64, :].astype(F32).reshape(8, 8, LANES)
                        extra = weight * (other - slab(cur, r, at))
                        put_slab(part, r, at, slab(part, r, at) + extra)

        with phase("m_load"):
            loads[0].wait()
        with phase("m_take"):
            take(0, 8)

        with phase("m_barrier"):
            pl.semaphore_wait(barrier, n_blk + beside)

        mine = grp * n_blk + blk

        with phase("m_send_oct"):
            for shift in far_first(True):
                c = columns[shift]
                send(oct_send.at[c], oct_in.at[mine], sent.at[0], got.at[0], n_mech, c)

        @pl.when(has_above)
        def _():
            send(fill_send, fill_in.at[0], sent.at[7 + 1], got.at[8 + 0], grp, blk + 1)

        @pl.when(has_below)
        def _():
            send(fill_send, fill_in.at[1], sent.at[7 + 0], got.at[8 + 1], grp, blk - 1)

        loads[1].wait()
        for step in range(STEPS):
            with phase("m_elastic"):
                lax.fori_loop(0, 8, elastic, 0)
            if step == 0:
                with phase("m_send_dil"):
                    send_taken(0, 0, 8)
            if step == 0:
                send_faces(0)
            if step > 0:
                send_faces(step)
            if step + 1 < STEPS:
                meet_faces(step)
            for at, (first, last) in enumerate(PRESSURE_SPANS[step]):
                lanes = slice(first * 64, last * 64)
                with phase("m_wait_press"):
                    wait_all(
                        press_in.at[step, :, :, pl.ds(first * 64, (last - first) * 64)],
                        got.at[3 * step + at],
                    )
                with phase("m_press"):
                    arrived = press_in[step, :, :, lanes].astype(F32)
                    press[lanes, :] = PRESSURE_SCALE * lax.dot_general(
                        arrived.reshape(slots, (last - first) * 64).astype(BF16),
                        perm[...],
                        (((0,), (0,)), ((), ())),
                        preferred_element_type=F32,
                    )
                with phase("m_swell"):
                    for i in range(first, last):
                        swell(i, 0)
                if step + 1 == STEPS:
                    meet_faces(step)
                with phase("m_advance"):
                    for i in range(max(first - 1, 0), last - 1 if last < 8 else 8):
                        advance(i, 0)
                if step + 1 < STEPS:
                    if at == 0:
                        wait_all(dil_send, sent.at[1 + step])
                    ready = (max(first - 2, 0), last - 2 if last < 8 else 8)
                    with phase("m_take"):
                        take(*ready)
                    with phase("m_send_dil"):
                        send_taken(step + 1, *ready)
        wait_all(oct_send, sent.at[0])
        wait_all(dil_send, sent.at[1 + STEPS - 1])

    def brick():
        with phase("s_greet"):
            for g in range(n_mech):

                for shift in far_first(g < 2):
                    greet(g, columns[shift])
        row = iota((768, LANES), 0)
        at_octant = row // 8 == iota((768, LANES), 1)
        for k in range(8):
            select[:, k * LANES : (k + 1) * LANES] = flag(at_octant & (row % 8 == k), BF16)
        def split(value, lanes):
            count = value.shape[0]
            high = value.astype(BF16)
            rest = value - high.astype(F32)
            middle = rest.astype(BF16)
            low = (rest - middle.astype(F32)).astype(BF16)
            for at, piece in enumerate((high, middle, low)):
                pieces[at * count : (at + 1) * count, lanes] = piece

        def joined(product):
            return product[0:256] + product[256:512] + product[512:768]

        def to_layers(source, target, first, scale):
            for zq in range(6):
                split(source[pl.ds(zq, 256, stride=6), :], slice(zq * LANES, zq * LANES + LANES))
            for pair in range(4):
                lanes = slice(pair * 256, pair * 256 + 256)
                both = joined(
                    jnp.dot(pieces[...], select[:, lanes], preferred_element_type=F32)
                )
                for half in range(2):
                    value = scale * both[:, half * LANES : (half + 1) * LANES]
                    for x in range(16):
                        at = ((first + x) * 8 + 2 * pair + half) * 16
                        target[at : at + 16, :] = value[x * 16 : x * 16 + 16]

        k_row, column_256 = iota((256, 256), 0), iota((256, 256), 1)
        for block in range(3):
            k_held = k_row // LANES * 4 + (k_row // 32 + 4 - block) % 4
            chosen = (k_row % 32 == column_256 // 8) & (k_held == column_256 % 8)
            pick[block] = flag(chosen, BF16)

        def from_layers(source, first, spans):
            count = 16 * sum(last - start for start, last in spans)
            place = iota((count, LANES), 1) // 32
            for half in range(2):
                lanes = slice(half * LANES, (half + 1) * LANES)
                turned = []
                for k in range(4 * half, 4 * half + 4):
                    rows = [
                        source[at : at + 16, :]
                        for start, last in spans
                        for at in [((first + x) * 8 + k) * 16 for x in range(start, last)]
                    ]
                    rows = jnp.concatenate(rows, axis=0)
                    turned.append(pltpu.roll(rows, 32 * (k % 4), 1) if k % 4 else rows)
                for block in range(3):
                    value = turned[(3 - block) % 4]
                    for at in range(3):
                        value = jnp.where(place == at, turned[(at - block) % 4], value)
                    high = value.astype(BF16)
                    packed[block, 0:count, lanes] = high
                    packed[block, count : 2 * count, lanes] = (
                        value - high.astype(F32)
                    ).astype(BF16)
            for block in range(3):
                both = jnp.dot(
                    packed[block, 0 : 2 * count, :], pick[block], preferred_element_type=F32
                )
                both = both[0:count] + both[count : 2 * count]
                for half in range(2):
                    taken = 0
                    for start, last in spans:
                        more = 16 * (last - start)
                        cur[pl.ds(start * 96 + 2 * block + half, more, stride=6), :] = both[
                            taken : taken + more, half * LANES : (half + 1) * LANES
                        ]
                        taken += more

        plane = (1, 16, LANES)
        not_first = flag(iota(plane, 1) > 0)
        not_last = flag(iota(plane, 1) < 15)
        at_start = iota(plane, 2) == 0
        at_end = iota(plane, 2) >= DEPTH_OCTANTS - 1

        def sweep(source, source_first, target, target_first, diff_first, start, last):
            source_first, target_first = source_first + start, target_first + start
            diff_first = diff_first + start

            def rows_from(row):
                return source[pl.ds(row, LAYER), :].reshape(8, 16, LANES)

            below = rows_from((source_first - 1) * LAYER)
            first = rows_from(source_first * LAYER)
            entering = (below * below + (first * first + 1.0)) * (first - below)

            def one_layer(x, carry):
                centre, entering = carry
                row = pl.multiple_of((source_first + x) * LAYER, LAYER)
                x_above = rows_from(pl.multiple_of(row + LAYER, LAYER))
                y_below, y_above = rows_from(row - 1), rows_from(row + 1)
                square = centre * centre
                weight = square + 1.0

                def flux(there):
                    return (weight + there * there) * (there - centre)

                leaving = flux(x_above)
                inflow = leaving - entering
                inflow = inflow + not_last * flux(y_above) + not_first * flux(y_below)
                after = jnp.where(at_end, centre[7:8], pltpu.roll(centre[0:1], LANES - 1, 2))
                before = jnp.where(at_start, centre[0:1], pltpu.roll(centre[7:8], 1, 2))
                inner = (weight[1:] + square[:-1]) * (centre[1:] - centre[:-1])
                leave = (weight[7:8] + after * after) * (after - centre[7:8])
                enter = (weight[0:1] + before * before) * (before - centre[0:1])
                inflow = inflow + (
                    jnp.concatenate([inner, leave], axis=0)
                    - jnp.concatenate([-enter, inner], axis=0)
                )
                gain = rows_of(diff, (diff_first + x) * LAYER, LAYER).reshape(8, 16, LANES)
                updated = centre + gain * inflow
                at = pl.multiple_of((target_first + x) * LAYER, LAYER)
                target[pl.ds(at, LAYER), :] = updated.reshape(LAYER, LANES)
                return x_above, leaving

            lax.fori_loop(0, last - start, one_layer, (first, entering), unroll=2)

        with phase("s_load"):
            loads[0].wait()
        with phase("s_to_layers"):
            to_layers(cur, phi_a.at[0], 2, 1.0)

        def make_pressure(step):
            phi = phi_a.at[step]

            def one_i(i, carry):
                for t in range(4):
                    x, y = 8 * (t // 2), 8 * (t % 2)
                    value = jnp.concatenate(
                        [rows_of(phi, ((2 + x + i) * 8 + k) * 16 + y, 8) for k in range(8)], axis=0
                    )
                    value = value + CUBIC_TERM * value * value * value
                    at = pl.multiple_of(i * 64, 64)
                    pi_rows[pl.ds(at, 64), t * LANES : (t + 1) * LANES] = value.astype(BF16)
                return carry

            lax.fori_loop(0, 8, one_i, 0)

        def send_pressure(step, span, g):
            first, last = PRESSURE_SPANS[step][span]
            wide = slice(first * 64, last * 64)
            lanes = pl.ds(first * 64, (last - first) * 64)
            taken = lax.dot_general(
                hits[g * n_blk * CAP : (g + 1) * n_blk * CAP, :],
                pi_rows[wide, :],
                (((1,), (1,)), ((), ())),
                preferred_element_type=F32,
            )
            press_send[step, g * n_blk : (g + 1) * n_blk, :, wide] = taken.reshape(
                n_blk, CAP, (last - first) * 64
            ).astype(BF16)
            for shift in far_first(g < 2):
                c = columns[shift]
                send(
                    press_send.at[step, g * n_blk + c, :, lanes],
                    press_in.at[step, blk, :, lanes],
                    sent.at[step],
                    got.at[3 * step + span],
                    g,
                    c,
                )

        with phase("s_pi"):
            make_pressure(0)
        loads[1].wait()
        with phase("s_to_layers_d"):
            to_layers(mat, diff, 1, 0.5 * SWEEP_STEP)
        with phase("s_barrier"):
            pl.semaphore_wait(barrier, beside)

        @pl.when(has_above)
        def _():
            rim = (sent.at[6 + 1], got.at[11 + 0])
            send_pieces(diff, 16 * LAYER, diff, 0, LAYER, *rim, grp, blk + 1)

        @pl.when(has_below)
        def _():
            rim = (sent.at[6 + 0], got.at[11 + 1])
            send_pieces(diff, LAYER, diff, 17 * LAYER, LAYER, *rim, grp, blk - 1)

        with phase("s_wait_oct"):
            wait_all(oct_in, got.at[0])
        def find_hits(g):
            spread = (n_blk, CAP, LANES)
            codes = jnp.broadcast_to(oct_in[g * n_blk : (g + 1) * n_blk], spread)
            one_code = jnp.where(iota(spread, 1) == iota(spread, 2), codes, 0.0)
            wanted = jnp.dot(
                one_code.reshape(n_blk * CAP, LANES).astype(BF16),
                jnp.ones((LANES, LANES), BF16),
                preferred_element_type=F32,
            )
            lane = iota(wanted.shape, 1)
            rows = slice(g * n_blk * CAP, (g + 1) * n_blk * CAP)
            for t in range(4):
                at_octant = (lane + t * DEPTH_OCTANTS).astype(F32) - CODE_SHIFT
                found = (wanted == at_octant) & (lane < DEPTH_OCTANTS)
                hits[rows, t * LANES : (t + 1) * LANES] = flag(found, BF16)

        with phase("s_send_press"):
            find_hits(0)
            send_pressure(0, 0, 0)
            find_hits(1)
            send_pressure(0, 0, 1)
            find_hits(2)
            send_pressure(0, 0, 2)
            send_pressure(0, 1, 0)
            send_pressure(0, 1, 1)
            send_pressure(0, 1, 2)
            send_pressure(0, 2, 0)
            send_pressure(0, 2, 1)
            send_pressure(0, 2, 2)
        @pl.when(jnp.logical_not(has_below))
        def _():
            diff[0:LAYER, :] = jnp.zeros((LAYER, LANES), F32)
            for step in range(STEPS):
                phi_a[step, 0 : 2 * LAYER, :] = jnp.zeros((2 * LAYER, LANES), F32)

        @pl.when(jnp.logical_not(has_above))
        def _():
            diff[17 * LAYER : 18 * LAYER, :] = jnp.zeros((LAYER, LANES), F32)
            for step in range(STEPS):
                phi_a[step, 18 * LAYER : 20 * LAYER, :] = jnp.zeros((2 * LAYER, LANES), F32)

        for step in range(STEPS):
            phi = phi_a.at[step]
            if step > 0:
                with phase("s_pi"):
                    make_pressure(step)
                with phase("s_send_press"):
                    for g in range(n_mech):
                        send_pressure(step, 0, g)
            for g in (2, 0, 1):
                span = slice(g * n_blk, (g + 1) * n_blk)
                rows = slice(g * n_blk * CAP, (g + 1) * n_blk * CAP)
                with phase("s_wait_dil"):
                    wait_all(dil_in.at[step, span], got.at[1 + n_mech * step + g])
                arrived = dil_in[step, span].astype(F32)
                arrived = arrived.reshape(n_blk * CAP, NODES).astype(BF16)
                if g != 1:
                    with phase("s_collect"):
                        share = lax.dot_general(
                            arrived,
                            hits[rows, :],
                            (((0,), (0,)), ((), ())),
                            preferred_element_type=F32,
                        )
                        total[...] = share if g == 2 else total[...] + share

            def finish(ox, first, last):
                taken = slice(first * 64, last * 64)
                lanes = slice(ox * 256, ox * 256 + 256)
                share = lax.dot_general(
                    arrived[:, taken],
                    hits[rows, lanes],
                    (((0,), (0,)), ((), ())),
                    preferred_element_type=F32,
                )
                source = (SWEEP_STEP * SOURCE_RATE) * (total[taken, lanes] + share)
                for i in range(first, last):
                    for k in range(8):
                        at, row = ((2 + 8 * ox + i) * 8 + k) * 16, (i - first) * 64 + k * 8
                        for oy in range(2):
                            cells = slice(at + 8 * oy, at + 8 * oy + 8)
                            more = source[row : row + 8, oy * LANES : (oy + 1) * LANES]
                            phi[cells, :] = phi[cells, :] + more

            with phase("s_deposit_edge"):
                finish(0, 0, 2)
                finish(1, 6, 8)

            @pl.when(has_above)
            def _():
                halo_send[1] = phi[16 * LAYER : 18 * LAYER, :].astype(BF16)
                halo = (sent.at[2 + 2 * step + 1], got.at[7 + 2 * step + 0])
                target = halo_in.at[step, 0]
                send_pieces(halo_send.at[1], 0, target, 0, 2 * LAYER, *halo, grp, blk + 1)

            @pl.when(has_below)
            def _():
                halo_send[0] = phi[2 * LAYER : 4 * LAYER, :].astype(BF16)
                halo = (sent.at[2 + 2 * step + 0], got.at[7 + 2 * step + 1])
                target = halo_in.at[step, 1]
                send_pieces(halo_send.at[0], 0, target, 0, 2 * LAYER, *halo, grp, blk - 1)

            with phase("s_deposit"):
                finish(0, 2, 8)
                finish(1, 0, 6)
            after = phi_a.at[(step + 1) % 2]
            with phase("s_sweep_inner"):
                sweep(phi, 2, phi_b, 1, 1, 1, 15)
                sweep(phi_b, 1, after, 2, 1, 2, 14)
            if step == STEPS - 1:
                with phase("s_from_inner"):
                    from_layers(after, 2, [(2, 14)])
            with phase("s_wait_halo"):
                for side, present, first in ((0, has_below, 0), (1, has_above, 18)):

                    @pl.when(present)
                    def _():
                        two = halo_in.at[step, side]
                        wait_all(two, got.at[7 + 2 * step + side])
                        wait_all(two, sent.at[2 + 2 * step + side])
                        phi[first * LAYER : (first + 2) * LAYER, :] = two[...].astype(F32)
                        if step == 0:
                            one = diff.at[pl.ds(0, LAYER)]
                            wait_all(one, got.at[11 + side])
                            wait_all(one, sent.at[6 + side])

            with phase("s_sweep_edge"):
                sweep(phi, 2, phi_b, 1, 1, -1, 1)
                sweep(phi, 2, phi_b, 1, 1, 15, 17)
                sweep(phi_b, 1, after, 2, 1, 0, 2)
                sweep(phi_b, 1, after, 2, 1, 14, 16)
            with phase("s_sent"):
                wait_all(press_send.at[step], sent.at[step])
        with phase("s_from_edge"):
            from_layers(phi_a.at[STEPS % 2], 2, [(0, 2), (14, 16)])

    @pl.when(solvent)
    def _():
        brick()

    @pl.when(jnp.logical_not(solvent))
    def _():
        mechanics()


def solution(mesh):
    n_grp, n_blk = mesh.shape["grp"], mesh.shape["blk"]
    n_mech = n_grp - 1
    slots = n_blk * CAP
    dma = pltpu.SemaphoreType.DMA
    vmem = pltpu.VMEM
    whole = (1536, LANES)
    call = pl.pallas_call(
        functools.partial(kernel, n_grp, n_blk),
        out_shape=jax.ShapeDtypeStruct(whole, F32),
        in_specs=[pl.BlockSpec(memory_space=pltpu.HBM)] * 5,
        out_specs=pl.BlockSpec(memory_space=vmem),
        scratch_shapes=[
            vmem(whole, F32),
            vmem((1, LANES), jnp.int32),
            vmem((1, LANES), jnp.int32),
            vmem((1, LANES), jnp.int32),
            vmem((slots, LANES), BF16),
            vmem((n_blk, 1, LANES), F32),
            vmem((n_blk, CAP, NODES), BF16),
            vmem((NODES, LANES), F32),
            vmem((STEPS, n_blk, CAP, NODES), BF16),
            vmem((NODES, LANES), F32),
            vmem((STEPS, 2, 192, LANES), BF16),
            vmem((2, 192, LANES), BF16),
            vmem((2, 8, LANES), F32),
            vmem((8, LANES), F32),
            vmem(whole, F32),
            vmem(whole, F32),
            vmem((9 * NODES, LANES), F32),
            vmem((n_mech * n_blk, 1, LANES), F32),
            vmem((STEPS, n_mech * n_blk, CAP, NODES), BF16),
            vmem((STEPS, n_mech * n_blk, CAP, NODES), BF16),
            vmem((n_mech * n_blk * CAP, NODES), BF16),
            vmem((768, 1024), BF16),
            vmem((768, 768), BF16),
            vmem((2, 20 * LAYER, LANES), F32),
            vmem((18 * LAYER, LANES), F32),
            vmem((18 * LAYER, LANES), F32),
            vmem((2, 2 * LAYER, LANES), BF16),
            vmem((STEPS, 2, 2 * LAYER, LANES), BF16),
            vmem((3, 256, 256), BF16),
            vmem((3, 384, 256), BF16),
            vmem((NODES, NODES), BF16),
            vmem((NODES, NODES), F32),
            dma((5,)),
            dma((9,)),
            dma((13,)),
        ],
        compiler_params=pltpu.CompilerParams(
            collective_id=0, has_side_effects=True, vmem_limit_bytes=55 * 1000000
        ),
    )

    def shards(state, material, occupied, brick_column, brick_octant):
        operands = (
            state.reshape(whole),
            material.reshape(whole),
            occupied.reshape(1, LANES),
            brick_column.reshape(1, LANES),
            brick_octant.reshape(1, LANES),
        )
        out = call(*(pltpu.with_memory_space_constraint(x, pltpu.HBM) for x in operands))
        return out.reshape(state.shape)

    in_specs = (
        P("grp", None, None, "blk"),
        P("grp", None, None, "blk"),
        P(("grp", "blk")),
        P(("grp", "blk"), None),
        P(("grp", "blk")),
    )
    out_specs = P("grp", None, None, "blk")
    return jax.shard_map(shards, mesh=mesh, in_specs=in_specs, out_specs=out_specs, check_vma=False)
```
